32 devices in a mesh: replica: 4 (over y, x), fsdp: 8 (over z, core).
Axes of the slice: x: 2, y: 2, z: 4, core: 2. Of those that a mesh axis runs over, the one named last changes fastest.
Arguments:
- latents: bfloat16 [32, 256, 1152], P(('replica', 'fsdp')), may hold values from -6 to 6
- condition: bfloat16 [32, 1152], P(('replica', 'fsdp')), may hold values from -6 to 6
- bucket: int32 [32], P(('replica', 'fsdp')), may hold values from 0 to 2, as said below
- keep_slots: int32 [32, 128], P(('replica', 'fsdp')), may hold values from 0 to 255, as said below
- modulation_weight: bfloat16 [1152, 6912], P('fsdp'), may hold values from -0.1875 to 0.1875
- modulation_bias: bfloat16 [6912], P('fsdp'), may hold values from -1.5 to 1.5
- projection_weight: bfloat16 [1152, 3456], P('fsdp'), may hold values from -0.1875 to 0.1875
- query_value_bias: bfloat16 [2304], P('fsdp'), may hold values from -1.5 to 1.5
- output_weight: bfloat16 [1152, 1152], P('fsdp'), may hold values from -0.75 to 0.75
- output_bias: bfloat16 [1152], P('fsdp'), may hold values from -1.5 to 1.5
- expand_weight: bfloat16 [1152, 4608], P('fsdp'), may hold values from -0.1875 to 0.1875
- expand_bias: bfloat16 [4608], P('fsdp'), may hold values from -2.5 to 2.5
- reduce_weight: bfloat16 [4608, 1152], P('fsdp'), may hold values from -0.125 to 0.125
- reduce_bias: bfloat16 [1152], P('fsdp'), may hold values from -1.5 to 1.5
- cotangent: bfloat16 [32, 256, 1152], P(('replica', 'fsdp')), may hold values from -6 to 6
Outputs:
- block_out: bfloat16 [32, 256, 1152], P(('replica', 'fsdp'))
- grad_latents: bfloat16 [32, 256, 1152], P(('replica', 'fsdp'))
- grad_condition: float32 [32, 1152], P(('replica', 'fsdp'))
- grad_modulation_weight: float32 [1152, 6912], P('fsdp')
- grad_modulation_bias: float32 [6912], P('fsdp')
- grad_projection_weight: float32 [1152, 3456], P('fsdp')
- grad_query_value_bias: float32 [2304], P('fsdp')
- grad_output_weight: float32 [1152, 1152], P('fsdp')
- grad_output_bias: float32 [1152], P('fsdp')
- grad_expand_weight: float32 [1152, 4608], P('fsdp')
- grad_expand_bias: float32 [4608], P('fsdp')
- grad_reduce_weight: float32 [4608, 1152], P('fsdp')
- grad_reduce_bias: float32 [1152], P('fsdp')
The draws below stay inside these ranges and needn't reach their ends.
Inputs may be any that keep to these rules, and one draw needn't show every extreme that they name: `bucket`: 0 marks a 16 x 16 grid of tokens, 1 and 2 grids of (12) x (20) and (20) x (12); an image's real tokens fill its first slots, the rest are padding. `keep_slots`: each row holds distinct slots of that image's real tokens in random order; the first live_count entries are the kept tokens, the others of the image are routed past the block.
All inputs are finite; a program needn't handle non-finite values.
Results may differ from the reference program's by a relative error of at most 0.02.
Values may be sent and summed in bfloat16 or wider, within the bound.
A program may use at most 256 MiB of HBM per device.

```python
import jax
import jax.numpy as jnp
from jax import lax

D = 1152
HEADS = 16
HEAD_DIM = 72
MLP = 4608
GRID = 16
SLOTS = 256
IMAGES = 32


def routing_tables(key):
    slot_count = GRID * GRID
    bucket_ids = jax.random.randint(jax.random.fold_in(key, 101), (IMAGES,), 0, 3).astype(jnp.int32)
    real_count = jnp.where(bucket_ids == 0, slot_count, slot_count - 16)
    image_keys = jax.random.split(jax.random.fold_in(key, 202), IMAGES)
    slot_ranks = jax.vmap(lambda image_key: jax.random.permutation(image_key, slot_count))(image_keys).astype(jnp.int32)
    position = jnp.arange(slot_count, dtype=jnp.int32)[None, :]
    slot_score = slot_ranks + slot_count * (position >= real_count[:, None]).astype(jnp.int32)
    slot_order = jnp.argsort(slot_score, axis=1, stable=True).astype(jnp.int32)
    return (bucket_ids, slot_order[:, :slot_count // 2])


def draw_bucket(key, part):
    return routing_tables(key)[0]


def draw_keep_slots(key, part):
    return routing_tables(key)[1]


def strengthened(values, rng, source, target, blocks, factor):
    owner, partner = [(jnp.arange(values.shape[axis_at]) // (values.shape[axis_at] // blocks)).reshape([-1 if axis == axis_at else 1 for axis in range(values.ndim)]) for axis_at in (source, target)]
    chosen = jax.random.permutation(rng, blocks)[partner]
    strong = (owner == chosen) | (owner == (partner + blocks // 2) % blocks)
    return jnp.where(strong, factor * values, values)


def level_of(stream_key, shape, shards, least, largest):
    gain = 1.0
    for dim, shards_of in shards:
        heights = jax.random.uniform(jax.random.fold_in(jax.random.fold_in(stream_key, 6), dim), (shards_of,), jnp.float32, least / len(shards), largest / len(shards))
        gain = gain * jnp.repeat(jnp.exp(heights), shape[dim] // shards_of).reshape((-1,) + (1,) * (len(shape) - 1 - dim))
    return gain


def bell_draw(stream_key, shape, scale, limit, cuts=(), held_as=jnp.bfloat16):
    level = level_of(stream_key, shape, cuts, -0.22, 0.18) if cuts else 1.0
    values = jax.random.normal(stream_key, shape, jnp.float32) * scale * level
    return jnp.minimum(jnp.maximum(values, -limit), limit).astype(held_as)


def heavy_noise(own_key, dims, scale, most, shards, heavy, kind=jnp.bfloat16):
    array = scale * jax.random.normal(own_key, dims, jnp.float32)
    if shards:
        array = array * level_of(own_key, dims, shards, -0.22, 0.18)
    return jnp.clip(strengthened(array, jax.random.fold_in(own_key, 3), *heavy), -most, most).astype(kind)


def setup_inputs(seed: int = 0) -> dict:
    splits = jax.random.split(jax.random.key(seed), 16)
    latents = bell_draw(splits[0], (IMAGES, SLOTS, D), 1.0, 6.0, ((0, 32),))
    condition = bell_draw(splits[1], (IMAGES, D), 1.0, 6.0, ((0, 32),))
    bucket = draw_bucket(jax.random.fold_in(splits[15], 71), 0)
    keep_slots = draw_keep_slots(jax.random.fold_in(splits[15], 71), 0)
    modulation_weight = bell_draw(splits[4], (D, 6 * D), D ** -0.5, 0.1875, ((0, 8),))
    modulation_bias = bell_draw(splits[5], (6 * D,), 0.3, 1.5, ((0, 8),))
    projection_weight = bell_draw(splits[6], (D, 3 * D), D ** -0.5, 0.1875, ((0, 8),))
    query_value_bias = bell_draw(splits[7], (2 * D,), 0.3, 1.5, ((0, 8),))
    output_weight = bell_draw(splits[8], (D, D), (D // 16) ** -0.5, 0.75, ((0, 8),))
    output_bias = bell_draw(splits[9], (D,), 0.3, 1.5, ((0, 8),))
    expand_weight = bell_draw(splits[10], (D, MLP), D ** -0.5, 0.1875, ((0, 8),))
    expand_bias = bell_draw(splits[11], (MLP,), 0.5, 2.5, ((0, 8),))
    reduce_weight = bell_draw(splits[12], (MLP, D), (MLP // 2) ** -0.5, 0.125, ((0, 8),))
    reduce_bias = bell_draw(splits[13], (D,), 0.3, 1.5, ((0, 8),))
    cotangent = heavy_noise(splits[14], (IMAGES, SLOTS, D), 1.0, 6.0, ((0, 32),), (0, 2, 32, 2.75))
    return {"latents": latents, "condition": condition, "bucket": bucket, "keep_slots": keep_slots, "modulation_weight": modulation_weight, "modulation_bias": modulation_bias, "projection_weight": projection_weight, "query_value_bias": query_value_bias, "output_weight": output_weight, "output_bias": output_bias, "expand_weight": expand_weight, "expand_bias": expand_bias, "reduce_weight": reduce_weight, "reduce_bias": reduce_bias, "cotangent": cotangent}


@jax.custom_vjp
def low(v):
    return lax.optimization_barrier(v.astype(jnp.bfloat16)).astype(jnp.float32)

@jax.custom_vjp
def low_back(v):
    return v

def low_keep(v):
    return (low(v), None)

def low_pass(kept, grad):
    return (grad,)

def back_keep(v):
    return (v, None)

def back_low(kept, grad):
    return (low(grad),)
low.defvjp(low_keep, low_pass)
low_back.defvjp(back_keep, back_low)
highest = lax.Precision.HIGHEST
batch_images = 16

def round_both(v):
    return low_back(low(v))

def layer_norm(rows_in):
    row_mean = lax.optimization_barrier(jnp.mean(rows_in, axis=-1, keepdims=True))
    centred = rows_in - row_mean
    row_var = lax.optimization_barrier(jnp.mean(centred * centred, axis=-1, keepdims=True))
    return centred * lax.rsqrt(row_var + 1e-06)

def forward(kept, condition_in, live_rows, params):
    mod_w, mod_b, proj_w, qv_b, out_w, out_b, exp_w, exp_b, red_w, red_b = params
    model_width = kept.shape[-1]
    group_size, kept_rows = (kept.shape[0], kept.shape[1])
    cond_act = low(jax.nn.silu(condition_in))
    modulation = low_back(jnp.einsum('gd,de->ge', cond_act, mod_w, precision=highest) + mod_b)
    pieces = [modulation[:, None, i * model_width:(i + 1) * model_width] for i in range(6)]
    shift_attn, scale_attn, gate_attn, shift_mlp, scale_mlp, gate_mlp = pieces
    normed_one = low(layer_norm(kept) * (1.0 + scale_attn) + shift_attn)
    projected = jnp.einsum('grd,de->gre', normed_one, proj_w, precision=highest)
    shape_heads = (group_size, kept_rows, HEADS, HEAD_DIM)
    query_rows = round_both(projected[..., :model_width] + qv_b[:model_width]).reshape(shape_heads)
    key_rows = round_both(projected[..., model_width:2 * model_width]).reshape(shape_heads)
    value_rows = round_both(projected[..., 2 * model_width:] + qv_b[model_width:]).reshape(shape_heads)
    scores = low_back(jnp.einsum('gqhd,gkhd->ghqk', query_rows, key_rows, precision=highest) * HEAD_DIM ** (-0.5))
    scores = jnp.where(live_rows[:, None, None, :], scores, -1e+30)
    probs = jax.nn.softmax(scores, axis=-1)
    attended = round_both(jnp.einsum('ghqk,gkhd->gqhd', low(probs), value_rows, precision=highest))
    attended = attended.reshape(group_size, kept_rows, model_width)
    branch_attn = low_back(jnp.einsum('grd,de->gre', attended, out_w, precision=highest) + out_b)
    mixed = kept + gate_attn * branch_attn
    normed_two = low(layer_norm(mixed) * (1.0 + scale_mlp) + shift_mlp)
    hidden = low_back(jnp.einsum('grd,dm->grm', normed_two, exp_w, precision=highest) + exp_b)
    activation = low(jax.nn.gelu(hidden, approximate=True))
    branch_mlp = low_back(jnp.einsum('grm,md->grd', activation, red_w, precision=highest) + red_b)
    return mixed + gate_mlp * branch_mlp

def place_rows(target_rows, target_index, new_rows):
    return target_rows.at[target_index].set(new_rows, mode='drop')

def reference(latents, condition, bucket, keep_slots, modulation_weight, modulation_bias, projection_weight, query_value_bias, output_weight, output_bias, expand_weight, expand_bias, reduce_weight, reduce_bias, cotangent):
    params = tuple((p.astype(jnp.float32) for p in (modulation_weight, modulation_bias, projection_weight, query_value_bias, output_weight, output_bias, expand_weight, expand_bias, reduce_weight, reduce_bias)))
    image_count, slot_count, model_width = latents.shape
    kept_rows = keep_slots.shape[1]
    step_count = image_count // batch_images

    def group(carry, step_index):
        first_image = step_index * batch_images
        x_group = lax.dynamic_slice_in_dim(latents, first_image, batch_images, 0).astype(jnp.float32)
        cond_group = lax.dynamic_slice_in_dim(condition, first_image, batch_images, 0).astype(jnp.float32)
        bucket_group = lax.dynamic_slice_in_dim(bucket, first_image, batch_images, 0)
        keep_group = lax.dynamic_slice_in_dim(keep_slots, first_image, batch_images, 0)
        cot_group = lax.dynamic_slice_in_dim(cotangent, first_image, batch_images, 0).astype(jnp.float32)
        live_count = jnp.where(bucket_group == 0, slot_count, slot_count - 16) // 2
        live_rows = jnp.arange(kept_rows, dtype=jnp.int32)[None, :] < live_count[:, None]
        kept = jnp.take_along_axis(x_group, keep_group[:, :, None], axis=1)

        def run(kept_in, cond_in, *weights):
            return forward(kept_in, cond_in, live_rows, weights)
        result, pull = jax.vjp(run, kept, cond_group, *params)
        grad_rows = jnp.take_along_axis(cot_group, keep_group[:, :, None], axis=1) * live_rows[:, :, None].astype(jnp.float32)
        gradients = pull(grad_rows)
        target = jnp.where(live_rows, keep_group, slot_count).astype(jnp.int32)
        out_group = jax.vmap(place_rows)(x_group, target, result).astype(jnp.bfloat16)
        grad_group = jax.vmap(place_rows)(cot_group, target, gradients[0]).astype(jnp.bfloat16)
        summed = tuple((c + g for c, g in zip(carry, gradients[2:])))
        return (summed, (out_group, grad_group, gradients[1]))
    start_sums = tuple((jnp.zeros(p.shape, jnp.float32) for p in params))
    weight_grads, stacked = lax.scan(group, start_sums, jnp.arange(step_count, dtype=jnp.int32))
    block_out = stacked[0].reshape(image_count, slot_count, model_width)
    grad_latents = stacked[1].reshape(image_count, slot_count, model_width)
    grad_condition = stacked[2].reshape(image_count, model_width)
    return (block_out, grad_latents, grad_condition, weight_grads[0], weight_grads[1], weight_grads[2], weight_grads[3], weight_grads[4], weight_grads[5], weight_grads[6], weight_grads[7], weight_grads[8], weight_grads[9])
```

```python
import jax
import jax.numpy as jnp
from jax import lax
from jax.sharding import PartitionSpec as P

HEADS = 16
HEAD_DIM = 72


def layer_norm(rows_in):
    row_mean = jnp.mean(rows_in, axis=-1, keepdims=True)
    centred = rows_in - row_mean
    row_var = jnp.mean(centred * centred, axis=-1, keepdims=True)
    return centred * lax.rsqrt(row_var + 1e-06)


def modulate(rows_in, shift_part, scale_part):
    return layer_norm(rows_in) * (1.0 + scale_part) + shift_part


def gelu_tanh(values_in):
    return jax.nn.gelu(values_in, approximate=True)


def place_rows(target_rows, target_index, new_rows):
    return target_rows.at[target_index].set(new_rows, mode="drop")


def column_sums(rows_in):
    return jnp.sum(rows_in.astype(jnp.float32), axis=0)


def local(
    latents,
    condition,
    bucket,
    keep_slots,
    modulation_weight,
    modulation_bias,
    projection_weight,
    query_value_bias,
    output_weight,
    output_bias,
    expand_weight,
    expand_bias,
    reduce_weight,
    reduce_bias,
    cotangent,
):
    f32 = jnp.float32
    bf16 = jnp.bfloat16
    images, slot_count, model_width = latents.shape
    kept_rows = keep_slots.shape[1]
    row_count = images * kept_rows
    score_scale = HEAD_DIM ** (-0.5)
    shape_heads = (images, kept_rows, HEADS, HEAD_DIM)
    (
        full_mod_w,
        full_mod_b,
        full_proj_w,
        full_qv_b,
        full_out_w,
        full_out_b,
        full_exp_w,
        full_exp_b,
        full_red_w,
        full_red_b,
    ) = (
        lax.all_gather(modulation_weight, "fsdp", axis=0, tiled=True),
        lax.all_gather(modulation_bias, "fsdp", axis=0, tiled=True),
        lax.all_gather(projection_weight, "fsdp", axis=0, tiled=True),
        lax.all_gather(query_value_bias, "fsdp", axis=0, tiled=True),
        lax.all_gather(output_weight, "fsdp", axis=0, tiled=True),
        lax.all_gather(output_bias, "fsdp", axis=0, tiled=True),
        lax.all_gather(expand_weight, "fsdp", axis=0, tiled=True),
        lax.all_gather(expand_bias, "fsdp", axis=0, tiled=True),
        lax.all_gather(reduce_weight, "fsdp", axis=0, tiled=True),
        lax.all_gather(reduce_bias, "fsdp", axis=0, tiled=True),
    )
    live_count = jnp.where(bucket == 0, slot_count, slot_count - 16) // 2
    live_rows = jnp.arange(kept_rows, dtype=jnp.int32)[None, :] < live_count[:, None]
    live_float = live_rows.astype(f32)[:, :, None]
    gather_index = keep_slots[:, :, None]
    kept = jnp.take_along_axis(latents, gather_index, axis=1).astype(f32)
    cond_float = condition.astype(f32)
    cond_act = jax.nn.silu(cond_float).astype(bf16)
    modulation = jnp.dot(cond_act, full_mod_w, preferred_element_type=f32) + full_mod_b.astype(f32)
    pieces = [modulation[:, None, i * model_width : (i + 1) * model_width] for i in range(6)]
    shift_attn, scale_attn, gate_attn, shift_mlp, scale_mlp, gate_mlp = pieces
    normed_one = modulate(kept, shift_attn, scale_attn).astype(bf16).reshape(row_count, model_width)
    projected = jnp.dot(normed_one, full_proj_w, preferred_element_type=f32)
    bias_qv = full_qv_b.astype(f32)
    query_rows = (
        (projected[:, :model_width] + bias_qv[:model_width]).astype(bf16).reshape(shape_heads)
    )
    key_rows = projected[:, model_width : 2 * model_width].astype(bf16).reshape(shape_heads)
    value_rows = (
        (projected[:, 2 * model_width :] + bias_qv[model_width:]).astype(bf16).reshape(shape_heads)
    )

    def masked_scores(queries, keys_in):
        raw = (
            jnp.einsum("bqhd,bkhd->bhqk", queries, keys_in, preferred_element_type=f32)
            * score_scale
        )
        return jnp.where(live_rows[:, None, None, :], raw, -1e30)

    scores = masked_scores(query_rows, key_rows)
    row_max = jnp.max(scores, axis=-1, keepdims=True)
    row_total = jnp.sum(jnp.exp(scores - row_max), axis=-1, keepdims=True)
    log_total = row_max + jnp.log(row_total)
    probs = jnp.exp(scores - log_total)
    attended = (
        jnp.einsum("bhqk,bkhd->bqhd", probs.astype(bf16), value_rows, preferred_element_type=f32)
        .astype(bf16)
        .reshape(row_count, model_width)
    )
    branch_attn = (
        jnp.dot(attended, full_out_w, preferred_element_type=f32) + full_out_b.astype(f32)
    ).reshape(images, kept_rows, model_width)
    mixed = kept + gate_attn * branch_attn
    normed_two = modulate(mixed, shift_mlp, scale_mlp).astype(bf16).reshape(row_count, model_width)
    hidden = jnp.dot(normed_two, full_exp_w, preferred_element_type=f32) + full_exp_b.astype(f32)
    activation = gelu_tanh(hidden).astype(bf16)
    branch_mlp = (
        jnp.dot(activation, full_red_w, preferred_element_type=f32) + full_red_b.astype(f32)
    ).reshape(images, kept_rows, model_width)
    result = mixed + gate_mlp * branch_mlp
    target = jnp.where(live_rows, keep_slots, slot_count)
    block_out = jax.vmap(place_rows)(latents, target, result.astype(bf16))
    back_mod_w, back_proj_w, back_out_w, back_exp_w, back_red_w = (
        lax.all_gather(modulation_weight, "fsdp", axis=0, tiled=True),
        lax.all_gather(projection_weight, "fsdp", axis=0, tiled=True),
        lax.all_gather(output_weight, "fsdp", axis=0, tiled=True),
        lax.all_gather(expand_weight, "fsdp", axis=0, tiled=True),
        lax.all_gather(reduce_weight, "fsdp", axis=0, tiled=True),
    )
    grad_rows = jnp.take_along_axis(cotangent, gather_index, axis=1).astype(f32) * live_float
    grad_gate_mlp = jnp.sum(grad_rows * branch_mlp, axis=1)
    grad_mlp = (gate_mlp * grad_rows).astype(bf16).reshape(row_count, model_width)
    local_red_w = jnp.einsum("rm,rd->md", activation, grad_mlp, preferred_element_type=f32)
    local_red_b = column_sums(grad_mlp)
    grad_act = jnp.einsum("rd,md->rm", grad_mlp, back_red_w, preferred_element_type=f32)
    gelu_pull = jax.vjp(gelu_tanh, hidden)[1]
    grad_hidden = gelu_pull(grad_act)[0].astype(bf16)
    local_exp_w = jnp.einsum("rd,rm->dm", normed_two, grad_hidden, preferred_element_type=f32)
    local_exp_b = column_sums(grad_hidden)
    mlp_red_w, mlp_red_b, mlp_exp_w, mlp_exp_b = (
        lax.psum_scatter(
            local_red_w.astype(jnp.bfloat16), "fsdp", scatter_dimension=0, tiled=True
        ).astype(jnp.float32),
        lax.psum_scatter(
            local_red_b.astype(jnp.bfloat16), "fsdp", scatter_dimension=0, tiled=True
        ).astype(jnp.float32),
        lax.psum_scatter(
            local_exp_w.astype(jnp.bfloat16), "fsdp", scatter_dimension=0, tiled=True
        ).astype(jnp.float32),
        lax.psum_scatter(
            local_exp_b.astype(jnp.bfloat16), "fsdp", scatter_dimension=0, tiled=True
        ).astype(jnp.float32),
    )
    grad_normed_two = jnp.einsum(
        "rm,dm->rd", grad_hidden, back_exp_w, preferred_element_type=f32
    ).reshape(images, kept_rows, model_width)
    pull_two = jax.vjp(modulate, mixed, shift_mlp, scale_mlp)[1]
    grad_mixed_ln, grad_shift_mlp, grad_scale_mlp = pull_two(grad_normed_two)
    grad_mixed = grad_rows + grad_mixed_ln
    grad_gate_attn = jnp.sum(grad_mixed * branch_attn, axis=1)
    grad_attn = (gate_attn * grad_mixed).astype(bf16).reshape(row_count, model_width)
    local_out_w = jnp.einsum("rd,re->de", attended, grad_attn, preferred_element_type=f32)
    local_out_b = column_sums(grad_attn)
    grad_attended = (
        jnp.einsum("re,de->rd", grad_attn, back_out_w, preferred_element_type=f32)
        .astype(bf16)
        .reshape(shape_heads)
    )
    scores_again = masked_scores(query_rows, key_rows)
    probs_again = jnp.exp(scores_again - log_total)
    grad_values = jnp.einsum(
        "bhqk,bqhd->bkhd", probs_again.astype(bf16), grad_attended, preferred_element_type=f32
    ).astype(bf16)
    grad_probs = jnp.einsum(
        "bqhd,bkhd->bhqk", grad_attended, value_rows, preferred_element_type=f32
    )
    row_inner = jnp.sum(grad_probs * probs_again, axis=-1, keepdims=True)
    grad_scores = (probs_again * (grad_probs - row_inner)).astype(bf16)
    grad_query = (
        jnp.einsum("bhqk,bkhd->bqhd", grad_scores, key_rows, preferred_element_type=f32)
        * score_scale
    ).astype(bf16)
    grad_keys = (
        jnp.einsum("bhqk,bqhd->bkhd", grad_scores, query_rows, preferred_element_type=f32)
        * score_scale
    ).astype(bf16)
    grad_projected = jnp.concatenate(
        [
            grad_query.reshape(row_count, model_width),
            grad_keys.reshape(row_count, model_width),
            grad_values.reshape(row_count, model_width),
        ],
        axis=1,
    )
    local_proj_w = jnp.einsum("rd,re->de", normed_one, grad_projected, preferred_element_type=f32)
    local_qv_b = jnp.concatenate(
        [
            column_sums(grad_projected[:, :model_width]),
            column_sums(grad_projected[:, 2 * model_width :]),
        ]
    )
    grad_normed_one = jnp.einsum(
        "re,de->rd", grad_projected, back_proj_w, preferred_element_type=f32
    ).reshape(images, kept_rows, model_width)
    pull_one = jax.vjp(modulate, kept, shift_attn, scale_attn)[1]
    grad_kept_ln, grad_shift_attn, grad_scale_attn = pull_one(grad_normed_one)
    grad_kept = grad_mixed + grad_kept_ln
    grad_latents = jax.vmap(place_rows)(cotangent, target, grad_kept.astype(bf16))
    grad_modulation = jnp.concatenate(
        [
            grad_shift_attn[:, 0],
            grad_scale_attn[:, 0],
            grad_gate_attn,
            grad_shift_mlp[:, 0],
            grad_scale_mlp[:, 0],
            grad_gate_mlp,
        ],
        axis=1,
    ).astype(bf16)
    grad_cond_act = jnp.einsum("be,de->bd", grad_modulation, back_mod_w, preferred_element_type=f32)
    silu_pull = jax.vjp(jax.nn.silu, cond_float)[1]
    grad_condition = silu_pull(grad_cond_act)[0]
    local_mod_w = jnp.einsum("bd,be->de", cond_act, grad_modulation, preferred_element_type=f32)
    local_mod_b = column_sums(grad_modulation)
    rest_mod_w, rest_mod_b, rest_proj_w, rest_qv_b, rest_out_w, rest_out_b = (
        lax.psum_scatter(
            local_mod_w.astype(jnp.bfloat16), "fsdp", scatter_dimension=0, tiled=True
        ).astype(jnp.float32),
        lax.psum_scatter(
            local_mod_b.astype(jnp.bfloat16), "fsdp", scatter_dimension=0, tiled=True
        ).astype(jnp.float32),
        lax.psum_scatter(
            local_proj_w.astype(jnp.bfloat16), "fsdp", scatter_dimension=0, tiled=True
        ).astype(jnp.float32),
        lax.psum_scatter(
            local_qv_b.astype(jnp.bfloat16), "fsdp", scatter_dimension=0, tiled=True
        ).astype(jnp.float32),
        lax.psum_scatter(
            local_out_w.astype(jnp.bfloat16), "fsdp", scatter_dimension=0, tiled=True
        ).astype(jnp.float32),
        lax.psum_scatter(
            local_out_b.astype(jnp.bfloat16), "fsdp", scatter_dimension=0, tiled=True
        ).astype(jnp.float32),
    )
    shares = (
        lax.psum_scatter(
            rest_mod_w.astype(jnp.bfloat16), "replica", scatter_dimension=1, tiled=True
        ).astype(jnp.float32),
        lax.psum_scatter(
            rest_proj_w.astype(jnp.bfloat16), "replica", scatter_dimension=1, tiled=True
        ).astype(jnp.float32),
        lax.psum_scatter(
            rest_out_w.astype(jnp.bfloat16), "replica", scatter_dimension=1, tiled=True
        ).astype(jnp.float32),
        lax.psum_scatter(
            mlp_exp_w.astype(jnp.bfloat16), "replica", scatter_dimension=1, tiled=True
        ).astype(jnp.float32),
        lax.psum_scatter(
            mlp_red_w.astype(jnp.bfloat16), "replica", scatter_dimension=1, tiled=True
        ).astype(jnp.float32),
    )
    sum_mod_w, sum_proj_w, sum_out_w, sum_exp_w, sum_red_w = (
        lax.all_gather(shares[0].astype(jnp.bfloat16), "replica", axis=1, tiled=True).astype(
            jnp.float32
        ),
        lax.all_gather(shares[1].astype(jnp.bfloat16), "replica", axis=1, tiled=True).astype(
            jnp.float32
        ),
        lax.all_gather(shares[2].astype(jnp.bfloat16), "replica", axis=1, tiled=True).astype(
            jnp.float32
        ),
        lax.all_gather(shares[3].astype(jnp.bfloat16), "replica", axis=1, tiled=True).astype(
            jnp.float32
        ),
        lax.all_gather(shares[4].astype(jnp.bfloat16), "replica", axis=1, tiled=True).astype(
            jnp.float32
        ),
    )
    sum_mod_b, sum_qv_b, sum_out_b, sum_exp_b, sum_red_b = lax.psum(
        (rest_mod_b, rest_qv_b, rest_out_b, mlp_exp_b, mlp_red_b), "replica"
    )
    return (
        block_out,
        grad_latents,
        grad_condition,
        sum_mod_w,
        sum_mod_b,
        sum_proj_w,
        sum_qv_b,
        sum_out_w,
        sum_out_b,
        sum_exp_w,
        sum_exp_b,
        sum_red_w,
        sum_red_b,
    )


def local_tp(
    latents,
    condition,
    bucket,
    keep_slots,
    modulation_weight,
    modulation_bias,
    projection_weight,
    query_value_bias,
    output_weight,
    output_bias,
    expand_weight,
    expand_bias,
    reduce_weight,
    reduce_bias,
    cotangent,
):
    f32 = jnp.float32
    bf16 = jnp.bfloat16
    n = lax.axis_size("fsdp")
    copies = lax.axis_size("replica")
    me = lax.axis_index("fsdp")
    images, slot_count, width = latents.shape
    kept_rows = keep_slots.shape[1]
    rows = images * kept_rows
    group_images = images * n
    group_rows = rows * n
    heads = HEADS // n
    part = width // n
    scale = HEAD_DIM ** (-0.5)

    def gather(value, axis=0):
        return lax.all_gather(value, "fsdp", axis=axis, tiled=True)

    def scatter(value):
        return lax.psum_scatter(value, "fsdp", scatter_dimension=0, tiled=True)

    def exchange(value, split, concat):
        return lax.all_to_all(value, "fsdp", split, concat, tiled=True)

    cond_float = condition.astype(f32)
    cond_act = jax.nn.silu(cond_float).astype(bf16)
    cond_cols = exchange(cond_act, 1, 0)
    modulation = scatter(jnp.dot(cond_cols, modulation_weight, preferred_element_type=f32))
    cuts = [modulation_bias.shape[0], query_value_bias.shape[0], output_bias.shape[0]]
    biases = gather(
        jnp.concatenate([modulation_bias, query_value_bias, output_bias, reduce_bias])[None]
    )
    mod_b = biases[:, : cuts[0]].reshape(-1).astype(f32)
    qv_b = biases[:, cuts[0] : cuts[0] + cuts[1]].reshape(2, n, part).astype(f32)
    out_b = biases[:, cuts[0] + cuts[1] : cuts[0] + cuts[1] + cuts[2]].reshape(-1).astype(f32)
    red_b = biases[:, cuts[0] + cuts[1] + cuts[2] :].reshape(-1).astype(f32)
    my_qv_b = lax.dynamic_index_in_dim(qv_b, me, 1, keepdims=False)
    modulation = modulation + mod_b
    pieces = [modulation[:, None, i * width : (i + 1) * width] for i in range(6)]
    shift_attn, scale_attn, gate_attn, shift_mlp, scale_mlp, gate_mlp = pieces

    proj = exchange(
        projection_weight.reshape(part, 3, n, part).transpose(2, 0, 1, 3), 0, 1
    ).reshape(width, 3 * part)
    exp_w = exchange(expand_weight, 1, 0)

    live_count = jnp.where(bucket == 0, slot_count, slot_count - 16) // 2
    live_rows = jnp.arange(kept_rows, dtype=jnp.int32)[None, :] < live_count[:, None]
    live_float = live_rows.astype(f32)[:, :, None]
    live_all = gather(live_rows.astype(f32)) > 0.5
    gather_index = keep_slots[:, :, None]
    kept = jnp.take_along_axis(latents, gather_index, axis=1).astype(f32)
    grad_rows = jnp.take_along_axis(cotangent, gather_index, axis=1).astype(f32) * live_float
    grad_mlp = (gate_mlp * grad_rows).astype(bf16).reshape(rows, width)
    all_grad_mlp = gather(grad_mlp)

    normed_one = gather(modulate(kept, shift_attn, scale_attn).astype(bf16).reshape(rows, width))
    projected = jnp.dot(normed_one, proj, preferred_element_type=f32)
    head_shape = (group_images, kept_rows, heads, HEAD_DIM)
    query = (projected[:, :part] + my_qv_b[0]).astype(bf16).reshape(head_shape)
    keys = projected[:, part : 2 * part].astype(bf16).reshape(head_shape)
    values = (projected[:, 2 * part :] + my_qv_b[1]).astype(bf16).reshape(head_shape)
    scores = jnp.einsum("bqhd,bkhd->bhqk", query, keys, preferred_element_type=f32) * scale
    scores = jnp.where(live_all[:, None, None, :], scores, -1e30)
    probs = jax.nn.softmax(scores, axis=-1)
    probs_low = probs.astype(bf16)
    attended = (
        jnp.einsum("bhqk,bkhd->bqhd", probs_low, values, preferred_element_type=f32)
        .astype(bf16)
        .reshape(group_rows, part)
    )
    branch_attn = scatter(
        jnp.dot(attended, output_weight, preferred_element_type=f32).astype(bf16)
    ).astype(f32)
    branch_attn = (branch_attn + out_b).reshape(images, kept_rows, width)
    mixed = kept + gate_attn * branch_attn
    normed_two = gather(modulate(mixed, shift_mlp, scale_mlp).astype(bf16).reshape(rows, width))
    hidden = jnp.dot(normed_two, exp_w, preferred_element_type=f32) + expand_bias.astype(f32)
    activation, gelu_pull = jax.vjp(gelu_tanh, hidden)
    activation = activation.astype(bf16)
    branch_mlp = scatter(
        jnp.dot(activation, reduce_weight, preferred_element_type=f32).astype(bf16)
    ).astype(f32)
    branch_mlp = (branch_mlp + red_b).reshape(images, kept_rows, width)
    result = mixed + gate_mlp * branch_mlp
    target = jnp.where(live_rows, keep_slots, slot_count)
    block_out = jax.vmap(place_rows)(latents, target, result.astype(bf16))
    grad_gate_mlp = jnp.sum(grad_rows * branch_mlp, axis=1)

    grad_act = jnp.einsum("rd,md->rm", all_grad_mlp, reduce_weight, preferred_element_type=f32)
    grad_hidden = gelu_pull(grad_act)[0].astype(bf16)
    local_red = jnp.einsum("rm,rd->md", activation, all_grad_mlp, preferred_element_type=f32)
    local_exp = jnp.einsum("rd,rm->dm", normed_two, grad_hidden, preferred_element_type=f32)
    grad_normed_two = scatter(
        jnp.einsum("rm,dm->rd", grad_hidden, exp_w, preferred_element_type=f32).astype(bf16)
    ).astype(f32)
    pull_two = jax.vjp(modulate, mixed, shift_mlp, scale_mlp)[1]
    grad_mixed_ln, grad_shift_mlp, grad_scale_mlp = pull_two(
        grad_normed_two.reshape(images, kept_rows, width)
    )
    grad_mixed = grad_rows + grad_mixed_ln
    grad_gate_attn = jnp.sum(grad_mixed * branch_attn, axis=1)
    grad_attn = gather((gate_attn * grad_mixed).astype(bf16).reshape(rows, width))
    local_out = jnp.einsum("rd,re->de", attended, grad_attn, preferred_element_type=f32)
    grad_attended = (
        jnp.einsum("re,de->rd", grad_attn, output_weight, preferred_element_type=f32)
        .astype(bf16)
        .reshape(head_shape)
    )
    grad_values = jnp.einsum(
        "bhqk,bqhd->bkhd", probs_low, grad_attended, preferred_element_type=f32
    ).astype(bf16)
    grad_probs = jnp.einsum("bqhd,bkhd->bhqk", grad_attended, values, preferred_element_type=f32)
    row_inner = jnp.sum(grad_probs * probs, axis=-1, keepdims=True)
    grad_scores = (probs * (grad_probs - row_inner)).astype(bf16)
    grad_query = (
        jnp.einsum("bhqk,bkhd->bqhd", grad_scores, keys, preferred_element_type=f32) * scale
    ).astype(bf16)
    grad_keys = (
        jnp.einsum("bhqk,bqhd->bkhd", grad_scores, query, preferred_element_type=f32) * scale
    ).astype(bf16)
    grad_projected = jnp.concatenate(
        [g.reshape(group_rows, part) for g in (grad_query, grad_keys, grad_values)], axis=1
    )
    local_proj = jnp.einsum("rd,re->de", normed_one, grad_projected, preferred_element_type=f32)
    grad_normed_one = scatter(
        jnp.einsum("re,de->rd", grad_projected, proj, preferred_element_type=f32).astype(bf16)
    ).astype(f32)
    pull_one = jax.vjp(modulate, kept, shift_attn, scale_attn)[1]
    grad_kept_ln, grad_shift_attn, grad_scale_attn = pull_one(
        grad_normed_one.reshape(images, kept_rows, width)
    )
    grad_kept = grad_mixed + grad_kept_ln
    grad_latents = jax.vmap(place_rows)(cotangent, target, grad_kept.astype(bf16))
    grad_modulation = jnp.concatenate(
        [
            grad_shift_attn[:, 0],
            grad_scale_attn[:, 0],
            grad_gate_attn,
            grad_shift_mlp[:, 0],
            grad_scale_mlp[:, 0],
            grad_gate_mlp,
        ],
        axis=1,
    ).astype(bf16)

    every = ("replica", "fsdp")
    all_grad_mod = lax.all_gather(grad_modulation, every, axis=0, tiled=True)
    all_cond = lax.all_gather(cond_cols, "replica", axis=0, tiled=True)
    sum_mod_w = jnp.einsum("bd,be->de", all_cond, all_grad_mod, preferred_element_type=f32)
    mod_part = modulation_bias.shape[0]
    sum_mod_b = column_sums(lax.dynamic_slice_in_dim(all_grad_mod, me * mod_part, mod_part, 1))
    group_grad_mod = lax.dynamic_slice_in_dim(
        all_grad_mod, lax.axis_index("replica") * group_images, group_images, 0
    )
    grad_cond_cols = jnp.einsum(
        "be,de->bd", group_grad_mod, modulation_weight, preferred_element_type=f32
    )
    grad_cond_act = exchange(grad_cond_cols, 0, 1)
    grad_condition = jax.vjp(jax.nn.silu, cond_float)[1](grad_cond_act)[0]

    local_exp = exchange(local_exp.astype(bf16), 0, 1)
    local_proj = (
        exchange(local_proj.astype(bf16).reshape(n, part, 3 * part), 0, 0)
        .reshape(n, part, 3, part)
        .transpose(1, 2, 0, 3)
        .reshape(part, 3 * width)
    )
    hidden_part = reduce_weight.shape[0]
    flat = jnp.concatenate(
        [
            local_proj,
            local_out.astype(bf16),
            local_exp,
            local_red.astype(bf16).reshape(part, hidden_part // part * width),
        ],
        axis=1,
    )
    flat = lax.psum_scatter(flat, "replica", scatter_dimension=1, tiled=True)
    flat = lax.all_gather(flat, "replica", axis=1, tiled=True).astype(f32)
    ends = [3 * width, 4 * width, 4 * width + expand_weight.shape[1]]
    sum_proj_w = flat[:, : ends[0]]
    sum_out_w = flat[:, ends[0] : ends[1]]
    sum_exp_w = flat[:, ends[1] : ends[2]]
    sum_red_w = flat[:, ends[2] :].reshape(hidden_part, width)

    qv_sums = column_sums(grad_projected)
    whole_red = lax.dynamic_slice_in_dim(column_sums(all_grad_mlp), me * part, part, 0)
    whole_out = lax.dynamic_slice_in_dim(column_sums(grad_attn), me * part, part, 0)
    exp_sums = column_sums(grad_hidden)
    sums = lax.psum(
        jnp.concatenate([qv_sums[:part], qv_sums[2 * part :], whole_out, exp_sums, whole_red]),
        "replica",
    )
    qv_all = gather(sums[: 2 * part].reshape(1, 2, part), 0).transpose(1, 0, 2).reshape(-1)
    sum_qv_b = lax.dynamic_slice_in_dim(qv_all, me * 2 * part, 2 * part, 0)
    sum_out_b = sums[2 * part : 3 * part]
    sum_exp_b = sums[3 * part : 3 * part + hidden_part]
    sum_red_b = sums[3 * part + hidden_part :]
    return (
        block_out,
        grad_latents,
        grad_condition,
        sum_mod_w,
        sum_mod_b,
        sum_proj_w,
        sum_qv_b,
        sum_out_w,
        sum_out_b,
        sum_exp_w,
        sum_exp_b,
        sum_red_w,
        sum_red_b,
    )


def solution(mesh):
    placed = (
        P(("replica", "fsdp"), None, None),
        P(("replica", "fsdp"), None),
        P(("replica", "fsdp")),
        P(("replica", "fsdp"), None),
        P("fsdp", None),
        P("fsdp"),
        P("fsdp", None),
        P("fsdp"),
        P("fsdp", None),
        P("fsdp"),
        P("fsdp", None),
        P("fsdp"),
        P("fsdp", None),
        P("fsdp"),
        P(("replica", "fsdp"), None, None),
    )
    body = local_tp if HEADS % mesh.shape["fsdp"] == 0 else local
    return jax.shard_map(
        body,
        mesh=mesh,
        in_specs=placed,
        out_specs=(
            P(("replica", "fsdp"), None, None),
            P(("replica", "fsdp"), None, None),
            P(("replica", "fsdp"), None),
            P("fsdp", None),
            P("fsdp"),
            P("fsdp", None),
            P("fsdp"),
            P("fsdp", None),
            P("fsdp"),
            P("fsdp", None),
            P("fsdp"),
            P("fsdp", None),
            P("fsdp"),
        ),
        check_vma=False,
    )
```

```python
import jax
import jax.numpy as jnp
from jax import lax
from jax.experimental import pallas as pl
from jax.experimental.pallas import tpu as pltpu
from jax.sharding import PartitionSpec as P

HEADS = 16
HEAD_DIM = 72


def layer_norm(rows_in):
    row_mean = jnp.mean(rows_in, axis=-1, keepdims=True)
    centred = rows_in - row_mean
    row_var = jnp.mean(centred * centred, axis=-1, keepdims=True)
    return centred * lax.rsqrt(row_var + 1e-06)


def modulate(rows_in, shift_part, scale_part):
    return layer_norm(rows_in) * (1.0 + scale_part) + shift_part


def gelu_tanh(values_in):
    return jax.nn.gelu(values_in, approximate=True)


def place_rows(target_rows, target_index, new_rows):
    return target_rows.at[target_index].set(new_rows, mode="drop")


def column_sums(rows_in):
    return jnp.sum(rows_in.astype(jnp.float32), axis=0)


def local(
    latents,
    condition,
    bucket,
    keep_slots,
    modulation_weight,
    modulation_bias,
    projection_weight,
    query_value_bias,
    output_weight,
    output_bias,
    expand_weight,
    expand_bias,
    reduce_weight,
    reduce_bias,
    cotangent,
):
    f32 = jnp.float32
    bf16 = jnp.bfloat16
    images, slot_count, model_width = latents.shape
    kept_rows = keep_slots.shape[1]
    row_count = images * kept_rows
    score_scale = HEAD_DIM ** (-0.5)
    shape_heads = (images, kept_rows, HEADS, HEAD_DIM)
    (
        full_mod_w,
        full_mod_b,
        full_proj_w,
        full_qv_b,
        full_out_w,
        full_out_b,
        full_exp_w,
        full_exp_b,
        full_red_w,
        full_red_b,
    ) = (
        lax.all_gather(modulation_weight, "fsdp", axis=0, tiled=True),
        lax.all_gather(modulation_bias, "fsdp", axis=0, tiled=True),
        lax.all_gather(projection_weight, "fsdp", axis=0, tiled=True),
        lax.all_gather(query_value_bias, "fsdp", axis=0, tiled=True),
        lax.all_gather(output_weight, "fsdp", axis=0, tiled=True),
        lax.all_gather(output_bias, "fsdp", axis=0, tiled=True),
        lax.all_gather(expand_weight, "fsdp", axis=0, tiled=True),
        lax.all_gather(expand_bias, "fsdp", axis=0, tiled=True),
        lax.all_gather(reduce_weight, "fsdp", axis=0, tiled=True),
        lax.all_gather(reduce_bias, "fsdp", axis=0, tiled=True),
    )
    live_count = jnp.where(bucket == 0, slot_count, slot_count - 16) // 2
    live_rows = jnp.arange(kept_rows, dtype=jnp.int32)[None, :] < live_count[:, None]
    live_float = live_rows.astype(f32)[:, :, None]
    gather_index = keep_slots[:, :, None]
    kept = jnp.take_along_axis(latents, gather_index, axis=1).astype(f32)
    cond_float = condition.astype(f32)
    cond_act = jax.nn.silu(cond_float).astype(bf16)
    modulation = jnp.dot(cond_act, full_mod_w, preferred_element_type=f32) + full_mod_b.astype(f32)
    pieces = [modulation[:, None, i * model_width : (i + 1) * model_width] for i in range(6)]
    shift_attn, scale_attn, gate_attn, shift_mlp, scale_mlp, gate_mlp = pieces
    normed_one = modulate(kept, shift_attn, scale_attn).astype(bf16).reshape(row_count, model_width)
    projected = jnp.dot(normed_one, full_proj_w, preferred_element_type=f32)
    bias_qv = full_qv_b.astype(f32)
    query_rows = (
        (projected[:, :model_width] + bias_qv[:model_width]).astype(bf16).reshape(shape_heads)
    )
    key_rows = projected[:, model_width : 2 * model_width].astype(bf16).reshape(shape_heads)
    value_rows = (
        (projected[:, 2 * model_width :] + bias_qv[model_width:]).astype(bf16).reshape(shape_heads)
    )

    def masked_scores(queries, keys_in):
        raw = (
            jnp.einsum("bqhd,bkhd->bhqk", queries, keys_in, preferred_element_type=f32)
            * score_scale
        )
        return jnp.where(live_rows[:, None, None, :], raw, -1e30)

    scores = masked_scores(query_rows, key_rows)
    row_max = jnp.max(scores, axis=-1, keepdims=True)
    row_total = jnp.sum(jnp.exp(scores - row_max), axis=-1, keepdims=True)
    log_total = row_max + jnp.log(row_total)
    probs = jnp.exp(scores - log_total)
    attended = (
        jnp.einsum("bhqk,bkhd->bqhd", probs.astype(bf16), value_rows, preferred_element_type=f32)
        .astype(bf16)
        .reshape(row_count, model_width)
    )
    branch_attn = (
        jnp.dot(attended, full_out_w, preferred_element_type=f32) + full_out_b.astype(f32)
    ).reshape(images, kept_rows, model_width)
    mixed = kept + gate_attn * branch_attn
    normed_two = modulate(mixed, shift_mlp, scale_mlp).astype(bf16).reshape(row_count, model_width)
    hidden = jnp.dot(normed_two, full_exp_w, preferred_element_type=f32) + full_exp_b.astype(f32)
    activation = gelu_tanh(hidden).astype(bf16)
    branch_mlp = (
        jnp.dot(activation, full_red_w, preferred_element_type=f32) + full_red_b.astype(f32)
    ).reshape(images, kept_rows, model_width)
    result = mixed + gate_mlp * branch_mlp
    target = jnp.where(live_rows, keep_slots, slot_count)
    block_out = jax.vmap(place_rows)(latents, target, result.astype(bf16))
    back_mod_w, back_proj_w, back_out_w, back_exp_w, back_red_w = (
        lax.all_gather(modulation_weight, "fsdp", axis=0, tiled=True),
        lax.all_gather(projection_weight, "fsdp", axis=0, tiled=True),
        lax.all_gather(output_weight, "fsdp", axis=0, tiled=True),
        lax.all_gather(expand_weight, "fsdp", axis=0, tiled=True),
        lax.all_gather(reduce_weight, "fsdp", axis=0, tiled=True),
    )
    grad_rows = jnp.take_along_axis(cotangent, gather_index, axis=1).astype(f32) * live_float
    grad_gate_mlp = jnp.sum(grad_rows * branch_mlp, axis=1)
    grad_mlp = (gate_mlp * grad_rows).astype(bf16).reshape(row_count, model_width)
    local_red_w = jnp.einsum("rm,rd->md", activation, grad_mlp, preferred_element_type=f32)
    local_red_b = column_sums(grad_mlp)
    grad_act = jnp.einsum("rd,md->rm", grad_mlp, back_red_w, preferred_element_type=f32)
    gelu_pull = jax.vjp(gelu_tanh, hidden)[1]
    grad_hidden = gelu_pull(grad_act)[0].astype(bf16)
    local_exp_w = jnp.einsum("rd,rm->dm", normed_two, grad_hidden, preferred_element_type=f32)
    local_exp_b = column_sums(grad_hidden)
    mlp_red_w, mlp_red_b, mlp_exp_w, mlp_exp_b = (
        lax.psum_scatter(
            local_red_w.astype(jnp.bfloat16), "fsdp", scatter_dimension=0, tiled=True
        ).astype(jnp.float32),
        lax.psum_scatter(
            local_red_b.astype(jnp.bfloat16), "fsdp", scatter_dimension=0, tiled=True
        ).astype(jnp.float32),
        lax.psum_scatter(
            local_exp_w.astype(jnp.bfloat16), "fsdp", scatter_dimension=0, tiled=True
        ).astype(jnp.float32),
        lax.psum_scatter(
            local_exp_b.astype(jnp.bfloat16), "fsdp", scatter_dimension=0, tiled=True
        ).astype(jnp.float32),
    )
    grad_normed_two = jnp.einsum(
        "rm,dm->rd", grad_hidden, back_exp_w, preferred_element_type=f32
    ).reshape(images, kept_rows, model_width)
    pull_two = jax.vjp(modulate, mixed, shift_mlp, scale_mlp)[1]
    grad_mixed_ln, grad_shift_mlp, grad_scale_mlp = pull_two(grad_normed_two)
    grad_mixed = grad_rows + grad_mixed_ln
    grad_gate_attn = jnp.sum(grad_mixed * branch_attn, axis=1)
    grad_attn = (gate_attn * grad_mixed).astype(bf16).reshape(row_count, model_width)
    local_out_w = jnp.einsum("rd,re->de", attended, grad_attn, preferred_element_type=f32)
    local_out_b = column_sums(grad_attn)
    grad_attended = (
        jnp.einsum("re,de->rd", grad_attn, back_out_w, preferred_element_type=f32)
        .astype(bf16)
        .reshape(shape_heads)
    )
    scores_again = masked_scores(query_rows, key_rows)
    probs_again = jnp.exp(scores_again - log_total)
    grad_values = jnp.einsum(
        "bhqk,bqhd->bkhd", probs_again.astype(bf16), grad_attended, preferred_element_type=f32
    ).astype(bf16)
    grad_probs = jnp.einsum(
        "bqhd,bkhd->bhqk", grad_attended, value_rows, preferred_element_type=f32
    )
    row_inner = jnp.sum(grad_probs * probs_again, axis=-1, keepdims=True)
    grad_scores = (probs_again * (grad_probs - row_inner)).astype(bf16)
    grad_query = (
        jnp.einsum("bhqk,bkhd->bqhd", grad_scores, key_rows, preferred_element_type=f32)
        * score_scale
    ).astype(bf16)
    grad_keys = (
        jnp.einsum("bhqk,bqhd->bkhd", grad_scores, query_rows, preferred_element_type=f32)
        * score_scale
    ).astype(bf16)
    grad_projected = jnp.concatenate(
        [
            grad_query.reshape(row_count, model_width),
            grad_keys.reshape(row_count, model_width),
            grad_values.reshape(row_count, model_width),
        ],
        axis=1,
    )
    local_proj_w = jnp.einsum("rd,re->de", normed_one, grad_projected, preferred_element_type=f32)
    local_qv_b = jnp.concatenate(
        [
            column_sums(grad_projected[:, :model_width]),
            column_sums(grad_projected[:, 2 * model_width :]),
        ]
    )
    grad_normed_one = jnp.einsum(
        "re,de->rd", grad_projected, back_proj_w, preferred_element_type=f32
    ).reshape(images, kept_rows, model_width)
    pull_one = jax.vjp(modulate, kept, shift_attn, scale_attn)[1]
    grad_kept_ln, grad_shift_attn, grad_scale_attn = pull_one(grad_normed_one)
    grad_kept = grad_mixed + grad_kept_ln
    grad_latents = jax.vmap(place_rows)(cotangent, target, grad_kept.astype(bf16))
    grad_modulation = jnp.concatenate(
        [
            grad_shift_attn[:, 0],
            grad_scale_attn[:, 0],
            grad_gate_attn,
            grad_shift_mlp[:, 0],
            grad_scale_mlp[:, 0],
            grad_gate_mlp,
        ],
        axis=1,
    ).astype(bf16)
    grad_cond_act = jnp.einsum("be,de->bd", grad_modulation, back_mod_w, preferred_element_type=f32)
    silu_pull = jax.vjp(jax.nn.silu, cond_float)[1]
    grad_condition = silu_pull(grad_cond_act)[0]
    local_mod_w = jnp.einsum("bd,be->de", cond_act, grad_modulation, preferred_element_type=f32)
    local_mod_b = column_sums(grad_modulation)
    rest_mod_w, rest_mod_b, rest_proj_w, rest_qv_b, rest_out_w, rest_out_b = (
        lax.psum_scatter(
            local_mod_w.astype(jnp.bfloat16), "fsdp", scatter_dimension=0, tiled=True
        ).astype(jnp.float32),
        lax.psum_scatter(
            local_mod_b.astype(jnp.bfloat16), "fsdp", scatter_dimension=0, tiled=True
        ).astype(jnp.float32),
        lax.psum_scatter(
            local_proj_w.astype(jnp.bfloat16), "fsdp", scatter_dimension=0, tiled=True
        ).astype(jnp.float32),
        lax.psum_scatter(
            local_qv_b.astype(jnp.bfloat16), "fsdp", scatter_dimension=0, tiled=True
        ).astype(jnp.float32),
        lax.psum_scatter(
            local_out_w.astype(jnp.bfloat16), "fsdp", scatter_dimension=0, tiled=True
        ).astype(jnp.float32),
        lax.psum_scatter(
            local_out_b.astype(jnp.bfloat16), "fsdp", scatter_dimension=0, tiled=True
        ).astype(jnp.float32),
    )
    shares = (
        lax.psum_scatter(
            rest_mod_w.astype(jnp.bfloat16), "replica", scatter_dimension=1, tiled=True
        ).astype(jnp.float32),
        lax.psum_scatter(
            rest_proj_w.astype(jnp.bfloat16), "replica", scatter_dimension=1, tiled=True
        ).astype(jnp.float32),
        lax.psum_scatter(
            rest_out_w.astype(jnp.bfloat16), "replica", scatter_dimension=1, tiled=True
        ).astype(jnp.float32),
        lax.psum_scatter(
            mlp_exp_w.astype(jnp.bfloat16), "replica", scatter_dimension=1, tiled=True
        ).astype(jnp.float32),
        lax.psum_scatter(
            mlp_red_w.astype(jnp.bfloat16), "replica", scatter_dimension=1, tiled=True
        ).astype(jnp.float32),
    )
    sum_mod_w, sum_proj_w, sum_out_w, sum_exp_w, sum_red_w = (
        lax.all_gather(shares[0].astype(jnp.bfloat16), "replica", axis=1, tiled=True).astype(
            jnp.float32
        ),
        lax.all_gather(shares[1].astype(jnp.bfloat16), "replica", axis=1, tiled=True).astype(
            jnp.float32
        ),
        lax.all_gather(shares[2].astype(jnp.bfloat16), "replica", axis=1, tiled=True).astype(
            jnp.float32
        ),
        lax.all_gather(shares[3].astype(jnp.bfloat16), "replica", axis=1, tiled=True).astype(
            jnp.float32
        ),
        lax.all_gather(shares[4].astype(jnp.bfloat16), "replica", axis=1, tiled=True).astype(
            jnp.float32
        ),
    )
    sum_mod_b, sum_qv_b, sum_out_b, sum_exp_b, sum_red_b = lax.psum(
        (rest_mod_b, rest_qv_b, rest_out_b, mlp_exp_b, mlp_red_b), "replica"
    )
    return (
        block_out,
        grad_latents,
        grad_condition,
        sum_mod_w,
        sum_mod_b,
        sum_proj_w,
        sum_qv_b,
        sum_out_w,
        sum_out_b,
        sum_exp_w,
        sum_exp_b,
        sum_red_w,
        sum_red_b,
    )


MESH = pl.DeviceIdType.MESH
SAME_CORE = ((1, 0), (0, 1), (1, 1))
PAD = 80
LANES_Q = 256


def fused_kernel(
    latents,
    cotangent,
    slots,
    live_col,
    live_row,
    cond_pack,
    mod_bias,
    extra,
    mod_w,
    proj_pack,
    exp_pack,
    red_pack,
    out_shard,
    o_block,
    o_latents,
    o_slabs,
    o_cond,
    o_gcond,
    o_exp,
    o_red,
    o_proj,
    o_out,
    cond_all,
    extra_all,
    live_all,
    mod_send,
    mod_all,
    proj_all,
    exp_all,
    red_all,
    out_w,
    proj_wide,
    spread,
    x_one,
    x_two,
    g_mlp,
    g_attn,
    qkv,
    probs,
    attended,
    act,
    g_hid,
    d_qkv,
    part_a,
    part_b,
    sib_a,
    sib_b,
    rows_a,
    rows_b,
    kept,
    norm_one,
    rstd_one,
    g_rows,
    branch_a,
    mixed,
    norm_two,
    rstd_two,
    g_mixed,
    slab,
    slabs,
    gcond,
    d_exp,
    d_red,
    d_proj,
    d_out,
    z_exp,
    z_red,
    z_proj,
    z_out,
    local_sem,
    small_s,
    small_r,
    w_s,
    w_r,
    ag_s,
    ag_r,
    sb_s,
    sb_r,
    rs_s,
    rs_r,
    dz_s,
    dz_r,
    dp_s,
    dp_r,
    ow_s,
    ow_r,
):
    f32 = jnp.float32
    bf16 = jnp.bfloat16
    r = lax.axis_index("replica")
    f = lax.axis_index("fsdp")
    x, y, c, z = r % 2, r // 2, f % 2, f // 2
    width = latents.shape[1]
    rows = slots.shape[0]
    part = out_shard.shape[0]
    third = width // 3
    me = 4 * c + r
    other = (c + 1) % 2

    def ident(r2, f2):
        return {"replica": r2, "fsdp": f2}

    def remote(src, dst, s_sem, r_sem, dev):
        return pltpu.make_async_remote_copy(
            src_ref=src,
            dst_ref=dst,
            send_sem=s_sem,
            recv_sem=r_sem,
            device_id=dev,
            device_id_type=MESH,
        )

    def plane(dx, dy):
        return ((y + dy) % 2) * 2 + (x + dx) % 2

    sibling = ident(r, 2 * z + other)
    line = []
    for dz in range(4):
        for dc in range(2):
            if dz or dc:
                line.append(((z + dz) % 4, (c + dc) % 2))
    board = []
    for dx in range(2):
        for dy in range(2):
            for dc in range(2):
                if dx or dy or dc:
                    board.append((plane(dx, dy), (c + dc) % 2))

    barrier = pltpu.get_barrier_semaphore()
    for z2, c2 in line:
        pl.semaphore_signal(barrier, inc=1, device_id=ident(r, 2 * z2 + c2), device_id_type=MESH)
    for r2, c2 in board:
        pl.semaphore_signal(barrier, inc=1, device_id=ident(r2, 2 * z + c2), device_id_type=MESH)
    pl.semaphore_wait(barrier, len(line) + len(board))

    def line_send(kind, sems_s, sems_r, src_of, dst_of):
        copies = []
        for k, (z2, c2) in enumerate(line):
            f2 = 2 * z2 + c2
            cp = remote(
                src_of(f2, c2),
                dst_of(f),
                sems_s.at[kind, k],
                sems_r.at[kind, f],
                ident(r, f2),
            )
            cp.start()
            copies.append(cp)
        return copies

    def line_wait(kind, sems_s, sems_r, src_of, dst_of):
        for k, (z2, c2) in enumerate(line):
            f2 = 2 * z2 + c2
            remote(
                src_of(f, c), dst_of(f2), sems_s.at[kind, k], sems_r.at[kind, f2], ident(r, f2)
            ).wait_recv()

    def drain(copies):
        for cp in copies:
            cp.wait_send()

    def cond_src(f2, c2):
        return cond_pack.at[f2]

    def cond_dst(f2):
        return cond_all.at[f2]

    def extra_src(f2, c2):
        return extra.at[c2]

    def extra_dst(f2):
        return extra_all.at[f2]

    def proj_src(f2, c2):
        return proj_pack.at[c2]

    def proj_dst(f2):
        return proj_all.at[pl.ds(pl.multiple_of(f2 * part, 16), part)]

    def exp_src(f2, c2):
        return exp_pack.at[c2]

    def exp_dst(f2):
        return exp_all.at[pl.ds(pl.multiple_of(f2 * part, 16), part)]

    def red_src(f2, c2):
        return red_pack.at[c2]

    def red_dst(f2):
        return red_all.at[pl.ds(pl.multiple_of(f2 * PAD, 16), PAD)]

    sent = line_send(0, small_s, small_r, cond_src, cond_dst)
    sent += line_send(0, w_s, w_r, proj_src, proj_dst)
    sent += line_send(1, small_s, small_r, extra_src, extra_dst)
    live_sent = []
    for k, (r2, c2) in enumerate(board):
        cp = remote(
            live_row,
            live_all.at[me],
            small_s.at[3, k],
            small_r.at[3, me],
            ident(r2, 2 * z + c2),
        )
        cp.start()
        live_sent.append(cp)
    local = [
        pltpu.make_async_copy(cond_pack.at[f], cond_all.at[f], local_sem.at[0]),
        pltpu.make_async_copy(extra.at[c], extra_all.at[f], local_sem.at[1]),
        pltpu.make_async_copy(proj_pack.at[c], proj_dst(f), local_sem.at[2]),
        pltpu.make_async_copy(exp_pack.at[c], exp_dst(f), local_sem.at[3]),
        pltpu.make_async_copy(red_pack.at[c], red_dst(f), local_sem.at[4]),
        pltpu.make_async_copy(live_row, live_all.at[me], local_sem.at[5]),
    ]
    for cp in local:
        cp.start()

    def one_hot():
        ids = lax.broadcasted_iota(jnp.int32, (rows, latents.shape[0]), 1)
        return jnp.where(ids == slots[...], 1.0, 0.0)

    def dot(a, b):
        return jnp.dot(a, b, preferred_element_type=f32)

    def dot_t(a, b):
        return lax.dot_general(a, b, (((1,), (1,)), ((), ())), preferred_element_type=f32)

    def t_dot(a, b):
        return lax.dot_general(a, b, (((0,), (0,)), ((), ())), preferred_element_type=f32)

    kept[...] = dot(one_hot().astype(bf16), latents[...])
    g_rows[...] = dot((one_hot() * live_col[...]).astype(bf16), cotangent[...])

    def normalise(values, norm_ref, rstd_ref):
        centred = values - jnp.mean(values, axis=-1, keepdims=True)
        rstd = lax.rsqrt(jnp.mean(centred * centred, axis=-1, keepdims=True) + 1e-06)
        norm_ref[...] = centred * rstd
        rstd_ref[...] = rstd

    normalise(kept[...], norm_one, rstd_one)
    out_w[part:, :] = jnp.zeros((out_w.shape[0] - part, width), bf16)
    split = lax.broadcasted_iota(jnp.int32, spread.shape, 0)
    column = lax.broadcasted_iota(jnp.int32, spread.shape, 1)
    skip = jnp.where(split >= part, LANES_Q - part, 0) + jnp.where(
        split >= 2 * part, LANES_Q - part, 0
    )
    spread[...] = jnp.where(column == split + skip, 1.0, 0.0).astype(bf16)

    for cp in local:
        cp.wait()
    line_wait(0, small_s, small_r, cond_src, cond_dst)
    cond_cols = jnp.sum(cond_all[...].astype(f32), axis=1).astype(bf16)
    mod_send[...] = jnp.zeros(mod_send.shape, f32)
    for p in range(6):
        piece = dot(cond_cols, mod_w[:, p * width : (p + 1) * width]) + mod_bias[p : p + 1, :]
        mod_send[:, p, :] = piece

    def mod_src(f2, c2):
        return mod_send.at[f2]

    def mod_dst(f2):
        return mod_all.at[f2]

    sent += line_send(2, small_s, small_r, mod_src, mod_dst)
    mod_all[f] = mod_send[f]
    cond_sent = []
    for k, (dx, dy) in enumerate(SAME_CORE):
        cp = remote(
            cond_all,
            o_cond.at[r],
            small_s.at[4, k],
            small_r.at[4, r],
            ident(plane(dx, dy), f),
        )
        cp.start()
        cond_sent.append(cp)
    own_cond = pltpu.make_async_copy(cond_all, o_cond.at[r], local_sem.at[0])
    own_cond.start()
    line_wait(2, small_s, small_r, mod_src, mod_dst)
    modulation = jnp.sum(mod_all[...], axis=0)
    shift_attn, scale_attn, gate_attn, shift_mlp, scale_mlp, gate_mlp = [
        modulation[p : p + 1, :] for p in range(6)
    ]

    def own(ref):
        return ref.at[pl.ds(pl.multiple_of(me * rows, rows), rows)]

    def slot(ref, u):
        return ref.at[pl.ds(pl.multiple_of(u * rows, rows), rows)]

    def gather_start(kind, buf):
        copies = [
            remote(own(buf), own(buf), ag_s.at[kind, 0], ag_r.at[kind, me], sibling),
        ]
        for k, (dx, dy) in enumerate(SAME_CORE):
            copies.append(
                remote(
                    own(buf),
                    own(buf),
                    ag_s.at[kind, 1 + k],
                    ag_r.at[kind, me],
                    ident(plane(dx, dy), f),
                )
            )
        for cp in copies:
            cp.start()
        return copies

    def gather_end(kind, buf):
        copies = []
        for k, (dx, dy) in enumerate(SAME_CORE):
            u = 4 * c + plane(dx, dy)
            cp = remote(slot(buf, u), slot(buf, u), ag_s.at[kind, 4 + k], ag_r.at[kind, u], sibling)
            cp.wait_recv()
            cp.start()
            copies.append(cp)
        for r2 in range(4):
            u = 4 * other + r2
            remote(
                slot(buf, u), slot(buf, u), ag_s.at[kind, 0], ag_r.at[kind, u], sibling
            ).wait_recv()
        return copies

    def reduce_chunk(kind, k, cc, values, buf, sib, landing):
        base = pl.multiple_of(cc * 4 * rows + (k % 2) * 2 * rows, 2 * rows)
        here = pl.ds(base, 2 * rows)
        there = pl.ds(pl.multiple_of((k % 2) * 2 * rows, 2 * rows), 2 * rows)
        slot_k = k % 2

        @pl.when(k < 2)
        def _():
            buf[here, :] = values.astype(bf16)
            remote(
                buf.at[here], sib.at[there], sb_s.at[kind, slot_k], sb_r.at[kind, slot_k], sibling
            ).start()

        @pl.when(k >= 2)
        def _():
            remote(
                buf.at[here], sib.at[there], sb_s.at[kind, slot_k], sb_r.at[kind, slot_k], sibling
            ).wait_recv()
            buf[here, :] = (values + sib[there, :].astype(f32)).astype(bf16)
            for x2 in range(2):
                r2 = 2 * slot_k + x2

                @pl.when(r2 != r)
                def _():
                    remote(
                        slot(buf, 4 * c + r2),
                        landing.at[r],
                        rs_s.at[kind, r2],
                        rs_r.at[kind, r],
                        ident(r2, f),
                    ).start()

    def reduce_end(kind, buf, landing):
        total = own(buf)[...].astype(f32)
        for dx, dy in SAME_CORE:
            r2 = plane(dx, dy)
            remote(
                own(buf), landing.at[r2], rs_s.at[kind, r2], rs_r.at[kind, r2], ident(r2, f)
            ).wait_recv()
            total += landing[r2].astype(f32)
        return total

    def reduce_drain(kind, buf, sib, landing):
        for k in range(2):
            there = pl.ds(k * 2 * rows, 2 * rows)
            remote(
                sib.at[there], sib.at[there], sb_s.at[kind, k], sb_r.at[kind, k], sibling
            ).wait_send()
        for dx, dy in SAME_CORE:
            r2 = plane(dx, dy)
            remote(
                own(buf), landing.at[r2], rs_s.at[kind, r2], rs_r.at[kind, r2], ident(r2, f)
            ).wait_send()

    own(x_one)[...] = (norm_one[...] * (1.0 + scale_attn) + shift_attn).astype(bf16)
    sent += gather_start(0, x_one)
    grad_mlp = (gate_mlp * g_rows[...]).astype(bf16)
    own(g_mlp)[...] = grad_mlp
    slab[...] = jnp.zeros(slab.shape, f32)
    slab[6:7, :] = jnp.sum(grad_mlp.astype(f32), axis=0, keepdims=True)

    @pl.when(z == r)
    def _():
        for dz in range(1, 4):
            remote(
                out_shard,
                out_w.at[pl.ds(0, part)],
                ow_s.at[dz - 1],
                ow_r.at[0],
                ident(r, 2 * ((z + dz) % 4) + c),
            ).start()
        out_w[:part, :] = out_shard[...]

    line_wait(0, w_s, w_r, proj_src, proj_dst)
    sent += line_send(1, w_s, w_r, exp_src, exp_dst)
    proj_wide[...] = dot(proj_all[...], spread[...]).astype(bf16)
    line_wait(1, small_s, small_r, extra_src, extra_dst)
    biases = jnp.sum(extra_all[...].astype(f32), axis=0)
    out_b, red_b, exp_b, qv_b = [biases[p : p + 1, :] for p in range(4)]
    for k, (r2, c2) in enumerate(board):
        remote(
            live_row,
            live_all.at[4 * c2 + r2],
            small_s.at[3, k],
            small_r.at[3, 4 * c2 + r2],
            ident(r2, 2 * z + c2),
        ).wait_recv()
    sent += gather_end(0, x_one)
    sent += gather_start(1, g_mlp)
    sent += line_send(2, w_s, w_r, red_src, red_dst)

    lane = lax.broadcasted_iota(jnp.int32, (1, LANES_Q), 1)
    heads = [
        jnp.where((lane >= h * HEAD_DIM) & (lane < (h + 1) * HEAD_DIM), 1.0, 0.0).astype(bf16)
        for h in range(2)
    ]
    scale = HEAD_DIM ** (-0.5)

    @pl.when(z != r)
    def _():
        remote(
            out_shard, out_w.at[pl.ds(0, part)], ow_s.at[0], ow_r.at[0], ident(r, 2 * z + c)
        ).wait_recv()

    def chunk_of(k):
        cc = (c + 1 + k // 2) % 2
        first = 4 * cc + 2 * (k % 2)
        return cc, first, pl.ds(pl.multiple_of(first * rows, 2 * rows), 2 * rows)

    def attend(k, carry):
        cc, first, here = chunk_of(k)
        wide = dot(x_one[here, :], proj_wide[...])
        qkv[here, :LANES_Q] = (wide[:, :LANES_Q] + qv_b[:, :LANES_Q]).astype(bf16)
        qkv[here, LANES_Q : 2 * LANES_Q] = wide[:, LANES_Q : 2 * LANES_Q].astype(bf16)
        qkv[here, 2 * LANES_Q :] = (
            wide[:, 2 * LANES_Q :] + qv_b[:, LANES_Q : 2 * LANES_Q]
        ).astype(bf16)
        for i in range(2):
            u = first + i
            at = pl.ds(pl.multiple_of(u * rows, rows), rows)
            q = qkv[at, :LANES_Q]
            key = qkv[at, LANES_Q : 2 * LANES_Q]
            val = qkv[at, 2 * LANES_Q :]
            alive = live_all[u][0:1, :] > 0.5
            total = jnp.zeros((rows, LANES_Q), f32)
            for h in range(2):
                s = dot_t(q * heads[h], key) * scale
                s = jnp.where(alive, s, -1e30)
                e = jnp.exp(s - jnp.max(s, axis=-1, keepdims=True))
                p = e / jnp.sum(e, axis=-1, keepdims=True)
                probs[2 * u + h] = p
                total += dot(p.astype(bf16), val) * heads[h].astype(f32)
            attended[at, :] = total.astype(bf16)
        values = dot(attended[here, :], out_w[...])
        reduce_chunk(0, k, cc, values, part_a, sib_a, rows_a)
        return carry

    lax.fori_loop(0, 4, attend, 0)
    branch = reduce_end(0, part_a, rows_a) + out_b
    branch_a[...] = branch
    mixed[...] = kept[...] + gate_attn * branch
    normalise(mixed[...], norm_two, rstd_two)
    own(x_two)[...] = (norm_two[...] * (1.0 + scale_mlp) + shift_mlp).astype(bf16)
    sent += gather_start(2, x_two)
    sent += gather_end(1, g_mlp)
    line_wait(1, w_s, w_r, exp_src, exp_dst)
    line_wait(2, w_s, w_r, red_src, red_dst)
    sent += gather_end(2, x_two)
    reduce_drain(0, part_a, sib_a, rows_a)

    k_gelu = 0.7978845608028654
    hid_b = exp_b[:, : exp_all.shape[1]]

    def feed(k, carry):
        cc, first, here = chunk_of(k)
        hid = dot(x_two[here, :], exp_all[...]) + hid_b
        square = hid * hid
        th = jnp.tanh(k_gelu * hid * (1.0 + 0.044715 * square))
        act[here, :] = (0.5 * hid * (1.0 + th)).astype(bf16)
        slope = 0.5 * (1.0 + th) + 0.5 * hid * (1.0 - th * th) * k_gelu * (
            1.0 + 3.0 * 0.044715 * square
        )
        grad = (dot_t(g_mlp[here, :], red_all[...]) * slope).astype(bf16)
        g_hid[here, :] = grad
        values = dot_t(grad, exp_all[...])
        reduce_chunk(1, k, cc, values, part_b, sib_b, rows_b)
        return carry

    lax.fori_loop(0, 4, feed, 0)

    hid_sum = jnp.sum(g_hid[...].astype(f32), axis=0, keepdims=True)
    slab[8:9, : exp_all.shape[1]] = hid_sum

    def zsend(kind, src, landing, height):
        copies = []
        for dz in range(1, 4):
            z2 = (z + dz) % 4
            cp = remote(
                src.at[pl.ds(pl.multiple_of(z2 * height, 16), height)],
                landing.at[dz - 1],
                dz_s.at[kind, dz - 1],
                dz_r.at[kind, dz - 1],
                ident(r, 2 * z2 + c),
            )
            cp.start()
            copies.append(cp)
        return copies

    def wide_grad(k, carry):
        at = pl.ds(pl.multiple_of(k * third, 128), third)
        d_exp[at, :] = t_dot(x_two[:, at], g_hid[...]).astype(bf16)
        return carry

    lax.fori_loop(0, 3, wide_grad, 0)
    sent += zsend(0, d_exp, z_exp, 2 * part)

    grad_two = reduce_end(1, part_b, rows_b)

    def back_norm(grad, scale_part, norm, rstd):
        g_shift = jnp.sum(grad, axis=0, keepdims=True)
        g_scale = jnp.sum(grad * norm, axis=0, keepdims=True)
        e = grad * (1.0 + scale_part)
        inner = jnp.mean(e * norm, axis=-1, keepdims=True)
        return g_shift, g_scale, (e - jnp.mean(e, axis=-1, keepdims=True) - norm * inner) * rstd

    g_shift, g_scale, through = back_norm(grad_two, scale_mlp, norm_two[...], rstd_two[...])
    slab[3:4, :] = g_shift
    slab[4:5, :] = g_scale
    g_mixed[...] = g_rows[...] + through
    slab[2:3, :] = jnp.sum(g_mixed[...] * branch_a[...], axis=0, keepdims=True)
    grad_at = (gate_attn * g_mixed[...]).astype(bf16)
    own(g_attn)[...] = grad_at
    slab[7:8, :] = jnp.sum(grad_at.astype(f32), axis=0, keepdims=True)
    sent += gather_start(3, g_attn)

    def red_grad(k, carry):
        at = pl.ds(pl.multiple_of(k * third, 128), third)
        d_red[:, at] = t_dot(act[...], g_mlp[:, at]).astype(bf16)
        return carry

    lax.fori_loop(0, 3, red_grad, 0)
    sent += zsend(1, d_red, z_red, 2 * PAD)
    sent += gather_end(3, g_attn)
    reduce_drain(1, part_b, sib_b, rows_b)

    def attend_back(k, carry):
        cc, first, here = chunk_of(k)
        g_att = dot_t(g_attn[here, :], out_w[...]).astype(bf16)
        for i in range(2):
            u = first + i
            at = pl.ds(pl.multiple_of(u * rows, rows), rows)
            q = qkv[at, :LANES_Q]
            key = qkv[at, LANES_Q : 2 * LANES_Q]
            val = qkv[at, 2 * LANES_Q :]
            up = g_att[i * rows : (i + 1) * rows, :]
            g_q = jnp.zeros((rows, LANES_Q), f32)
            g_k = jnp.zeros((rows, LANES_Q), f32)
            g_v = jnp.zeros((rows, LANES_Q), f32)
            for h in range(2):
                p = probs[2 * u + h]
                up_h = up * heads[h]
                g_v += t_dot(p.astype(bf16), up_h)
                g_p = dot_t(up_h, val)
                inner = jnp.sum(g_p * p, axis=-1, keepdims=True)
                g_s = (p * (g_p - inner)).astype(bf16)
                g_q += dot(g_s, key) * heads[h].astype(f32)
                g_k += t_dot(g_s, q * heads[h])
            wide = jnp.concatenate([g_q * scale, g_k * scale, g_v], axis=1).astype(bf16)
            d_qkv[at, :] = dot_t(wide, spread[...]).astype(bf16)
        values = dot_t(d_qkv[here, :], proj_all[...])
        reduce_chunk(2, k, cc, values, part_a, sib_a, rows_a)
        return carry

    lax.fori_loop(0, 4, attend_back, 0)

    def proj_grad(k, carry):
        at = pl.ds(pl.multiple_of(k * third, 128), third)
        d_proj[at, :] = t_dot(x_one[:, at], d_qkv[...]).astype(bf16)
        return carry

    lax.fori_loop(0, 3, proj_grad, 0)
    sent += zsend(2, d_proj, z_proj, 2 * part)
    d_out[...] = t_dot(attended[...], g_attn[...]).astype(bf16)

    @pl.when(z != r)
    def _():
        slot_z = (r - z + 4) % 4 - 1
        remote(
            d_out.at[pl.ds(0, part)],
            z_out.at[slot_z],
            ow_s.at[3],
            ow_r.at[1 + slot_z],
            ident(r, 2 * r + c),
        ).start()

    slab[9:10, : d_qkv.shape[1]] = jnp.sum(d_qkv[...].astype(f32), axis=0, keepdims=True)

    def feed_out(k, carry):
        cc, first, here = chunk_of(k)
        values = dot(act[here, :], red_all[...])
        reduce_chunk(3, k, cc, values, part_b, sib_b, rows_b)
        return carry

    lax.fori_loop(0, 4, feed_out, 0)

    def place(values, base):
        live_hot = (one_hot() * live_col[...]).astype(bf16)
        placed = t_dot(live_hot, values.astype(bf16))
        hit = t_dot(live_hot, jnp.ones((rows, 128), bf16))[:, 0:1]
        return jnp.where(hit > 0.5, placed.astype(bf16), base)

    grad_one = reduce_end(2, part_a, rows_a)
    g_shift, g_scale, through = back_norm(grad_one, scale_attn, norm_one[...], rstd_one[...])
    slab[0:1, :] = g_shift
    slab[1:2, :] = g_scale
    o_latents[...] = place(g_mixed[...] + through, cotangent[...])
    branch = reduce_end(3, part_b, rows_b) + red_b
    slab[5:6, :] = jnp.sum(g_rows[...] * branch, axis=0, keepdims=True)
    slabs[f] = slab[...].astype(bf16)

    def slab_src(f2, c2):
        return slabs.at[f]

    def slab_dst(f2):
        return slabs.at[f2]

    sent += line_send(5, small_s, small_r, slab_src, slab_dst)
    o_block[...] = place(mixed[...] + gate_mlp * branch, latents[...])

    outs = []

    def spread_out(kind, src, landing, height, dest):
        total = src[pl.ds(pl.multiple_of(z * height, 16), height), :].astype(f32)
        for dz in range(1, 4):
            remote(
                src.at[pl.ds(0, height)],
                landing.at[dz - 1],
                dz_s.at[kind, dz - 1],
                dz_r.at[kind, dz - 1],
                ident(r, 2 * ((z + dz) % 4) + c),
            ).wait_recv()
            total += landing[dz - 1].astype(f32)
        half = height // 2
        keep = src.at[pl.ds(pl.multiple_of(z * height, 16), height)]
        keep[...] = total.astype(bf16)
        for k, (r2, c2) in enumerate(board):
            cp = remote(
                src.at[pl.ds(pl.multiple_of(z * height + c2 * half, 16), half)],
                dest.at[me],
                dp_s.at[kind, k],
                dp_r.at[kind, me],
                ident(r2, 2 * z + c2),
            )
            cp.start()
            sent.append(cp)
        cp = pltpu.make_async_copy(
            src.at[pl.ds(pl.multiple_of(z * height + c * half, 16), half)],
            dest.at[me],
            local_sem.at[1 + kind],
        )
        cp.start()
        outs.append(cp)

    spread_out(0, d_exp, z_exp, 2 * part, o_exp)
    spread_out(1, d_red, z_red, 2 * PAD, o_red)

    @pl.when(z == r)
    def _():
        total = d_out[:part, :].astype(f32)
        for k in range(3):
            remote(
                d_out.at[pl.ds(0, part)], z_out.at[k], ow_s.at[3], ow_r.at[1 + k], ident(r, f)
            ).wait_recv()
            total += z_out[k].astype(f32)
        d_out[:part, :] = total.astype(bf16)
        for k, (dx, dy) in enumerate(SAME_CORE):
            remote(
                d_out.at[pl.ds(0, part)], o_out, ow_s.at[4 + k], ow_r.at[4], ident(plane(dx, dy), f)
            ).start()
        cp = pltpu.make_async_copy(d_out.at[pl.ds(0, part)], o_out, local_sem.at[5])
        cp.start()
        cp.wait()

    line_wait(5, small_s, small_r, slab_src, slab_dst)
    for k, (dx, dy) in enumerate(SAME_CORE):
        cp = remote(
            slabs, o_slabs.at[r], small_s.at[6, k], small_r.at[6, r], ident(plane(dx, dy), f)
        )
        cp.start()
        sent.append(cp)
    own_slabs = pltpu.make_async_copy(slabs, o_slabs.at[r], local_sem.at[4])
    own_slabs.start()
    back_cond = jnp.zeros((8, part), f32)
    for p in range(6):
        back_cond += dot_t(slabs[:, p, :], mod_w[:, p * width : (p + 1) * width])
    for i in range(8):
        gcond[i] = jnp.broadcast_to(back_cond[i : i + 1, :], (8, part))

    def gc_src(f2, c2):
        return gcond.at[f2]

    def gc_dst(f2):
        return o_gcond.at[f2]

    sent += line_send(7, small_s, small_r, gc_src, gc_dst)
    o_gcond[f] = gcond[f]

    spread_out(2, d_proj, z_proj, 2 * part, o_proj)

    line_wait(7, small_s, small_r, gc_src, gc_dst)
    for dx, dy in SAME_CORE:
        r2 = plane(dx, dy)
        remote(
            cond_all, o_cond.at[r2], small_s.at[4, 0], small_r.at[4, r2], ident(r2, f)
        ).wait_recv()
        remote(
            slabs, o_slabs.at[r2], small_s.at[6, 0], small_r.at[6, r2], ident(r2, f)
        ).wait_recv()
    for kind, dest in ((0, o_exp), (1, o_red), (2, o_proj)):
        for r2, c2 in board:
            u = 4 * c2 + r2
            remote(
                dest.at[u], dest.at[u], dp_s.at[kind, 0], dp_r.at[kind, u], ident(r2, 2 * z + c2)
            ).wait_recv()

    @pl.when(z == r)
    def _():
        for dz in range(3):
            remote(
                out_shard, out_w.at[pl.ds(0, part)], ow_s.at[dz], ow_r.at[0], ident(r, f)
            ).wait_send()
            remote(
                out_shard, o_out, ow_s.at[4 + dz], ow_r.at[4], ident(r, f)
            ).wait_send()

    @pl.when(z != r)
    def _():
        remote(out_shard, o_out, ow_s.at[3], ow_r.at[4], ident(r, f)).wait_recv()
        remote(
            d_out.at[pl.ds(0, part)], z_out.at[0], ow_s.at[3], ow_r.at[1], ident(r, f)
        ).wait_send()

    reduce_drain(2, part_a, sib_a, rows_a)
    reduce_drain(3, part_b, sib_b, rows_b)
    drain(sent)
    drain(live_sent)
    drain(cond_sent)
    own_cond.wait()
    own_slabs.wait()
    for cp in outs:
        cp.wait()


def fused_local(
    latents,
    condition,
    bucket,
    keep_slots,
    modulation_weight,
    modulation_bias,
    projection_weight,
    query_value_bias,
    output_weight,
    output_bias,
    expand_weight,
    expand_bias,
    reduce_weight,
    reduce_bias,
    cotangent,
):
    f32 = jnp.float32
    bf16 = jnp.bfloat16
    r = lax.axis_index("replica")
    f = lax.axis_index("fsdp")
    slot_count, width = latents.shape[1:]
    rows = keep_slots.shape[1]
    part = output_weight.shape[0]
    hid = expand_weight.shape[1]
    share = hid // 64
    wide = 8 * PAD

    def placed(shard, count):
        return lax.dynamic_update_slice_in_dim(
            jnp.zeros((count,), f32), shard.astype(f32), f * shard.shape[0], 0
        )

    def mine(value, axis):
        return lax.dynamic_slice_in_dim(value, 2 * r, 2, axis)

    cond_float = condition.astype(f32)
    cond_act = jax.nn.silu(cond_float).astype(bf16)
    cond_pack = jnp.pad(cond_act.reshape(8, 1, part), ((0, 0), (0, 15), (0, 0)))
    mod_bias = jnp.pad(placed(modulation_bias, 6 * width).reshape(6, width), ((0, 2), (0, 0)))
    live_count = jnp.where(bucket[0] == 0, slot_count, slot_count - 16) // 2
    live = (jnp.arange(rows, dtype=jnp.int32) < live_count).astype(f32)
    qv = mine(placed(query_value_bias, 2 * width).reshape(2, 8, part), 1)
    qv = jnp.pad(qv.transpose(1, 0, 2), ((0, 0), (0, 0), (0, LANES_Q - part))).reshape(2, -1)
    expand_b = mine(placed(expand_bias, hid).reshape(8, 8, share), 1).transpose(1, 0, 2)
    expand_b = jnp.pad(expand_b, ((0, 0), (0, 0), (0, PAD - share))).reshape(2, wide)
    extra = jnp.stack(
        [
            jnp.broadcast_to(placed(output_bias, width), (2, width)),
            jnp.broadcast_to(placed(reduce_bias, width), (2, width)),
            jnp.pad(expand_b, ((0, 0), (0, width - wide))),
            jnp.pad(qv, ((0, 0), (0, width - 2 * LANES_Q))),
        ],
        axis=1,
    ).astype(bf16)
    extra = jnp.pad(extra, ((0, 0), (0, 12), (0, 0)))
    proj_pack = mine(projection_weight.reshape(part, 3, 8, part), 2)
    proj_pack = proj_pack.transpose(2, 0, 1, 3).reshape(2, part, 3 * part)
    exp_pack = mine(expand_weight.reshape(part, 8, 8, share), 2).transpose(2, 0, 1, 3)
    exp_pack = jnp.pad(exp_pack, ((0, 0),) * 3 + ((0, PAD - share),)).reshape(2, part, wide)
    red_pack = mine(reduce_weight.reshape(8, share, width), 0)
    red_pack = jnp.pad(red_pack, ((0, 0), (0, PAD - share), (0, 0)))

    total = 8 * rows
    vmem = pltpu.VMEM
    dma = pltpu.SemaphoreType.DMA
    scratch = [
        vmem((8, 16, part), bf16),
        vmem((8, 16, width), bf16),
        vmem((8, 8, rows), f32),
        vmem((8, 8, width), f32),
        vmem((8, 8, width), f32),
        vmem((width, 3 * part), bf16),
        vmem((width, wide), bf16),
        vmem((wide, width), bf16),
        vmem((LANES_Q, width), bf16),
        vmem((width, 3 * LANES_Q), bf16),
        vmem((3 * part, 3 * LANES_Q), bf16),
        vmem((total, width), bf16),
        vmem((total, width), bf16),
        vmem((total, width), bf16),
        vmem((total, width), bf16),
        vmem((total, 3 * LANES_Q), bf16),
        vmem((16, rows, rows), f32),
        vmem((total, LANES_Q), bf16),
        vmem((total, wide), bf16),
        vmem((total, wide), bf16),
        vmem((total, 3 * part), bf16),
        vmem((total, width), bf16),
        vmem((total, width), bf16),
    ]
    scratch += [vmem((4 * rows, width), bf16)] * 2
    scratch += [vmem((4, rows, width), bf16)] * 2
    scratch += [
        vmem((rows, width), f32),
        vmem((rows, width), f32),
        vmem((rows, 1), f32),
        vmem((rows, width), f32),
        vmem((rows, width), f32),
        vmem((rows, width), f32),
        vmem((rows, width), f32),
        vmem((rows, 1), f32),
        vmem((rows, width), f32),
        vmem((16, width), f32),
        vmem((8, 16, width), bf16),
        vmem((8, 8, part), f32),
        vmem((width, wide), bf16),
        vmem((wide, width), bf16),
        vmem((width, 3 * part), bf16),
        vmem((LANES_Q, width), bf16),
        vmem((3, 2 * part, wide), bf16),
        vmem((3, 2 * PAD, width), bf16),
        vmem((3, 2 * part, 3 * part), bf16),
        vmem((3, part, width), bf16),
        dma((8,)),
        dma((8, 7)),
        dma((8, 8)),
        dma((3, 7)),
        dma((3, 8)),
        dma((4, 7)),
        dma((4, 8)),
        dma((4, 2)),
        dma((4, 2)),
        dma((4, 4)),
        dma((4, 4)),
        dma((3, 3)),
        dma((3, 3)),
        dma((3, 7)),
        dma((3, 8)),
        dma((7,)),
        dma((5,)),
    ]
    in_vmem = pl.BlockSpec(memory_space=pltpu.VMEM)
    anywhere = pl.BlockSpec(memory_space=pl.ANY)
    outputs = pl.pallas_call(
        fused_kernel,
        out_shape=(
            jax.ShapeDtypeStruct((slot_count, width), bf16),
            jax.ShapeDtypeStruct((slot_count, width), bf16),
            jax.ShapeDtypeStruct((4, 8, 16, width), bf16),
            jax.ShapeDtypeStruct((4, 8, 16, part), bf16),
            jax.ShapeDtypeStruct((8, 8, part), f32),
            jax.ShapeDtypeStruct((8, part, wide), bf16),
            jax.ShapeDtypeStruct((8, PAD, width), bf16),
            jax.ShapeDtypeStruct((8, part, 3 * part), bf16),
            jax.ShapeDtypeStruct((part, width), bf16),
        ),
        in_specs=[in_vmem] * 13,
        out_specs=(
            in_vmem,
            in_vmem,
            anywhere,
            anywhere,
            in_vmem,
            anywhere,
            anywhere,
            anywhere,
            anywhere,
        ),
        scratch_shapes=scratch,
        compiler_params=pltpu.CompilerParams(
            collective_id=0, has_side_effects=True, vmem_limit_bytes=60 << 20
        ),
    )(
        latents[0],
        cotangent[0],
        keep_slots.reshape(rows, 1),
        live.reshape(rows, 1),
        jnp.broadcast_to(live[None], (8, rows)),
        cond_pack,
        mod_bias,
        extra,
        modulation_weight,
        proj_pack,
        exp_pack,
        red_pack,
        output_weight,
    )
    block, grad_latents, slabs, conds, g_cond, g_exp, g_red, g_proj, g_out = outputs

    def shard(value, axis, size):
        return lax.dynamic_slice_in_dim(value, f * size, size, axis)

    slabs = slabs.reshape(32, 16, width)
    grad_mod = slabs[:, :6].reshape(32, 6 * width)
    cond_cols = conds[:, :, 0].reshape(32, part)
    sum_mod_w = jnp.einsum("bd,be->de", cond_cols, grad_mod, preferred_element_type=f32)
    sums = jnp.sum(slabs[:, :8].astype(f32), axis=0)
    sum_mod_b = shard(sums[:6].reshape(-1), 0, modulation_bias.shape[0])
    sum_red_b = shard(sums[6], 0, part)
    sum_out_b = shard(sums[7], 0, part)
    tails = jnp.sum(slabs[:, 8:10].astype(f32).reshape(4, 4, 2, 2, width), axis=1)
    exp_sums = tails[:, :, 0, :wide].reshape(8, 8, PAD)
    sum_exp_b = lax.dynamic_index_in_dim(exp_sums, f, 1, keepdims=False)[:, :share].reshape(-1)
    qv_sums = tails[:, :, 1, : 3 * part].reshape(8, 3, part)
    qv_sums = jnp.concatenate([qv_sums[:, 0].reshape(-1), qv_sums[:, 2].reshape(-1)])
    sum_qv_b = shard(qv_sums, 0, query_value_bias.shape[0])
    grad_condition = jax.vjp(jax.nn.silu, cond_float)[1](g_cond[:, 0].reshape(1, width))[0]
    g_exp = g_exp.reshape(2, 4, part, 8, PAD)[..., :share].transpose(2, 3, 1, 0, 4)
    g_red = g_red.reshape(2, 4, PAD, width)[:, :, :share].transpose(1, 0, 2, 3)
    g_proj = g_proj.reshape(2, 4, part, 3, part).transpose(2, 3, 1, 0, 4)
    return (
        block[None],
        grad_latents[None],
        grad_condition,
        sum_mod_w,
        sum_mod_b,
        g_proj.reshape(part, 3 * width).astype(f32),
        sum_qv_b,
        g_out.astype(f32),
        sum_out_b,
        g_exp.reshape(part, hid).astype(f32),
        sum_exp_b,
        g_red.reshape(8 * share, width).astype(f32),
        sum_red_b,
    )


def solution(mesh):
    placed = (
        P(("replica", "fsdp"), None, None),
        P(("replica", "fsdp"), None),
        P(("replica", "fsdp")),
        P(("replica", "fsdp"), None),
        P("fsdp", None),
        P("fsdp"),
        P("fsdp", None),
        P("fsdp"),
        P("fsdp", None),
        P("fsdp"),
        P("fsdp", None),
        P("fsdp"),
        P("fsdp", None),
        P("fsdp"),
        P(("replica", "fsdp"), None, None),
    )
    body = fused_local if tuple(mesh.shape.values()) == (4, 8) else local
    return jax.shard_map(
        body,
        mesh=mesh,
        in_specs=placed,
        out_specs=(
            P(("replica", "fsdp"), None, None),
            P(("replica", "fsdp"), None, None),
            P(("replica", "fsdp"), None),
            P("fsdp", None),
            P("fsdp"),
            P("fsdp", None),
            P("fsdp"),
            P("fsdp", None),
            P("fsdp"),
            P("fsdp", None),
            P("fsdp"),
            P("fsdp", None),
            P("fsdp"),
        ),
        check_vma=False,
    )
```

```python
import jax
import jax.numpy as jnp
from jax import lax
from jax.experimental import pallas as pl
from jax.experimental.pallas import tpu as pltpu
from jax.sharding import PartitionSpec as P

HEADS = 16
HEAD_DIM = 72


def layer_norm(rows_in):
    row_mean = jnp.mean(rows_in, axis=-1, keepdims=True)
    centred = rows_in - row_mean
    row_var = jnp.mean(centred * centred, axis=-1, keepdims=True)
    return centred * lax.rsqrt(row_var + 1e-06)


def modulate(rows_in, shift_part, scale_part):
    return layer_norm(rows_in) * (1.0 + scale_part) + shift_part


def gelu_tanh(values_in):
    return jax.nn.gelu(values_in, approximate=True)


def place_rows(target_rows, target_index, new_rows):
    return target_rows.at[target_index].set(new_rows, mode="drop")


def column_sums(rows_in):
    return jnp.sum(rows_in.astype(jnp.float32), axis=0)


def local(
    latents,
    condition,
    bucket,
    keep_slots,
    modulation_weight,
    modulation_bias,
    projection_weight,
    query_value_bias,
    output_weight,
    output_bias,
    expand_weight,
    expand_bias,
    reduce_weight,
    reduce_bias,
    cotangent,
):
    f32 = jnp.float32
    bf16 = jnp.bfloat16
    images, slot_count, model_width = latents.shape
    kept_rows = keep_slots.shape[1]
    row_count = images * kept_rows
    score_scale = HEAD_DIM ** (-0.5)
    shape_heads = (images, kept_rows, HEADS, HEAD_DIM)
    (
        full_mod_w,
        full_mod_b,
        full_proj_w,
        full_qv_b,
        full_out_w,
        full_out_b,
        full_exp_w,
        full_exp_b,
        full_red_w,
        full_red_b,
    ) = (
        lax.all_gather(modulation_weight, "fsdp", axis=0, tiled=True),
        lax.all_gather(modulation_bias, "fsdp", axis=0, tiled=True),
        lax.all_gather(projection_weight, "fsdp", axis=0, tiled=True),
        lax.all_gather(query_value_bias, "fsdp", axis=0, tiled=True),
        lax.all_gather(output_weight, "fsdp", axis=0, tiled=True),
        lax.all_gather(output_bias, "fsdp", axis=0, tiled=True),
        lax.all_gather(expand_weight, "fsdp", axis=0, tiled=True),
        lax.all_gather(expand_bias, "fsdp", axis=0, tiled=True),
        lax.all_gather(reduce_weight, "fsdp", axis=0, tiled=True),
        lax.all_gather(reduce_bias, "fsdp", axis=0, tiled=True),
    )
    live_count = jnp.where(bucket == 0, slot_count, slot_count - 16) // 2
    live_rows = jnp.arange(kept_rows, dtype=jnp.int32)[None, :] < live_count[:, None]
    live_float = live_rows.astype(f32)[:, :, None]
    gather_index = keep_slots[:, :, None]
    kept = jnp.take_along_axis(latents, gather_index, axis=1).astype(f32)
    cond_float = condition.astype(f32)
    cond_act = jax.nn.silu(cond_float).astype(bf16)
    modulation = jnp.dot(cond_act, full_mod_w, preferred_element_type=f32) + full_mod_b.astype(f32)
    pieces = [modulation[:, None, i * model_width : (i + 1) * model_width] for i in range(6)]
    shift_attn, scale_attn, gate_attn, shift_mlp, scale_mlp, gate_mlp = pieces
    normed_one = modulate(kept, shift_attn, scale_attn).astype(bf16).reshape(row_count, model_width)
    projected = jnp.dot(normed_one, full_proj_w, preferred_element_type=f32)
    bias_qv = full_qv_b.astype(f32)
    query_rows = (
        (projected[:, :model_width] + bias_qv[:model_width]).astype(bf16).reshape(shape_heads)
    )
    key_rows = projected[:, model_width : 2 * model_width].astype(bf16).reshape(shape_heads)
    value_rows = (
        (projected[:, 2 * model_width :] + bias_qv[model_width:]).astype(bf16).reshape(shape_heads)
    )

    def masked_scores(queries, keys_in):
        raw = (
            jnp.einsum("bqhd,bkhd->bhqk", queries, keys_in, preferred_element_type=f32)
            * score_scale
        )
        return jnp.where(live_rows[:, None, None, :], raw, -1e30)

    scores = masked_scores(query_rows, key_rows)
    row_max = jnp.max(scores, axis=-1, keepdims=True)
    row_total = jnp.sum(jnp.exp(scores - row_max), axis=-1, keepdims=True)
    log_total = row_max + jnp.log(row_total)
    probs = jnp.exp(scores - log_total)
    attended = (
        jnp.einsum("bhqk,bkhd->bqhd", probs.astype(bf16), value_rows, preferred_element_type=f32)
        .astype(bf16)
        .reshape(row_count, model_width)
    )
    branch_attn = (
        jnp.dot(attended, full_out_w, preferred_element_type=f32) + full_out_b.astype(f32)
    ).reshape(images, kept_rows, model_width)
    mixed = kept + gate_attn * branch_attn
    normed_two = modulate(mixed, shift_mlp, scale_mlp).astype(bf16).reshape(row_count, model_width)
    hidden = jnp.dot(normed_two, full_exp_w, preferred_element_type=f32) + full_exp_b.astype(f32)
    activation = gelu_tanh(hidden).astype(bf16)
    branch_mlp = (
        jnp.dot(activation, full_red_w, preferred_element_type=f32) + full_red_b.astype(f32)
    ).reshape(images, kept_rows, model_width)
    result = mixed + gate_mlp * branch_mlp
    target = jnp.where(live_rows, keep_slots, slot_count)
    block_out = jax.vmap(place_rows)(latents, target, result.astype(bf16))
    back_mod_w, back_proj_w, back_out_w, back_exp_w, back_red_w = (
        lax.all_gather(modulation_weight, "fsdp", axis=0, tiled=True),
        lax.all_gather(projection_weight, "fsdp", axis=0, tiled=True),
        lax.all_gather(output_weight, "fsdp", axis=0, tiled=True),
        lax.all_gather(expand_weight, "fsdp", axis=0, tiled=True),
        lax.all_gather(reduce_weight, "fsdp", axis=0, tiled=True),
    )
    grad_rows = jnp.take_along_axis(cotangent, gather_index, axis=1).astype(f32) * live_float
    grad_gate_mlp = jnp.sum(grad_rows * branch_mlp, axis=1)
    grad_mlp = (gate_mlp * grad_rows).astype(bf16).reshape(row_count, model_width)
    local_red_w = jnp.einsum("rm,rd->md", activation, grad_mlp, preferred_element_type=f32)
    local_red_b = column_sums(grad_mlp)
    grad_act = jnp.einsum("rd,md->rm", grad_mlp, back_red_w, preferred_element_type=f32)
    gelu_pull = jax.vjp(gelu_tanh, hidden)[1]
    grad_hidden = gelu_pull(grad_act)[0].astype(bf16)
    local_exp_w = jnp.einsum("rd,rm->dm", normed_two, grad_hidden, preferred_element_type=f32)
    local_exp_b = column_sums(grad_hidden)
    mlp_red_w, mlp_red_b, mlp_exp_w, mlp_exp_b = (
        lax.psum_scatter(
            local_red_w.astype(jnp.bfloat16), "fsdp", scatter_dimension=0, tiled=True
        ).astype(jnp.float32),
        lax.psum_scatter(
            local_red_b.astype(jnp.bfloat16), "fsdp", scatter_dimension=0, tiled=True
        ).astype(jnp.float32),
        lax.psum_scatter(
            local_exp_w.astype(jnp.bfloat16), "fsdp", scatter_dimension=0, tiled=True
        ).astype(jnp.float32),
        lax.psum_scatter(
            local_exp_b.astype(jnp.bfloat16), "fsdp", scatter_dimension=0, tiled=True
        ).astype(jnp.float32),
    )
    grad_normed_two = jnp.einsum(
        "rm,dm->rd", grad_hidden, back_exp_w, preferred_element_type=f32
    ).reshape(images, kept_rows, model_width)
    pull_two = jax.vjp(modulate, mixed, shift_mlp, scale_mlp)[1]
    grad_mixed_ln, grad_shift_mlp, grad_scale_mlp = pull_two(grad_normed_two)
    grad_mixed = grad_rows + grad_mixed_ln
    grad_gate_attn = jnp.sum(grad_mixed * branch_attn, axis=1)
    grad_attn = (gate_attn * grad_mixed).astype(bf16).reshape(row_count, model_width)
    local_out_w = jnp.einsum("rd,re->de", attended, grad_attn, preferred_element_type=f32)
    local_out_b = column_sums(grad_attn)
    grad_attended = (
        jnp.einsum("re,de->rd", grad_attn, back_out_w, preferred_element_type=f32)
        .astype(bf16)
        .reshape(shape_heads)
    )
    scores_again = masked_scores(query_rows, key_rows)
    probs_again = jnp.exp(scores_again - log_total)
    grad_values = jnp.einsum(
        "bhqk,bqhd->bkhd", probs_again.astype(bf16), grad_attended, preferred_element_type=f32
    ).astype(bf16)
    grad_probs = jnp.einsum(
        "bqhd,bkhd->bhqk", grad_attended, value_rows, preferred_element_type=f32
    )
    row_inner = jnp.sum(grad_probs * probs_again, axis=-1, keepdims=True)
    grad_scores = (probs_again * (grad_probs - row_inner)).astype(bf16)
    grad_query = (
        jnp.einsum("bhqk,bkhd->bqhd", grad_scores, key_rows, preferred_element_type=f32)
        * score_scale
    ).astype(bf16)
    grad_keys = (
        jnp.einsum("bhqk,bqhd->bkhd", grad_scores, query_rows, preferred_element_type=f32)
        * score_scale
    ).astype(bf16)
    grad_projected = jnp.concatenate(
        [
            grad_query.reshape(row_count, model_width),
            grad_keys.reshape(row_count, model_width),
            grad_values.reshape(row_count, model_width),
        ],
        axis=1,
    )
    local_proj_w = jnp.einsum("rd,re->de", normed_one, grad_projected, preferred_element_type=f32)
    local_qv_b = jnp.concatenate(
        [
            column_sums(grad_projected[:, :model_width]),
            column_sums(grad_projected[:, 2 * model_width :]),
        ]
    )
    grad_normed_one = jnp.einsum(
        "re,de->rd", grad_projected, back_proj_w, preferred_element_type=f32
    ).reshape(images, kept_rows, model_width)
    pull_one = jax.vjp(modulate, kept, shift_attn, scale_attn)[1]
    grad_kept_ln, grad_shift_attn, grad_scale_attn = pull_one(grad_normed_one)
    grad_kept = grad_mixed + grad_kept_ln
    grad_latents = jax.vmap(place_rows)(cotangent, target, grad_kept.astype(bf16))
    grad_modulation = jnp.concatenate(
        [
            grad_shift_attn[:, 0],
            grad_scale_attn[:, 0],
            grad_gate_attn,
            grad_shift_mlp[:, 0],
            grad_scale_mlp[:, 0],
            grad_gate_mlp,
        ],
        axis=1,
    ).astype(bf16)
    grad_cond_act = jnp.einsum("be,de->bd", grad_modulation, back_mod_w, preferred_element_type=f32)
    silu_pull = jax.vjp(jax.nn.silu, cond_float)[1]
    grad_condition = silu_pull(grad_cond_act)[0]
    local_mod_w = jnp.einsum("bd,be->de", cond_act, grad_modulation, preferred_element_type=f32)
    local_mod_b = column_sums(grad_modulation)
    rest_mod_w, rest_mod_b, rest_proj_w, rest_qv_b, rest_out_w, rest_out_b = (
        lax.psum_scatter(
            local_mod_w.astype(jnp.bfloat16), "fsdp", scatter_dimension=0, tiled=True
        ).astype(jnp.float32),
        lax.psum_scatter(
            local_mod_b.astype(jnp.bfloat16), "fsdp", scatter_dimension=0, tiled=True
        ).astype(jnp.float32),
        lax.psum_scatter(
            local_proj_w.astype(jnp.bfloat16), "fsdp", scatter_dimension=0, tiled=True
        ).astype(jnp.float32),
        lax.psum_scatter(
            local_qv_b.astype(jnp.bfloat16), "fsdp", scatter_dimension=0, tiled=True
        ).astype(jnp.float32),
        lax.psum_scatter(
            local_out_w.astype(jnp.bfloat16), "fsdp", scatter_dimension=0, tiled=True
        ).astype(jnp.float32),
        lax.psum_scatter(
            local_out_b.astype(jnp.bfloat16), "fsdp", scatter_dimension=0, tiled=True
        ).astype(jnp.float32),
    )
    shares = (
        lax.psum_scatter(
            rest_mod_w.astype(jnp.bfloat16), "replica", scatter_dimension=1, tiled=True
        ).astype(jnp.float32),
        lax.psum_scatter(
            rest_proj_w.astype(jnp.bfloat16), "replica", scatter_dimension=1, tiled=True
        ).astype(jnp.float32),
        lax.psum_scatter(
            rest_out_w.astype(jnp.bfloat16), "replica", scatter_dimension=1, tiled=True
        ).astype(jnp.float32),
        lax.psum_scatter(
            mlp_exp_w.astype(jnp.bfloat16), "replica", scatter_dimension=1, tiled=True
        ).astype(jnp.float32),
        lax.psum_scatter(
            mlp_red_w.astype(jnp.bfloat16), "replica", scatter_dimension=1, tiled=True
        ).astype(jnp.float32),
    )
    sum_mod_w, sum_proj_w, sum_out_w, sum_exp_w, sum_red_w = (
        lax.all_gather(shares[0].astype(jnp.bfloat16), "replica", axis=1, tiled=True).astype(
            jnp.float32
        ),
        lax.all_gather(shares[1].astype(jnp.bfloat16), "replica", axis=1, tiled=True).astype(
            jnp.float32
        ),
        lax.all_gather(shares[2].astype(jnp.bfloat16), "replica", axis=1, tiled=True).astype(
            jnp.float32
        ),
        lax.all_gather(shares[3].astype(jnp.bfloat16), "replica", axis=1, tiled=True).astype(
            jnp.float32
        ),
        lax.all_gather(shares[4].astype(jnp.bfloat16), "replica", axis=1, tiled=True).astype(
            jnp.float32
        ),
    )
    sum_mod_b, sum_qv_b, sum_out_b, sum_exp_b, sum_red_b = lax.psum(
        (rest_mod_b, rest_qv_b, rest_out_b, mlp_exp_b, mlp_red_b), "replica"
    )
    return (
        block_out,
        grad_latents,
        grad_condition,
        sum_mod_w,
        sum_mod_b,
        sum_proj_w,
        sum_qv_b,
        sum_out_w,
        sum_out_b,
        sum_exp_w,
        sum_exp_b,
        sum_red_w,
        sum_red_b,
    )


MESH = pl.DeviceIdType.MESH
SAME_CORE = ((1, 0), (0, 1), (1, 1))
LANES = 128
HALF = 64
LANES_Q = 256


def fused_kernel(
    latents,
    cotangent,
    slots,
    live_col,
    live_row,
    cond_pack,
    mod_bias,
    extra,
    mod_w,
    proj_w,
    exp_w,
    red_w,
    out_shard,
    o_block,
    o_latents,
    o_slabs,
    o_cond,
    o_gcond,
    o_exp,
    o_red,
    o_proj,
    o_out,
    cond_all,
    extra_all,
    live_all,
    mod_send,
    mod_all,
    proj_all,
    exp_all,
    red_all,
    out_w,
    proj_pack,
    exp_pack,
    proj_wide,
    spread,
    x_one,
    x_two,
    g_mlp,
    g_attn,
    qkv,
    probs,
    attended,
    act,
    g_hid,
    d_qkv,
    part_a,
    part_b,
    sib_a,
    sib_b,
    rows_a,
    rows_b,
    norm_one,
    rstd_one,
    g_rows,
    branch_a,
    mixed,
    norm_two,
    rstd_two,
    g_mixed,
    slab,
    slabs,
    gcond,
    d_exp,
    d_red,
    d_proj,
    d_out,
    z_exp,
    z_red,
    z_proj,
    z_out,
    proj_land,
    local_sem,
    small_s,
    small_r,
    w_s,
    w_r,
    ag_s,
    ag_r,
    sb_s,
    sb_r,
    rs_s,
    rs_r,
    dz_s,
    dz_r,
    dp_s,
    dp_r,
    ow_s,
    ow_r,
    red_s,
    red_r,
    red_l,
    zr_s,
    zr_r,
    pe_s,
    et_s,
    et_r,
    et_l,
    pr_s,
    pr_r,
    pr_l,
    relay_s,
    red_f,
):
    f32 = jnp.float32
    bf16 = jnp.bfloat16
    r = lax.axis_index("replica")
    f = lax.axis_index("fsdp")
    x, y, c, z = r % 2, r // 2, f % 2, f // 2
    width = latents.shape[1]
    rows = slots.shape[0]
    part = out_shard.shape[0]
    third = width // 3
    kept = g_mixed
    blocks = red_w.shape[0] // HALF
    slots_of = red_all.shape[0] // LANES
    tiles = exp_w.shape[1] // LANES
    me = 4 * c + r
    other = (c + 1) % 2

    def ident(r2, f2):
        return {"replica": r2, "fsdp": f2}

    def remote(src, dst, s_sem, r_sem, dev):
        return pltpu.make_async_remote_copy(
            src_ref=src,
            dst_ref=dst,
            send_sem=s_sem,
            recv_sem=r_sem,
            device_id=dev,
            device_id_type=MESH,
        )

    def plane(dx, dy):
        return ((y + dy) % 2) * 2 + (x + dx) % 2

    sibling = ident(r, 2 * z + other)
    line = []
    across = (z, z + 1 - 2 * (z % 2), (z + 2) % 4, 3 - z)
    for dz in (2, 1, 3, 0):
        for dc in range(2):
            if dz or dc:
                line.append((across[dz], (c + dc) % 2))
    far = (4, 5)
    via = (0, 1)
    outer = (z == 0) | (z == 3)
    inner = (z == 1) | (z == 2)
    board = []
    for dx in range(2):
        for dy in range(2):
            for dc in range(2):
                if dx or dy or dc:
                    board.append((plane(dx, dy), (c + dc) % 2))

    barrier = pltpu.get_barrier_semaphore()
    for z2, c2 in line:
        pl.semaphore_signal(barrier, inc=1, device_id=ident(r, 2 * z2 + c2), device_id_type=MESH)
    for r2, c2 in board:
        pl.semaphore_signal(barrier, inc=1, device_id=ident(r2, 2 * z + c2), device_id_type=MESH)
    pl.semaphore_wait(barrier, len(line) + len(board))

    def line_copy(kind, k, sems_s, sems_r, src_of, dst_of):
        z2, c2 = line[k]
        f2 = 2 * z2 + c2
        return remote(
            src_of(f2, c2), dst_of(f), sems_s.at[kind, k], sems_r.at[kind, f], ident(r, f2)
        )

    def line_from(kind, k, sems_s, sems_r, src_of, dst_of):
        z2, c2 = line[k]
        f2 = 2 * z2 + c2
        return remote(
            src_of(f, c), dst_of(f2), sems_s.at[kind, k], sems_r.at[kind, f2], ident(r, f2)
        )

    def line_send(*what):
        copies = [line_copy(what[0], k, *what[1:]) for k in range(len(line))]
        for cp in copies:
            cp.start()
        return copies

    def line_wait(*what):
        for k in range(len(line)):
            line_from(what[0], k, *what[1:]).wait_recv()

    def relay_send(*what):
        for k in range(len(line)):
            cp = line_copy(what[0], k, *what[1:])
            if k in far:
                pl.when(inner)(cp.start)
            else:
                cp.start()

    def relay_copy(k, kind, sems_s, sems_r, src_of, dst_of):
        z2, c2 = line[k]
        f2 = 2 * z2 + c2
        return remote(
            dst_of(f2),
            dst_of(f2),
            relay_s.at[kind, k],
            sems_r.at[kind, f2],
            ident(r, 2 * across[1] + c),
        )

    def relay_pass(*what):
        @pl.when(outer)
        def _():
            for k in via:
                line_from(what[0], k, *what[1:]).wait_recv()

        @pl.when(inner)
        def _():
            for k in via:
                line_from(what[0], k, *what[1:]).wait_recv()
                relay_copy(k, *what).start()

    def relay_wait(*what):
        for k in range(len(line)):
            if k not in via:
                line_from(what[0], k, *what[1:]).wait_recv()

    def relay_drain(*what):
        for k in range(len(line)):
            cp = line_copy(what[0], k, *what[1:])
            if k in far:
                pl.when(inner)(cp.wait_send)
            else:
                cp.wait_send()

        @pl.when(inner)
        def _():
            for k in via:
                relay_copy(k, *what).wait_send()

    def drain(copies):
        for cp in copies:
            cp.wait_send()

    def cond_src(f2, c2):
        return cond_pack.at[f2]

    def cond_dst(f2):
        return cond_all.at[f2]

    def extra_src(f2, c2):
        return extra.at[c2]

    def extra_dst(f2):
        return extra_all.at[f2]

    def proj_src(f2, c2):
        return proj_pack.at[c2]

    def proj_dst(f2):
        return proj_all.at[pl.ds(pl.multiple_of(f2 * part, 16), part)]

    tail = pl.ds(LANES, exp_all.shape[1] - LANES)
    head = pl.ds(0, LANES)

    def exp_src(f2, c2):
        return exp_pack.at[c2, :, tail]

    def exp_dst(f2):
        return exp_all.at[pl.ds(pl.multiple_of(f2 * part, 16), part), tail]

    def exp_head(f2):
        return exp_all.at[pl.ds(pl.multiple_of(f2 * part, 16), part), head]

    def half_tile(i):
        p = i // 2
        c2 = p // slots_of
        at = 2 * (r + 4 * p) + i % 2
        return c2, 2 * (p - 4 * c2) + i % 2, at // blocks, at % blocks

    def red_rows(j):
        return red_all.at[pl.ds(pl.multiple_of(j * HALF, HALF), HALF)]

    def red_copy(i, z2):
        c2, j, owner, block = half_tile(i)
        return remote(
            red_w.at[pl.ds(pl.multiple_of(block * HALF, HALF), HALF)],
            red_rows(j),
            red_s.at[i, z2],
            red_r.at[j],
            ident(r, 2 * z2 + c2),
        )

    def red_local(i):
        c2, j, owner, block = half_tile(i)
        return pltpu.make_async_copy(
            red_w.at[pl.ds(pl.multiple_of(block * HALF, HALF), HALF)], red_rows(j), red_l.at[j]
        )

    def red_goes(i, z2):
        c2, j, owner, block = half_tile(i)
        return (owner == f) & (2 * z2 + c2 != f) & (inner | (z2 + z != 3))

    def red_stops(i):
        c2, j, owner, block = half_tile(i)
        return (c2 == c) & (owner // 2 == across[2])

    def red_onward(i):
        c2, j, owner, block = half_tile(i)
        return remote(
            red_rows(j), red_rows(j), red_f.at[j], red_r.at[j], ident(r, 2 * across[1] + c)
        )

    def each_half(step):
        def body(i, carry):
            step(i)
            return carry

        lax.fori_loop(0, 2 * blocks, body, 0)

    def red_send():
        def step(i):
            c2, j, owner, block = half_tile(i)
            for z2 in range(4):
                pl.when(red_goes(i, z2))(red_copy(i, z2).start)
            pl.when((owner == f) & (c2 == c))(red_local(i).start)

        each_half(step)

    def red_pass():
        def step(i):
            @pl.when(red_stops(i))
            def _():
                red_copy(i, z).wait_recv()
                pl.when(inner)(red_onward(i).start)

        each_half(step)

    def red_wait():
        def step(i):
            c2, j, owner, block = half_tile(i)
            pl.when((c2 == c) & (owner != f) & (owner // 2 != across[2]))(red_copy(i, z).wait_recv)
            pl.when((owner == f) & (c2 == c))(red_local(i).wait)

        each_half(step)

    def red_drain():
        def step(i):
            for z2 in range(4):
                pl.when(red_goes(i, z2))(red_copy(i, z2).wait_send)
            pl.when(red_stops(i) & inner)(red_onward(i).wait_send)

        each_half(step)

    exp_main = (1, w_s, w_r, exp_src, exp_dst)
    proj_main = (0, w_s, w_r, proj_src, proj_dst)

    def first_src(f2, c2):
        return exp_pack.at[0, :, head]

    exp_lead = (2, w_s, w_r, first_src, exp_head)

    def lead_send(start):
        for k, (z2, c2) in enumerate(line):
            keep = c2 == 0
            if k in far:
                keep = keep & inner
            cp = line_copy(exp_lead[0], k, *exp_lead[1:])
            pl.when(keep)(cp.start if start else cp.wait_send)

    def exp_send():
        relay_send(*exp_main)
        lead_send(True)

    def exp_pass():
        relay_pass(*exp_main)

        @pl.when(c == 0)
        def _():
            relay_pass(*exp_lead)

    def exp_wait():
        relay_wait(*exp_main)

        @pl.when(c == 0)
        def _():
            relay_wait(*exp_lead)

    def exp_drain():
        relay_drain(*exp_main)
        lead_send(False)

        @pl.when((c == 0) & inner)
        def _():
            for k in via:
                relay_copy(k, *exp_lead).wait_send()

    sent = line_send(0, small_s, small_r, cond_src, cond_dst)
    sent += line_send(1, small_s, small_r, extra_src, extra_dst)
    packs = []
    for c2 in range(2):
        for i in range(slots_of):
            if c2 and not i:
                continue
            tile = r + 4 * (4 * c2 + i)
            cp = pltpu.make_async_copy(
                exp_w.at[:, pl.ds(pl.multiple_of(tile * LANES, LANES), LANES)],
                exp_pack.at[c2, :, pl.ds(i * LANES, LANES)],
                pe_s.at[c2, i],
            )
            cp.start()
            packs.append(cp)
    live_sent = []
    for k, (r2, c2) in enumerate(board):
        cp = remote(
            live_row,
            live_all.at[me],
            small_s.at[3, k],
            small_r.at[3, me],
            ident(r2, 2 * z + c2),
        )
        cp.start()
        live_sent.append(cp)
    local = [
        pltpu.make_async_copy(cond_pack.at[f], cond_all.at[f], local_sem.at[0]),
        pltpu.make_async_copy(extra.at[c], extra_all.at[f], local_sem.at[1]),
        pltpu.make_async_copy(live_row, live_all.at[me], local_sem.at[5]),
    ]
    for cp in local:
        cp.start()

    def one_hot():
        ids = lax.broadcasted_iota(jnp.int32, (rows, latents.shape[0]), 1)
        return jnp.where(ids == slots[...], 1.0, 0.0)

    def dot(a, b):
        return jnp.dot(a, b, preferred_element_type=f32)

    def dot_t(a, b):
        return lax.dot_general(a, b, (((1,), (1,)), ((), ())), preferred_element_type=f32)

    def t_dot(a, b):
        return lax.dot_general(a, b, (((0,), (0,)), ((), ())), preferred_element_type=f32)

    local[0].wait()
    line_wait(0, small_s, small_r, cond_src, cond_dst)
    cond_cols = jnp.sum(cond_all[...].astype(f32), axis=1).astype(bf16)
    mod_send[...] = jnp.zeros(mod_send.shape, f32)
    for p in range(6):
        piece = dot(cond_cols, mod_w[:, p * width : (p + 1) * width]) + mod_bias[p : p + 1, :]
        mod_send[:, p, :] = piece

    def mod_src(f2, c2):
        return mod_send.at[f2]

    def mod_dst(f2):
        return mod_all.at[f2]

    sent += line_send(2, small_s, small_r, mod_src, mod_dst)
    mod_all[f] = mod_send[f]

    wide_columns = proj_all.shape[1]
    for c2 in range(2):
        t = 2 * r + c2
        picked = jnp.zeros((part, wide_columns), f32)
        for q in range(3):
            window = proj_w[
                :, pl.ds(pl.multiple_of(q * width + t * LANES, LANES), LANES_Q)
            ]
            source = lax.broadcasted_iota(jnp.int32, (LANES_Q, wide_columns), 0)
            goal = lax.broadcasted_iota(jnp.int32, (LANES_Q, wide_columns), 1)
            picks = (source - t * (part - LANES) == goal - q * part) & (
                (goal >= q * part) & (goal < (q + 1) * part)
            )
            picked += dot(window, jnp.where(picks, 1.0, 0.0).astype(bf16))
        proj_pack[c2] = picked.astype(bf16)
    relay_send(0, w_s, w_r, proj_src, proj_dst)
    own_proj = pltpu.make_async_copy(proj_pack.at[c], proj_dst(f), local_sem.at[2])
    own_proj.start()
    local.append(own_proj)

    kept[...] = dot(one_hot().astype(bf16), latents[...])
    g_rows[...] = dot((one_hot() * live_col[...]).astype(bf16), cotangent[...])

    def normalise(values, norm_ref, rstd_ref):
        centred = values - jnp.mean(values, axis=-1, keepdims=True)
        rstd = lax.rsqrt(jnp.mean(centred * centred, axis=-1, keepdims=True) + 1e-06)
        norm_ref[...] = centred * rstd
        rstd_ref[...] = rstd

    normalise(kept[...], norm_one, rstd_one)
    out_w[part:, :] = jnp.zeros((out_w.shape[0] - part, width), bf16)
    split = lax.broadcasted_iota(jnp.int32, spread.shape, 0)
    column = lax.broadcasted_iota(jnp.int32, spread.shape, 1)
    skip = jnp.where(split >= part, LANES_Q - part, 0) + jnp.where(
        split >= 2 * part, LANES_Q - part, 0
    )
    spread[...] = jnp.where(column == split + skip, 1.0, 0.0).astype(bf16)

    @pl.when(c == 1)
    def _():
        exp_all[:, :LANES] = jnp.zeros((width, LANES), bf16)
        red_all[:LANES, :] = jnp.zeros((LANES, width), bf16)

    for cp in local[1:]:
        cp.wait()

    line_wait(2, small_s, small_r, mod_src, mod_dst)
    modulation = jnp.sum(mod_all[...], axis=0)
    shift_attn, scale_attn, gate_attn, shift_mlp, scale_mlp, gate_mlp = [
        modulation[p : p + 1, :] for p in range(6)
    ]

    def own(ref):
        return ref.at[pl.ds(pl.multiple_of(me * rows, rows), rows)]

    def slot(ref, u):
        return ref.at[pl.ds(pl.multiple_of(u * rows, rows), rows)]

    def gather_start(kind, buf):
        copies = [
            remote(own(buf), own(buf), ag_s.at[kind, 0], ag_r.at[kind, me], sibling),
        ]
        for k, (dx, dy) in enumerate(SAME_CORE):
            copies.append(
                remote(
                    own(buf),
                    own(buf),
                    ag_s.at[kind, 1 + k],
                    ag_r.at[kind, me],
                    ident(plane(dx, dy), f),
                )
            )
        for cp in copies:
            cp.start()
        return copies

    def gather_end(kind, buf):
        copies = []
        for k, (dx, dy) in enumerate(SAME_CORE):
            u = 4 * c + plane(dx, dy)
            cp = remote(slot(buf, u), slot(buf, u), ag_s.at[kind, 4 + k], ag_r.at[kind, u], sibling)
            cp.wait_recv()
            cp.start()
            copies.append(cp)
        for r2 in range(4):
            u = 4 * other + r2
            remote(
                slot(buf, u), slot(buf, u), ag_s.at[kind, 0], ag_r.at[kind, u], sibling
            ).wait_recv()
        return copies

    def reduce_send(kind, buf, landing, r2):
        remote(
            slot(buf, 4 * c + r2),
            landing.at[r],
            rs_s.at[kind, r2],
            rs_r.at[kind, r],
            ident(r2, f),
        ).start()

    def reduce_chunk(kind, k, cc, values, buf, sib, landing, hold=False):
        base = pl.multiple_of(cc * 4 * rows + (k % 2) * 2 * rows, 2 * rows)
        here = pl.ds(base, 2 * rows)
        there = pl.ds(pl.multiple_of((k % 2) * 2 * rows, 2 * rows), 2 * rows)
        slot_k = k % 2

        @pl.when(k < 2)
        def _():
            buf[here, :] = values.astype(bf16)
            remote(
                buf.at[here], sib.at[there], sb_s.at[kind, slot_k], sb_r.at[kind, slot_k], sibling
            ).start()

        @pl.when(k >= 2)
        def _():
            remote(
                buf.at[here], sib.at[there], sb_s.at[kind, slot_k], sb_r.at[kind, slot_k], sibling
            ).wait_recv()
            buf[here, :] = (values + sib[there, :].astype(f32)).astype(bf16)
            for x2 in range(0 if hold else 2):
                r2 = 2 * slot_k + x2

                @pl.when(r2 != r)
                def _():
                    reduce_send(kind, buf, landing, r2)

    def reduce_end(kind, buf, landing):
        total = own(buf)[...].astype(f32)
        for dx, dy in SAME_CORE:
            r2 = plane(dx, dy)
            remote(
                own(buf), landing.at[r2], rs_s.at[kind, r2], rs_r.at[kind, r2], ident(r2, f)
            ).wait_recv()
            total += landing[r2].astype(f32)
        return total

    def reduce_drain(kind, buf, sib, landing):
        for k in range(2):
            there = pl.ds(k * 2 * rows, 2 * rows)
            remote(
                sib.at[there], sib.at[there], sb_s.at[kind, k], sb_r.at[kind, k], sibling
            ).wait_send()
        for dx, dy in SAME_CORE:
            r2 = plane(dx, dy)
            remote(
                own(buf), landing.at[r2], rs_s.at[kind, r2], rs_r.at[kind, r2], ident(r2, f)
            ).wait_send()

    own(x_one)[...] = (norm_one[...] * (1.0 + scale_attn) + shift_attn).astype(bf16)
    sent += gather_start(0, x_one)
    grad_mlp = (gate_mlp * g_rows[...]).astype(bf16)
    own(g_mlp)[...] = grad_mlp
    slab[...] = jnp.zeros(slab.shape, f32)
    slab[6:7, :] = jnp.sum(grad_mlp.astype(f32), axis=0, keepdims=True)

    def out_copy(z2):
        return remote(
            out_shard,
            out_w.at[pl.ds(0, part)],
            ow_s.at[z2],
            ow_r.at[0],
            ident(r, 2 * z2 + c),
        )

    def out_onward():
        return remote(
            out_w.at[pl.ds(0, part)],
            out_w.at[pl.ds(0, part)],
            ow_s.at[7],
            ow_r.at[0],
            ident(r, 2 * across[1] + c),
        )

    def out_goes(z2):
        return (z == r) & (z2 != z) & (inner | (z2 + z != 3))

    for z2 in range(4):
        pl.when(out_goes(z2))(out_copy(z2).start)

    @pl.when(z == r)
    def _():
        out_w[:part, :] = out_shard[...]

    relay_pass(*proj_main)
    relay_wait(*proj_main)
    for cp in packs:
        cp.wait()
    own_exp = pltpu.make_async_copy(exp_pack.at[c, :, tail], exp_dst(f), local_sem.at[3])
    own_exp.start()

    @pl.when(c == 0)
    def _():
        cp = pltpu.make_async_copy(exp_pack.at[0, :, head], exp_head(f), local_sem.at[6])
        cp.start()
        cp.wait()

    exp_send()
    proj_wide[...] = dot(proj_all[...], spread[...]).astype(bf16)
    line_wait(1, small_s, small_r, extra_src, extra_dst)
    biases = jnp.sum(extra_all[...].astype(f32), axis=0)
    out_b, red_b, exp_b, qv_b = [biases[p : p + 1, :] for p in range(4)]
    for k, (r2, c2) in enumerate(board):
        remote(
            live_row,
            live_all.at[4 * c2 + r2],
            small_s.at[3, k],
            small_r.at[3, 4 * c2 + r2],
            ident(r2, 2 * z + c2),
        ).wait_recv()
    sent += gather_end(0, x_one)
    sent += gather_start(1, g_mlp)
    cond_sent = []
    for k, (dx, dy) in enumerate(SAME_CORE):
        cp = remote(
            cond_all,
            o_cond.at[r],
            small_s.at[4, k],
            small_r.at[4, r],
            ident(plane(dx, dy), f),
        )
        cp.start()
        cond_sent.append(cp)
    own_cond = pltpu.make_async_copy(cond_all, o_cond.at[r], local_sem.at[0])
    own_cond.start()

    lane = lax.broadcasted_iota(jnp.int32, (1, LANES_Q), 1)
    heads = [
        jnp.where((lane >= h * HEAD_DIM) & (lane < (h + 1) * HEAD_DIM), 1.0, 0.0).astype(bf16)
        for h in range(2)
    ]
    scale = HEAD_DIM ** (-0.5)

    @pl.when(z != r)
    def _():
        out_copy(z).wait_recv()

    pl.when(inner & (across[2] == r))(out_onward().start)
    red_send()

    def chunk_of(k):
        cc = (c + 1 + k // 2) % 2
        first = 4 * cc + 2 * (k % 2)
        return cc, first, pl.ds(pl.multiple_of(first * rows, 2 * rows), 2 * rows)

    def attend(k, carry):
        cc, first, here = chunk_of(k)
        wide = dot(x_one[here, :], proj_wide[...])
        qkv[here, :LANES_Q] = (wide[:, :LANES_Q] + qv_b[:, :LANES_Q]).astype(bf16)
        qkv[here, LANES_Q : 2 * LANES_Q] = wide[:, LANES_Q : 2 * LANES_Q].astype(bf16)
        qkv[here, 2 * LANES_Q :] = (
            wide[:, 2 * LANES_Q :] + qv_b[:, LANES_Q : 2 * LANES_Q]
        ).astype(bf16)
        for i in range(2):
            u = first + i
            at = pl.ds(pl.multiple_of(u * rows, rows), rows)
            q = qkv[at, :LANES_Q]
            key = qkv[at, LANES_Q : 2 * LANES_Q]
            val = qkv[at, 2 * LANES_Q :]
            alive = live_all[u][0:1, :] > 0.5
            total = jnp.zeros((rows, LANES_Q), f32)
            for h in range(2):
                s = dot_t(q * heads[h], key) * scale
                s = jnp.where(alive, s, -1e30)
                e = jnp.exp(s - jnp.max(s, axis=-1, keepdims=True))
                p = e / jnp.sum(e, axis=-1, keepdims=True)
                probs[2 * u + h] = p
                total += dot(p.astype(bf16), val) * heads[h].astype(f32)
            attended[at, :] = total.astype(bf16)
        values = dot(attended[here, :], out_w[...])
        reduce_chunk(0, k, cc, values, part_a, sib_a, rows_a)
        return carry

    lax.fori_loop(0, 4, attend, 0)
    exp_pass()
    branch = reduce_end(0, part_a, rows_a) + out_b
    branch_a[...] = branch
    mixed[...] = kept[...] + gate_attn * branch
    normalise(mixed[...], norm_two, rstd_two)
    own(x_two)[...] = (norm_two[...] * (1.0 + scale_mlp) + shift_mlp).astype(bf16)
    sent += gather_start(2, x_two)
    sent += gather_end(1, g_mlp)
    red_pass()
    exp_wait()
    own_exp.wait()
    red_wait()
    sent += gather_end(2, x_two)
    reduce_drain(0, part_a, sib_a, rows_a)

    k_gelu = 0.7978845608028654
    hid_b = exp_b[:, : exp_all.shape[1]]

    def feed(k, carry):
        cc, first, here = chunk_of(k)
        hid = dot(x_two[here, :], exp_all[...]) + hid_b
        square = hid * hid
        th = jnp.tanh(k_gelu * hid * (1.0 + 0.044715 * square))
        act[here, :] = (0.5 * hid * (1.0 + th)).astype(bf16)
        slope = 0.5 * (1.0 + th) + 0.5 * hid * (1.0 - th * th) * k_gelu * (
            1.0 + 3.0 * 0.044715 * square
        )
        grad = (dot_t(g_mlp[here, :], red_all[...]) * slope).astype(bf16)
        g_hid[here, :] = grad
        values = dot_t(grad, exp_all[...])
        reduce_chunk(1, k, cc, values, part_b, sib_b, rows_b)
        return carry

    lax.fori_loop(0, 4, feed, 0)

    hid_sum = jnp.sum(g_hid[...].astype(f32), axis=0, keepdims=True)
    slab[8:9, : exp_all.shape[1]] = hid_sum

    def zsend(kind, src, landing, height, lanes=slice(None)):
        copies = []
        for dz in range(1, 4):
            z2 = (z + dz) % 4
            cp = remote(
                src.at[pl.ds(pl.multiple_of(z2 * height, 16), height), lanes],
                landing.at[dz - 1, :, lanes],
                dz_s.at[kind, dz - 1],
                dz_r.at[kind, dz - 1],
                ident(r, 2 * z2 + c),
            )
            cp.start()
            copies.append(cp)
        return copies

    def wide_grad(k, carry):
        at = pl.ds(pl.multiple_of(k * third, 128), third)
        d_exp[at, :] = t_dot(x_two[:, at], g_hid[...]).astype(bf16)
        return carry

    lax.fori_loop(0, 3, wide_grad, 0)
    sent += zsend(0, d_exp, z_exp, 2 * part, tail)

    @pl.when(c == 0)
    def _():
        zsend(1, d_exp, z_exp, 2 * part, head)


    grad_two = reduce_end(1, part_b, rows_b)

    def back_norm(grad, scale_part, norm, rstd):
        g_shift = jnp.sum(grad, axis=0, keepdims=True)
        g_scale = jnp.sum(grad * norm, axis=0, keepdims=True)
        e = grad * (1.0 + scale_part)
        inner = jnp.mean(e * norm, axis=-1, keepdims=True)
        return g_shift, g_scale, (e - jnp.mean(e, axis=-1, keepdims=True) - norm * inner) * rstd

    g_shift, g_scale, through = back_norm(grad_two, scale_mlp, norm_two[...], rstd_two[...])
    slab[3:4, :] = g_shift
    slab[4:5, :] = g_scale
    g_mixed[...] = g_rows[...] + through
    slab[2:3, :] = jnp.sum(g_mixed[...] * branch_a[...], axis=0, keepdims=True)
    grad_at = (gate_attn * g_mixed[...]).astype(bf16)
    own(g_attn)[...] = grad_at
    slab[7:8, :] = jnp.sum(grad_at.astype(f32), axis=0, keepdims=True)
    sent += gather_start(3, g_attn)

    def red_grad(k, carry):
        at = pl.ds(pl.multiple_of(k * third, 128), third)
        d_red[:, at] = t_dot(act[...], g_mlp[:, at]).astype(bf16)
        return carry

    lax.fori_loop(0, 3, red_grad, 0)

    def red_tile(i):
        p = 4 * c + i
        at = r + 4 * p
        return (p >= 5 * c), at, (2 * at) // (2 * blocks)

    def red_up(i, src_z):
        there = (src_z - red_tile(i)[2] + 4) % 4 - 1
        return remote(
            d_red.at[pl.ds(i * LANES, LANES)],
            z_red.at[there, i % 3],
            zr_s.at[i],
            zr_r.at[there, i % 3],
            ident(r, 2 * red_tile(i)[2] + c),
        )

    for i in range(slots_of):
        real, at, goal = red_tile(i)

        @pl.when(real & (goal != z))
        def _():
            red_up(i, z).start()

    reduce_drain(1, part_b, sib_b, rows_b)
    def feed_out(k, carry):
        cc, first, here = chunk_of(k)
        values = dot(act[here, :], red_all[...])
        reduce_chunk(3, k, cc, values, part_b, sib_a, rows_b, hold=True)
        return carry

    lax.fori_loop(0, 4, feed_out, 0)

    sent += gather_end(3, g_attn)
    for dx, dy in SAME_CORE:
        reduce_send(3, part_b, rows_b, plane(dx, dy))

    def attend_back(k, carry):
        cc, first, here = chunk_of(k)
        g_att = dot_t(g_attn[here, :], out_w[...]).astype(bf16)
        for i in range(2):
            u = first + i
            at = pl.ds(pl.multiple_of(u * rows, rows), rows)
            q = qkv[at, :LANES_Q]
            key = qkv[at, LANES_Q : 2 * LANES_Q]
            val = qkv[at, 2 * LANES_Q :]
            up = g_att[i * rows : (i + 1) * rows, :]
            g_q = jnp.zeros((rows, LANES_Q), f32)
            g_k = jnp.zeros((rows, LANES_Q), f32)
            g_v = jnp.zeros((rows, LANES_Q), f32)
            for h in range(2):
                p = probs[2 * u + h]
                up_h = up * heads[h]
                g_v += t_dot(p.astype(bf16), up_h)
                g_p = dot_t(up_h, val)
                inner = jnp.sum(g_p * p, axis=-1, keepdims=True)
                g_s = (p * (g_p - inner)).astype(bf16)
                g_q += dot(g_s, key) * heads[h].astype(f32)
                g_k += t_dot(g_s, q * heads[h])
            wide = jnp.concatenate([g_q * scale, g_k * scale, g_v], axis=1).astype(bf16)
            d_qkv[at, :] = dot_t(wide, spread[...]).astype(bf16)
        values = dot_t(d_qkv[here, :], proj_all[...])
        reduce_chunk(2, k, cc, values, part_a, sib_b, rows_a)
        return carry

    lax.fori_loop(0, 4, attend_back, 0)

    own_z = pl.ds(pl.multiple_of(z * 2 * part, 16), 2 * part)

    def line_sum(kind, src, landing, lanes):
        total = src[own_z, lanes].astype(f32)
        for dz in range(1, 4):
            remote(
                src.at[own_z, lanes],
                landing.at[dz - 1, :, lanes],
                dz_s.at[kind, dz - 1],
                dz_r.at[kind, dz - 1],
                ident(r, 2 * ((z + dz) % 4) + c),
            ).wait_recv()
            total += landing[dz - 1, :, lanes].astype(f32)
        src[own_z, lanes] = total.astype(bf16)

    def exp_up(k, i, r2, c2):
        at = red_tile(i)[1]
        return remote(
            d_exp.at[
                pl.ds(pl.multiple_of(z * 2 * part + c2 * part, 16), part), pl.ds(i * LANES, LANES)
            ],
            o_exp.at[:, pl.ds(pl.multiple_of(at * LANES, LANES), LANES)],
            et_s.at[k, i],
            et_r.at[at],
            ident(r2, 2 * z + c2),
        )

    def exp_here(i):
        at = red_tile(i)[1]
        return pltpu.make_async_copy(
            d_exp.at[
                pl.ds(pl.multiple_of(z * 2 * part + c * part, 16), part), pl.ds(i * LANES, LANES)
            ],
            o_exp.at[:, pl.ds(pl.multiple_of(at * LANES, LANES), LANES)],
            et_l.at[i],
        )

    line_sum(0, d_exp, z_exp, tail)

    @pl.when(c == 0)
    def _():
        line_sum(1, d_exp, z_exp, head)

    for i in range(slots_of):

        @pl.when(red_tile(i)[0])
        def _():
            for k, (r2, c2) in enumerate(board):
                exp_up(k, i, r2, c2).start()
            exp_here(i).start()

    def red_out(i, h, r2):
        half = 2 * red_tile(i)[1] + h
        return remote(
            d_red.at[pl.ds(i * LANES + h * HALF, HALF)],
            o_red.at[pl.ds(pl.multiple_of(half % blocks * HALF, HALF), HALF)],
            pr_s.at[2 * i + h, r2],
            pr_r.at[half % blocks],
            ident(r2, half // blocks),
        )

    def red_here(i, h):
        half = 2 * red_tile(i)[1] + h
        return pltpu.make_async_copy(
            d_red.at[pl.ds(i * LANES + h * HALF, HALF)],
            o_red.at[pl.ds(pl.multiple_of(half % blocks * HALF, HALF), HALF)],
            pr_l.at[2 * i + h],
        )

    def red_each(i, remote_part, local_part):
        for h in range(2):
            owner = (2 * red_tile(i)[1] + h) // blocks
            for r2 in range(4):

                @pl.when((owner != f) | (r2 != r))
                def _():
                    remote_part(red_out(i, h, r2))

            @pl.when(owner == f)
            def _():
                local_part(red_here(i, h))


    def proj_grad(k, carry):
        at = pl.ds(pl.multiple_of(k * third, 128), third)
        d_proj[at, :] = t_dot(x_one[:, at], d_qkv[...]).astype(bf16)
        return carry

    lax.fori_loop(0, 3, proj_grad, 0)
    sent += zsend(2, d_proj, z_proj, 2 * part)
    d_out[...] = t_dot(attended[...], g_attn[...]).astype(bf16)

    @pl.when(z != r)
    def _():
        slot_z = (r - z + 4) % 4 - 1
        remote(
            d_out.at[pl.ds(0, part)],
            z_out.at[slot_z],
            ow_s.at[8],
            ow_r.at[1 + slot_z],
            ident(r, 2 * r + c),
        ).start()

    slab[9:10, : d_qkv.shape[1]] = jnp.sum(d_qkv[...].astype(f32), axis=0, keepdims=True)


    for i in range(slots_of):
        real, at, goal = red_tile(i)

        @pl.when(real & (goal == z))
        def _():
            rows_i = slice(i * LANES, (i + 1) * LANES)
            total = d_red[rows_i, :].astype(f32)
            for there in range(3):
                remote(
                    d_red.at[pl.ds(i * LANES, LANES)],
                    z_red.at[there, i % 3],
                    zr_s.at[i],
                    zr_r.at[there, i % 3],
                    ident(r, f),
                ).wait_recv()
                total += z_red[there, i % 3].astype(f32)
            d_red[rows_i, :] = total.astype(bf16)
            red_each(i, lambda cp: cp.start(), lambda cp: cp.start())

    def place(values, base):
        live_hot = (one_hot() * live_col[...]).astype(bf16)
        placed = t_dot(live_hot, values.astype(bf16))
        hit = t_dot(live_hot, jnp.ones((rows, 128), bf16))[:, 0:1]
        return jnp.where(hit > 0.5, placed.astype(bf16), base)

    branch = reduce_end(3, part_b, rows_b) + red_b
    slab[5:6, :] = jnp.sum(g_rows[...] * branch, axis=0, keepdims=True)
    o_block[...] = place(mixed[...] + gate_mlp * branch, latents[...])

    def slab_at(f2):
        return 4 * (f2 % 2) + f2 // 2

    grad_one = reduce_end(2, part_a, rows_a)
    g_shift, g_scale, through = back_norm(grad_one, scale_attn, norm_one[...], rstd_one[...])
    slab[0:1, :] = g_shift
    slab[1:2, :] = g_scale
    o_latents[...] = place(g_mixed[...] + through, cotangent[...])
    slabs[slab_at(f)] = slab[...].astype(bf16)

    def slab_src(f2, c2):
        return slabs.at[slab_at(f)]

    def slab_dst(f2):
        return slabs.at[slab_at(f2)]

    sent += line_send(5, small_s, small_r, slab_src, slab_dst)

    @pl.when(z == r)
    def _():
        total = d_out[:part, :].astype(f32)
        for k in range(3):
            remote(
                d_out.at[pl.ds(0, part)], z_out.at[k], ow_s.at[3], ow_r.at[1 + k], ident(r, f)
            ).wait_recv()
            total += z_out[k].astype(f32)
        d_out[:part, :] = total.astype(bf16)
        for k, (dx, dy) in enumerate(SAME_CORE):
            remote(
                d_out.at[pl.ds(0, part)], o_out, ow_s.at[4 + k], ow_r.at[4], ident(plane(dx, dy), f)
            ).start()
        cp = pltpu.make_async_copy(d_out.at[pl.ds(0, part)], o_out, local_sem.at[5])
        cp.start()
        cp.wait()

    line_wait(5, small_s, small_r, slab_src, slab_dst)
    mine = pl.ds(pl.multiple_of(4 * c, 4), 4)
    for k, (dx, dy) in enumerate(SAME_CORE):
        cp = remote(
            slabs.at[mine],
            o_slabs.at[r, mine],
            small_s.at[6, k],
            small_r.at[6, r],
            ident(plane(dx, dy), f),
        )
        cp.start()
        sent.append(cp)
    own_slabs = pltpu.make_async_copy(slabs, o_slabs.at[r], local_sem.at[4])
    own_slabs.start()
    back_cond = jnp.zeros((8, part), f32)
    for p in range(6):
        back_cond += dot_t(slabs[:, p, :], mod_w[:, p * width : (p + 1) * width])
    for i in range(8):
        gcond[2 * (i % 4) + i // 4] = jnp.broadcast_to(back_cond[i : i + 1, :], (8, part))

    def gc_src(f2, c2):
        return gcond.at[f2]

    def gc_dst(f2):
        return o_gcond.at[f2]

    sent += line_send(7, small_s, small_r, gc_src, gc_dst)
    o_gcond[f] = gcond[f]

    every = slice(None)
    line_sum(2, d_proj, z_proj, every)

    def proj_up(k, r2, c2):
        return remote(
            d_proj.at[pl.ds(pl.multiple_of(z * 2 * part + c2 * part, 16), part)],
            proj_land.at[me],
            dp_s.at[k],
            dp_r.at[me],
            ident(r2, 2 * z + c2),
        )

    for k, (r2, c2) in enumerate(board):
        proj_up(k, r2, c2).start()
    proj_land[me] = d_proj[pl.ds(pl.multiple_of(z * 2 * part + c * part, 16), part), :]

    for k, (dx, dy) in enumerate(SAME_CORE):
        r2 = plane(dx, dy)
        remote(
            slabs.at[mine], o_slabs.at[r2, mine], small_s.at[6, 0], small_r.at[6, r2], sibling
        ).wait_recv()
        cp = remote(
            o_slabs.at[r2, mine],
            o_slabs.at[r2, mine],
            small_s.at[6, 3 + k],
            small_r.at[6, 4 + r2],
            sibling,
        )
        cp.start()
        sent.append(cp)
    line_wait(7, small_s, small_r, gc_src, gc_dst)
    for dx, dy in SAME_CORE:
        r2 = plane(dx, dy)
        remote(
            cond_all, o_cond.at[r2], small_s.at[4, 0], small_r.at[4, r2], ident(r2, f)
        ).wait_recv()
        theirs = pl.ds(pl.multiple_of(4 * other, 4), 4)
        remote(
            slabs.at[theirs], o_slabs.at[r2, theirs], small_s.at[6, 3], small_r.at[6, 4 + r2], sibling
        ).wait_recv()
    for r2, c2 in board:
        u = 4 * c2 + r2
        remote(
            proj_land.at[u], proj_land.at[u], dp_s.at[0], dp_r.at[u], ident(r2, 2 * z + c2)
        ).wait_recv()

    o_proj[...] = jnp.zeros(o_proj.shape, bf16)
    for u in range(8):
        t = 2 * (u % 4) + u // 4
        wide = dot(proj_land[u], spread[...])
        for q in range(3):
            piece = wide[:, q * LANES_Q : (q + 1) * LANES_Q]
            if t:
                piece = pltpu.roll(piece, t * (part - LANES), 1)
            first = q * width + t * LANES
            o_proj[:, first : first + LANES_Q] = (
                o_proj[:, first : first + LANES_Q].astype(f32) + piece
            ).astype(bf16)

    def tile_arrival(at, carry):
        p = at // 4

        @pl.when((at % 4 != r) | (p // slots_of != c))
        def _():
            remote(
                d_exp.at[pl.ds(0, part), pl.ds(0, LANES)],
                o_exp.at[:, pl.ds(pl.multiple_of(at * LANES, LANES), LANES)],
                et_s.at[0, 0],
                et_r.at[at],
                sibling,
            ).wait_recv()

        return carry

    lax.fori_loop(0, tiles, tile_arrival, 0)

    def block_arrival(block, carry):
        at = (blocks * f + block) // 2
        p = at // 4

        @pl.when((at % 4 != r) | (p // slots_of != c))
        def _():
            remote(
                d_red.at[pl.ds(0, HALF)],
                o_red.at[pl.ds(pl.multiple_of(block * HALF, HALF), HALF)],
                pr_s.at[0, 0],
                pr_r.at[block],
                sibling,
            ).wait_recv()

        return carry

    lax.fori_loop(0, blocks, block_arrival, 0)
    for i in range(slots_of):
        real, at, goal = red_tile(i)

        @pl.when(real)
        def _():
            for k, (r2, c2) in enumerate(board):
                exp_up(k, i, r2, c2).wait_send()
            exp_here(i).wait()

        @pl.when(real & (goal == z))
        def _():
            red_each(i, lambda cp: cp.wait_send(), lambda cp: cp.wait())

        @pl.when(real & (goal != z))
        def _():
            red_up(i, z).wait_send()

    for k, (r2, c2) in enumerate(board):
        proj_up(k, r2, c2).wait_send()
    red_drain()
    exp_drain()

    @pl.when(c == 0)
    def _():
        for dz in range(1, 4):
            remote(
                d_exp.at[own_z, head],
                z_exp.at[dz - 1, :, head],
                dz_s.at[1, dz - 1],
                dz_r.at[1, dz - 1],
                ident(r, f),
            ).wait_send()

    for z2 in range(4):
        pl.when(out_goes(z2))(out_copy(z2).wait_send)
    pl.when(inner & (across[2] == r))(out_onward().wait_send)

    @pl.when(z == r)
    def _():
        for k in range(3):
            remote(out_shard, o_out, ow_s.at[4 + k], ow_r.at[4], ident(r, f)).wait_send()

    @pl.when(z != r)
    def _():
        remote(out_shard, o_out, ow_s.at[3], ow_r.at[4], ident(r, f)).wait_recv()
        remote(
            d_out.at[pl.ds(0, part)], z_out.at[0], ow_s.at[8], ow_r.at[1], ident(r, f)
        ).wait_send()

    relay_drain(*proj_main)
    reduce_drain(2, part_a, sib_b, rows_a)
    reduce_drain(3, part_b, sib_a, rows_b)
    drain(sent)
    drain(live_sent)
    drain(cond_sent)
    own_cond.wait()
    own_slabs.wait()


def fused_local(
    latents,
    condition,
    bucket,
    keep_slots,
    modulation_weight,
    modulation_bias,
    projection_weight,
    query_value_bias,
    output_weight,
    output_bias,
    expand_weight,
    expand_bias,
    reduce_weight,
    reduce_bias,
    cotangent,
):
    f32 = jnp.float32
    bf16 = jnp.bfloat16
    r = lax.axis_index("replica")
    f = lax.axis_index("fsdp")
    slot_count, width = latents.shape[1:]
    rows = keep_slots.shape[1]
    part = output_weight.shape[0]
    hid = expand_weight.shape[1]
    slots_of = (hid // LANES + 7) // 8
    wide = slots_of * LANES

    def placed(shard, count):
        return lax.dynamic_update_slice_in_dim(
            jnp.zeros((count,), f32), shard.astype(f32), f * shard.shape[0], 0
        )

    def mine(value, axis):
        return lax.dynamic_slice_in_dim(value, 2 * r, 2, axis)

    cond_float = condition.astype(f32)
    cond_act = jax.nn.silu(cond_float).astype(bf16)
    cond_pack = jnp.pad(cond_act.reshape(8, 1, part), ((0, 0), (0, 15), (0, 0)))
    mod_bias = jnp.pad(placed(modulation_bias, 6 * width).reshape(6, width), ((0, 2), (0, 0)))
    live_count = jnp.where(bucket[0] == 0, slot_count, slot_count - 16) // 2
    live = (jnp.arange(rows, dtype=jnp.int32) < live_count).astype(f32)
    qv = mine(placed(query_value_bias, 2 * width).reshape(2, 8, part), 1)
    qv = jnp.pad(qv.transpose(1, 0, 2), ((0, 0), (0, 0), (0, LANES_Q - part))).reshape(2, -1)
    tiled_b = placed(expand_bias, hid).reshape(hid // (4 * LANES), 4, LANES)
    tiled_b = lax.dynamic_index_in_dim(tiled_b, r, 1, keepdims=False)
    second_b = jnp.pad(tiled_b[slots_of:], ((1, 0), (0, 0)))
    expand_b = jnp.stack([tiled_b[:slots_of].reshape(-1), second_b.reshape(-1)])
    extra = jnp.stack(
        [
            jnp.broadcast_to(placed(output_bias, width), (2, width)),
            jnp.broadcast_to(placed(reduce_bias, width), (2, width)),
            jnp.pad(expand_b, ((0, 0), (0, width - wide))),
            jnp.pad(qv, ((0, 0), (0, width - 2 * LANES_Q))),
        ],
        axis=1,
    ).astype(bf16)
    extra = jnp.pad(extra, ((0, 0), (0, 12), (0, 0)))
    total = 8 * rows
    vmem = pltpu.VMEM
    dma = pltpu.SemaphoreType.DMA
    scratch = [
        vmem((8, 16, part), bf16),
        vmem((8, 16, width), bf16),
        vmem((8, 8, rows), f32),
        vmem((8, 8, width), f32),
        vmem((8, 8, width), f32),
        vmem((width, 3 * part), bf16),
        vmem((width, wide), bf16),
        vmem((wide, width), bf16),
        vmem((LANES_Q, width), bf16),
        vmem((2, part, 3 * part), bf16),
        vmem((2, part, wide), bf16),
        vmem((width, 3 * LANES_Q), bf16),
        vmem((3 * part, 3 * LANES_Q), bf16),
        vmem((total, width), bf16),
        vmem((total, width), bf16),
        vmem((total, width), bf16),
        vmem((total, width), bf16),
        vmem((total, 3 * LANES_Q), bf16),
        vmem((16, rows, rows), f32),
        vmem((total, LANES_Q), bf16),
        vmem((total, wide), bf16),
        vmem((total, wide), bf16),
        vmem((total, 3 * part), bf16),
        vmem((total, width), bf16),
        vmem((total, width), bf16),
    ]
    scratch += [vmem((4 * rows, width), bf16)] * 2
    scratch += [vmem((4, rows, width), bf16)] * 2
    scratch += [
        vmem((rows, width), f32),
        vmem((rows, 1), f32),
        vmem((rows, width), f32),
        vmem((rows, width), f32),
        vmem((rows, width), f32),
        vmem((rows, width), f32),
        vmem((rows, 1), f32),
        vmem((rows, width), f32),
        vmem((16, width), f32),
        vmem((8, 16, width), bf16),
        vmem((8, 8, part), f32),
        vmem((width, wide), bf16),
        vmem((wide, width), bf16),
        vmem((width, 3 * part), bf16),
        vmem((LANES_Q, width), bf16),
        vmem((3, 2 * part, wide), bf16),
        vmem((3, 3, LANES, width), bf16),
        vmem((3, 2 * part, 3 * part), bf16),
        vmem((3, part, width), bf16),
        vmem((8, part, 3 * part), bf16),
        dma((8,)),
        dma((8, 7)),
        dma((8, 8)),
        dma((3, 7)),
        dma((3, 8)),
        dma((4, 7)),
        dma((4, 8)),
        dma((4, 2)),
        dma((4, 2)),
        dma((4, 4)),
        dma((4, 4)),
        dma((3, 3)),
        dma((3, 3)),
        dma((7,)),
        dma((8,)),
        dma((9,)),
        dma((5,)),
        dma((hid // HALF // 4, 4)),
        dma((2 * slots_of,)),
        dma((2 * slots_of,)),
        dma((slots_of,)),
        dma((3, 3)),
        dma((2, slots_of)),
        dma((7, slots_of)),
        dma((hid // LANES,)),
        dma((slots_of,)),
        dma((2 * slots_of, 4)),
        dma((hid // HALF // 8,)),
        dma((2 * slots_of,)),
        dma((3, 2)),
        dma((2 * slots_of,)),
    ]
    in_vmem = pl.BlockSpec(memory_space=pltpu.VMEM)
    anywhere = pl.BlockSpec(memory_space=pl.ANY)
    outputs = pl.pallas_call(
        fused_kernel,
        out_shape=(
            jax.ShapeDtypeStruct((slot_count, width), bf16),
            jax.ShapeDtypeStruct((slot_count, width), bf16),
            jax.ShapeDtypeStruct((4, 8, 16, width), bf16),
            jax.ShapeDtypeStruct((4, 8, 16, part), bf16),
            jax.ShapeDtypeStruct((8, 8, part), f32),
            jax.ShapeDtypeStruct((part, hid), bf16),
            jax.ShapeDtypeStruct((hid // 8, width), bf16),
            jax.ShapeDtypeStruct((part, 3 * width), bf16),
            jax.ShapeDtypeStruct((part, width), bf16),
        ),
        in_specs=[in_vmem] * 10 + [anywhere] * 2 + [in_vmem],
        out_specs=(
            in_vmem,
            in_vmem,
            anywhere,
            anywhere,
            in_vmem,
            anywhere,
            anywhere,
            in_vmem,
            anywhere,
        ),
        scratch_shapes=scratch,
        compiler_params=pltpu.CompilerParams(
            collective_id=0, has_side_effects=True, vmem_limit_bytes=60 << 20
        ),
    )(
        latents[0],
        cotangent[0],
        keep_slots.reshape(rows, 1),
        live.reshape(rows, 1),
        jnp.broadcast_to(live[None], (8, rows)),
        cond_pack,
        mod_bias,
        extra,
        modulation_weight,
        projection_weight,
        expand_weight,
        reduce_weight,
        output_weight,
    )
    block, grad_latents, slabs, conds, g_cond, g_exp, g_red, g_proj, g_out = outputs

    def shard(value, axis, size):
        return lax.dynamic_slice_in_dim(value, f * size, size, axis)

    slabs = slabs.reshape(32, 16, width)
    grad_mod = slabs[:, :6].reshape(32, 6 * width)
    cond_cols = conds[:, :, 0].reshape(4, 4, 2, part).transpose(0, 2, 1, 3).reshape(32, part)
    sum_mod_w = jnp.einsum("bd,be->de", cond_cols, grad_mod, preferred_element_type=f32)
    sums = jnp.sum(slabs[:, :8].astype(f32), axis=0)
    sum_mod_b = shard(sums[:6].reshape(-1), 0, modulation_bias.shape[0])
    sum_red_b = shard(sums[6], 0, part)
    sum_out_b = shard(sums[7], 0, part)
    tails = jnp.sum(slabs[:, 8:10].astype(f32).reshape(4, 2, 4, 2, width), axis=2)
    exp_sums = tails[:, :, 0, :wide].reshape(4, 2, slots_of, LANES)
    exp_sums = jnp.concatenate([exp_sums[:, 0], exp_sums[:, 1, 1:]], axis=1)
    sum_exp_b = shard(exp_sums.transpose(1, 0, 2).reshape(-1), 0, expand_bias.shape[0])
    qv_sums = tails[:, :, 1, : 3 * part].reshape(8, 3, part)
    qv_sums = jnp.concatenate([qv_sums[:, 0].reshape(-1), qv_sums[:, 2].reshape(-1)])
    sum_qv_b = shard(qv_sums, 0, query_value_bias.shape[0])
    grad_condition = jax.vjp(jax.nn.silu, cond_float)[1](g_cond[:, 0].reshape(1, width))[0]
    return (
        block[None],
        grad_latents[None],
        grad_condition,
        sum_mod_w,
        sum_mod_b,
        g_proj.astype(f32),
        sum_qv_b,
        g_out.astype(f32),
        sum_out_b,
        g_exp.astype(f32),
        sum_exp_b,
        g_red.astype(f32),
        sum_red_b,
    )


def solution(mesh):
    placed = (
        P(("replica", "fsdp"), None, None),
        P(("replica", "fsdp"), None),
        P(("replica", "fsdp")),
        P(("replica", "fsdp"), None),
        P("fsdp", None),
        P("fsdp"),
        P("fsdp", None),
        P("fsdp"),
        P("fsdp", None),
        P("fsdp"),
        P("fsdp", None),
        P("fsdp"),
        P("fsdp", None),
        P("fsdp"),
        P(("replica", "fsdp"), None, None),
    )
    body = fused_local if tuple(mesh.shape.values()) == (4, 8) else local
    return jax.shard_map(
        body,
        mesh=mesh,
        in_specs=placed,
        out_specs=(
            P(("replica", "fsdp"), None, None),
            P(("replica", "fsdp"), None, None),
            P(("replica", "fsdp"), None),
            P("fsdp", None),
            P("fsdp"),
            P("fsdp", None),
            P("fsdp"),
            P("fsdp", None),
            P("fsdp"),
            P("fsdp", None),
            P("fsdp"),
            P("fsdp", None),
            P("fsdp"),
        ),
        check_vma=False,
    )
```

```python
import jax
import jax.numpy as jnp
from jax import lax
from jax.experimental import pallas as pl
from jax.experimental.pallas import tpu as pltpu
from jax.sharding import PartitionSpec as P

HEADS = 16
HEAD_DIM = 72


def layer_norm(rows_in):
    row_mean = jnp.mean(rows_in, axis=-1, keepdims=True)
    centred = rows_in - row_mean
    row_var = jnp.mean(centred * centred, axis=-1, keepdims=True)
    return centred * lax.rsqrt(row_var + 1e-06)


def modulate(rows_in, shift_part, scale_part):
    return layer_norm(rows_in) * (1.0 + scale_part) + shift_part


def gelu_tanh(values_in):
    return jax.nn.gelu(values_in, approximate=True)


def place_rows(target_rows, target_index, new_rows):
    return target_rows.at[target_index].set(new_rows, mode="drop")


def column_sums(rows_in):
    return jnp.sum(rows_in.astype(jnp.float32), axis=0)


def local(
    latents,
    condition,
    bucket,
    keep_slots,
    modulation_weight,
    modulation_bias,
    projection_weight,
    query_value_bias,
    output_weight,
    output_bias,
    expand_weight,
    expand_bias,
    reduce_weight,
    reduce_bias,
    cotangent,
):
    f32 = jnp.float32
    bf16 = jnp.bfloat16
    images, slot_count, model_width = latents.shape
    kept_rows = keep_slots.shape[1]
    row_count = images * kept_rows
    score_scale = HEAD_DIM ** (-0.5)
    shape_heads = (images, kept_rows, HEADS, HEAD_DIM)
    (
        full_mod_w,
        full_mod_b,
        full_proj_w,
        full_qv_b,
        full_out_w,
        full_out_b,
        full_exp_w,
        full_exp_b,
        full_red_w,
        full_red_b,
    ) = (
        lax.all_gather(modulation_weight, "fsdp", axis=0, tiled=True),
        lax.all_gather(modulation_bias, "fsdp", axis=0, tiled=True),
        lax.all_gather(projection_weight, "fsdp", axis=0, tiled=True),
        lax.all_gather(query_value_bias, "fsdp", axis=0, tiled=True),
        lax.all_gather(output_weight, "fsdp", axis=0, tiled=True),
        lax.all_gather(output_bias, "fsdp", axis=0, tiled=True),
        lax.all_gather(expand_weight, "fsdp", axis=0, tiled=True),
        lax.all_gather(expand_bias, "fsdp", axis=0, tiled=True),
        lax.all_gather(reduce_weight, "fsdp", axis=0, tiled=True),
        lax.all_gather(reduce_bias, "fsdp", axis=0, tiled=True),
    )
    live_count = jnp.where(bucket == 0, slot_count, slot_count - 16) // 2
    live_rows = jnp.arange(kept_rows, dtype=jnp.int32)[None, :] < live_count[:, None]
    live_float = live_rows.astype(f32)[:, :, None]
    gather_index = keep_slots[:, :, None]
    kept = jnp.take_along_axis(latents, gather_index, axis=1).astype(f32)
    cond_float = condition.astype(f32)
    cond_act = jax.nn.silu(cond_float).astype(bf16)
    modulation = jnp.dot(cond_act, full_mod_w, preferred_element_type=f32) + full_mod_b.astype(f32)
    pieces = [modulation[:, None, i * model_width : (i + 1) * model_width] for i in range(6)]
    shift_attn, scale_attn, gate_attn, shift_mlp, scale_mlp, gate_mlp = pieces
    normed_one = modulate(kept, shift_attn, scale_attn).astype(bf16).reshape(row_count, model_width)
    projected = jnp.dot(normed_one, full_proj_w, preferred_element_type=f32)
    bias_qv = full_qv_b.astype(f32)
    query_rows = (
        (projected[:, :model_width] + bias_qv[:model_width]).astype(bf16).reshape(shape_heads)
    )
    key_rows = projected[:, model_width : 2 * model_width].astype(bf16).reshape(shape_heads)
    value_rows = (
        (projected[:, 2 * model_width :] + bias_qv[model_width:]).astype(bf16).reshape(shape_heads)
    )

    def masked_scores(queries, keys_in):
        raw = (
            jnp.einsum("bqhd,bkhd->bhqk", queries, keys_in, preferred_element_type=f32)
            * score_scale
        )
        return jnp.where(live_rows[:, None, None, :], raw, -1e30)

    scores = masked_scores(query_rows, key_rows)
    row_max = jnp.max(scores, axis=-1, keepdims=True)
    row_total = jnp.sum(jnp.exp(scores - row_max), axis=-1, keepdims=True)
    log_total = row_max + jnp.log(row_total)
    probs = jnp.exp(scores - log_total)
    attended = (
        jnp.einsum("bhqk,bkhd->bqhd", probs.astype(bf16), value_rows, preferred_element_type=f32)
        .astype(bf16)
        .reshape(row_count, model_width)
    )
    branch_attn = (
        jnp.dot(attended, full_out_w, preferred_element_type=f32) + full_out_b.astype(f32)
    ).reshape(images, kept_rows, model_width)
    mixed = kept + gate_attn * branch_attn
    normed_two = modulate(mixed, shift_mlp, scale_mlp).astype(bf16).reshape(row_count, model_width)
    hidden = jnp.dot(normed_two, full_exp_w, preferred_element_type=f32) + full_exp_b.astype(f32)
    activation = gelu_tanh(hidden).astype(bf16)
    branch_mlp = (
        jnp.dot(activation, full_red_w, preferred_element_type=f32) + full_red_b.astype(f32)
    ).reshape(images, kept_rows, model_width)
    result = mixed + gate_mlp * branch_mlp
    target = jnp.where(live_rows, keep_slots, slot_count)
    block_out = jax.vmap(place_rows)(latents, target, result.astype(bf16))
    back_mod_w, back_proj_w, back_out_w, back_exp_w, back_red_w = (
        lax.all_gather(modulation_weight, "fsdp", axis=0, tiled=True),
        lax.all_gather(projection_weight, "fsdp", axis=0, tiled=True),
        lax.all_gather(output_weight, "fsdp", axis=0, tiled=True),
        lax.all_gather(expand_weight, "fsdp", axis=0, tiled=True),
        lax.all_gather(reduce_weight, "fsdp", axis=0, tiled=True),
    )
    grad_rows = jnp.take_along_axis(cotangent, gather_index, axis=1).astype(f32) * live_float
    grad_gate_mlp = jnp.sum(grad_rows * branch_mlp, axis=1)
    grad_mlp = (gate_mlp * grad_rows).astype(bf16).reshape(row_count, model_width)
    local_red_w = jnp.einsum("rm,rd->md", activation, grad_mlp, preferred_element_type=f32)
    local_red_b = column_sums(grad_mlp)
    grad_act = jnp.einsum("rd,md->rm", grad_mlp, back_red_w, preferred_element_type=f32)
    gelu_pull = jax.vjp(gelu_tanh, hidden)[1]
    grad_hidden = gelu_pull(grad_act)[0].astype(bf16)
    local_exp_w = jnp.einsum("rd,rm->dm", normed_two, grad_hidden, preferred_element_type=f32)
    local_exp_b = column_sums(grad_hidden)
    mlp_red_w, mlp_red_b, mlp_exp_w, mlp_exp_b = (
        lax.psum_scatter(
            local_red_w.astype(jnp.bfloat16), "fsdp", scatter_dimension=0, tiled=True
        ).astype(jnp.float32),
        lax.psum_scatter(
            local_red_b.astype(jnp.bfloat16), "fsdp", scatter_dimension=0, tiled=True
        ).astype(jnp.float32),
        lax.psum_scatter(
            local_exp_w.astype(jnp.bfloat16), "fsdp", scatter_dimension=0, tiled=True
        ).astype(jnp.float32),
        lax.psum_scatter(
            local_exp_b.astype(jnp.bfloat16), "fsdp", scatter_dimension=0, tiled=True
        ).astype(jnp.float32),
    )
    grad_normed_two = jnp.einsum(
        "rm,dm->rd", grad_hidden, back_exp_w, preferred_element_type=f32
    ).reshape(images, kept_rows, model_width)
    pull_two = jax.vjp(modulate, mixed, shift_mlp, scale_mlp)[1]
    grad_mixed_ln, grad_shift_mlp, grad_scale_mlp = pull_two(grad_normed_two)
    grad_mixed = grad_rows + grad_mixed_ln
    grad_gate_attn = jnp.sum(grad_mixed * branch_attn, axis=1)
    grad_attn = (gate_attn * grad_mixed).astype(bf16).reshape(row_count, model_width)
    local_out_w = jnp.einsum("rd,re->de", attended, grad_attn, preferred_element_type=f32)
    local_out_b = column_sums(grad_attn)
    grad_attended = (
        jnp.einsum("re,de->rd", grad_attn, back_out_w, preferred_element_type=f32)
        .astype(bf16)
        .reshape(shape_heads)
    )
    scores_again = masked_scores(query_rows, key_rows)
    probs_again = jnp.exp(scores_again - log_total)
    grad_values = jnp.einsum(
        "bhqk,bqhd->bkhd", probs_again.astype(bf16), grad_attended, preferred_element_type=f32
    ).astype(bf16)
    grad_probs = jnp.einsum(
        "bqhd,bkhd->bhqk", grad_attended, value_rows, preferred_element_type=f32
    )
    row_inner = jnp.sum(grad_probs * probs_again, axis=-1, keepdims=True)
    grad_scores = (probs_again * (grad_probs - row_inner)).astype(bf16)
    grad_query = (
        jnp.einsum("bhqk,bkhd->bqhd", grad_scores, key_rows, preferred_element_type=f32)
        * score_scale
    ).astype(bf16)
    grad_keys = (
        jnp.einsum("bhqk,bqhd->bkhd", grad_scores, query_rows, preferred_element_type=f32)
        * score_scale
    ).astype(bf16)
    grad_projected = jnp.concatenate(
        [
            grad_query.reshape(row_count, model_width),
            grad_keys.reshape(row_count, model_width),
            grad_values.reshape(row_count, model_width),
        ],
        axis=1,
    )
    local_proj_w = jnp.einsum("rd,re->de", normed_one, grad_projected, preferred_element_type=f32)
    local_qv_b = jnp.concatenate(
        [
            column_sums(grad_projected[:, :model_width]),
            column_sums(grad_projected[:, 2 * model_width :]),
        ]
    )
    grad_normed_one = jnp.einsum(
        "re,de->rd", grad_projected, back_proj_w, preferred_element_type=f32
    ).reshape(images, kept_rows, model_width)
    pull_one = jax.vjp(modulate, kept, shift_attn, scale_attn)[1]
    grad_kept_ln, grad_shift_attn, grad_scale_attn = pull_one(grad_normed_one)
    grad_kept = grad_mixed + grad_kept_ln
    grad_latents = jax.vmap(place_rows)(cotangent, target, grad_kept.astype(bf16))
    grad_modulation = jnp.concatenate(
        [
            grad_shift_attn[:, 0],
            grad_scale_attn[:, 0],
            grad_gate_attn,
            grad_shift_mlp[:, 0],
            grad_scale_mlp[:, 0],
            grad_gate_mlp,
        ],
        axis=1,
    ).astype(bf16)
    grad_cond_act = jnp.einsum("be,de->bd", grad_modulation, back_mod_w, preferred_element_type=f32)
    silu_pull = jax.vjp(jax.nn.silu, cond_float)[1]
    grad_condition = silu_pull(grad_cond_act)[0]
    local_mod_w = jnp.einsum("bd,be->de", cond_act, grad_modulation, preferred_element_type=f32)
    local_mod_b = column_sums(grad_modulation)
    rest_mod_w, rest_mod_b, rest_proj_w, rest_qv_b, rest_out_w, rest_out_b = (
        lax.psum_scatter(
            local_mod_w.astype(jnp.bfloat16), "fsdp", scatter_dimension=0, tiled=True
        ).astype(jnp.float32),
        lax.psum_scatter(
            local_mod_b.astype(jnp.bfloat16), "fsdp", scatter_dimension=0, tiled=True
        ).astype(jnp.float32),
        lax.psum_scatter(
            local_proj_w.astype(jnp.bfloat16), "fsdp", scatter_dimension=0, tiled=True
        ).astype(jnp.float32),
        lax.psum_scatter(
            local_qv_b.astype(jnp.bfloat16), "fsdp", scatter_dimension=0, tiled=True
        ).astype(jnp.float32),
        lax.psum_scatter(
            local_out_w.astype(jnp.bfloat16), "fsdp", scatter_dimension=0, tiled=True
        ).astype(jnp.float32),
        lax.psum_scatter(
            local_out_b.astype(jnp.bfloat16), "fsdp", scatter_dimension=0, tiled=True
        ).astype(jnp.float32),
    )
    shares = (
        lax.psum_scatter(
            rest_mod_w.astype(jnp.bfloat16), "replica", scatter_dimension=1, tiled=True
        ).astype(jnp.float32),
        lax.psum_scatter(
            rest_proj_w.astype(jnp.bfloat16), "replica", scatter_dimension=1, tiled=True
        ).astype(jnp.float32),
        lax.psum_scatter(
            rest_out_w.astype(jnp.bfloat16), "replica", scatter_dimension=1, tiled=True
        ).astype(jnp.float32),
        lax.psum_scatter(
            mlp_exp_w.astype(jnp.bfloat16), "replica", scatter_dimension=1, tiled=True
        ).astype(jnp.float32),
        lax.psum_scatter(
            mlp_red_w.astype(jnp.bfloat16), "replica", scatter_dimension=1, tiled=True
        ).astype(jnp.float32),
    )
    sum_mod_w, sum_proj_w, sum_out_w, sum_exp_w, sum_red_w = (
        lax.all_gather(shares[0].astype(jnp.bfloat16), "replica", axis=1, tiled=True).astype(
            jnp.float32
        ),
        lax.all_gather(shares[1].astype(jnp.bfloat16), "replica", axis=1, tiled=True).astype(
            jnp.float32
        ),
        lax.all_gather(shares[2].astype(jnp.bfloat16), "replica", axis=1, tiled=True).astype(
            jnp.float32
        ),
        lax.all_gather(shares[3].astype(jnp.bfloat16), "replica", axis=1, tiled=True).astype(
            jnp.float32
        ),
        lax.all_gather(shares[4].astype(jnp.bfloat16), "replica", axis=1, tiled=True).astype(
            jnp.float32
        ),
    )
    sum_mod_b, sum_qv_b, sum_out_b, sum_exp_b, sum_red_b = lax.psum(
        (rest_mod_b, rest_qv_b, rest_out_b, mlp_exp_b, mlp_red_b), "replica"
    )
    return (
        block_out,
        grad_latents,
        grad_condition,
        sum_mod_w,
        sum_mod_b,
        sum_proj_w,
        sum_qv_b,
        sum_out_w,
        sum_out_b,
        sum_exp_w,
        sum_exp_b,
        sum_red_w,
        sum_red_b,
    )


MESH = pl.DeviceIdType.MESH
SAME_CORE = ((1, 0), (0, 1), (1, 1))
LANES = 128
HALF = 64
LANES_Q = 256


def fused_kernel(
    latents,
    cotangent,
    slots,
    live_row,
    cond_pack,
    mod_bias,
    extra,
    mod_w,
    proj_w,
    exp_w,
    red_w,
    out_shard,
    o_block,
    o_latents,
    o_slabs,
    o_cond,
    o_gcond,
    o_exp,
    o_red,
    o_proj,
    o_out,
    cond_all,
    extra_all,
    live_all,
    mod_send,
    mod_all,
    proj_all,
    exp_all,
    red_all,
    out_w,
    proj_pack,
    exp_pack,
    proj_wide,
    spread,
    x_one,
    x_two,
    g_mlp,
    g_attn,
    qkv,
    probs,
    attended,
    g_hid,
    d_qkv,
    part_a,
    part_b,
    sib_a,
    sib_b,
    rows_a,
    rows_b,
    norm_one,
    rstd_one,
    g_rows,
    branch_a,
    mixed,
    norm_two,
    rstd_two,
    g_mixed,
    slab,
    slabs,
    gcond,
    d_exp,
    d_red,
    d_proj,
    d_out,
    z_exp,
    z_red,
    z_proj,
    z_out,
    proj_land,
    local_sem,
    small_s,
    small_r,
    w_s,
    w_r,
    ag_s,
    ag_r,
    sb_s,
    sb_r,
    rs_s,
    rs_r,
    dz_s,
    dz_r,
    dp_s,
    dp_r,
    ow_s,
    ow_r,
    red_s,
    red_r,
    red_l,
    zr_s,
    zr_r,
    pe_s,
    et_s,
    et_r,
    et_l,
    pr_s,
    pr_r,
    pr_l,
    relay_s,
    red_f,
):
    f32 = jnp.float32
    bf16 = jnp.bfloat16
    r = lax.axis_index("replica")
    f = lax.axis_index("fsdp")
    x, y, c, z = r % 2, r // 2, f % 2, f // 2
    width = latents.shape[1]
    rows = slots.shape[1]
    part = out_shard.shape[0]
    third = width // 3
    kept = g_mixed
    total_rows = x_one.shape[0]
    hid_lanes = pl.ds(0, red_all.shape[0])
    blocks = red_w.shape[0] // HALF
    slots_of = red_all.shape[0] // LANES
    tiles = exp_w.shape[1] // LANES
    me = 4 * c + r
    other = (c + 1) % 2

    def ident(r2, f2):
        return {"replica": r2, "fsdp": f2}

    def remote(src, dst, s_sem, r_sem, dev):
        return pltpu.make_async_remote_copy(
            src_ref=src,
            dst_ref=dst,
            send_sem=s_sem,
            recv_sem=r_sem,
            device_id=dev,
            device_id_type=MESH,
        )

    def plane(dx, dy):
        return ((y + dy) % 2) * 2 + (x + dx) % 2

    sibling = ident(r, 2 * z + other)
    line = []
    across = (z, z + 1 - 2 * (z % 2), (z + 2) % 4, 3 - z)
    for dz in (2, 1, 3, 0):
        for dc in range(2):
            if dz or dc:
                line.append((across[dz], (c + dc) % 2))
    far = (4, 5)
    via = (0, 1)
    outer = (z == 0) | (z == 3)
    inner = (z == 1) | (z == 2)
    board = []
    for dx in range(2):
        for dy in range(2):
            for dc in range(2):
                if dx or dy or dc:
                    board.append((plane(dx, dy), (c + dc) % 2))

    barrier = pltpu.get_barrier_semaphore()
    for z2, c2 in line:
        pl.semaphore_signal(barrier, inc=1, device_id=ident(r, 2 * z2 + c2), device_id_type=MESH)
    for r2, c2 in board:
        pl.semaphore_signal(barrier, inc=1, device_id=ident(r2, 2 * z + c2), device_id_type=MESH)
    pl.semaphore_wait(barrier, len(line) + len(board))

    def line_copy(kind, k, sems_s, sems_r, src_of, dst_of):
        z2, c2 = line[k]
        f2 = 2 * z2 + c2
        return remote(
            src_of(f2, c2), dst_of(f), sems_s.at[kind, k], sems_r.at[kind, f], ident(r, f2)
        )

    def line_from(kind, k, sems_s, sems_r, src_of, dst_of):
        z2, c2 = line[k]
        f2 = 2 * z2 + c2
        return remote(
            src_of(f, c), dst_of(f2), sems_s.at[kind, k], sems_r.at[kind, f2], ident(r, f2)
        )

    def line_send(*what):
        copies = [line_copy(what[0], k, *what[1:]) for k in range(len(line))]
        for cp in copies:
            cp.start()
        return copies

    def line_wait(*what):
        for k in range(len(line)):
            line_from(what[0], k, *what[1:]).wait_recv()

    def relay_send(*what):
        for k in range(len(line)):
            cp = line_copy(what[0], k, *what[1:])
            if k in far:
                pl.when(inner)(cp.start)
            else:
                cp.start()

    def relay_copy(k, kind, sems_s, sems_r, src_of, dst_of):
        z2, c2 = line[k]
        f2 = 2 * z2 + c2
        return remote(
            dst_of(f2),
            dst_of(f2),
            relay_s.at[kind, k],
            sems_r.at[kind, f2],
            ident(r, 2 * across[1] + c),
        )

    def relay_pass(*what):
        @pl.when(outer)
        def _():
            for k in via:
                line_from(what[0], k, *what[1:]).wait_recv()

        @pl.when(inner)
        def _():
            for k in via:
                line_from(what[0], k, *what[1:]).wait_recv()
                relay_copy(k, *what).start()

    def relay_wait(*what):
        for k in range(len(line)):
            if k not in via:
                line_from(what[0], k, *what[1:]).wait_recv()

    def relay_drain(*what):
        for k in range(len(line)):
            cp = line_copy(what[0], k, *what[1:])
            if k in far:
                pl.when(inner)(cp.wait_send)
            else:
                cp.wait_send()

        @pl.when(inner)
        def _():
            for k in via:
                relay_copy(k, *what).wait_send()

    def drain(copies):
        for cp in copies:
            cp.wait_send()

    def cond_src(f2, c2):
        return cond_pack.at[f2]

    def cond_dst(f2):
        return cond_all.at[f2]

    def extra_src(f2, c2):
        return extra.at[c2]

    def extra_dst(f2):
        return extra_all.at[f2]

    def proj_src(f2, c2):
        return proj_pack.at[c2]

    def proj_dst(f2):
        return proj_all.at[pl.ds(pl.multiple_of(f2 * part, 16), part)]

    tail = pl.ds(LANES, exp_all.shape[1] - LANES)
    head = pl.ds(0, LANES)

    def exp_src(f2, c2):
        return exp_pack.at[c2, :, tail]

    def exp_dst(f2):
        return exp_all.at[pl.ds(pl.multiple_of(f2 * part, 16), part), tail]

    def exp_head(f2):
        return exp_all.at[pl.ds(pl.multiple_of(f2 * part, 16), part), head]

    def half_tile(i):
        p = i // 2
        c2 = p // slots_of
        at = 2 * (r + 4 * p) + i % 2
        return c2, 2 * (p - 4 * c2) + i % 2, at // blocks, at % blocks

    def red_rows(j):
        return red_all.at[pl.ds(pl.multiple_of(j * HALF, HALF), HALF)]

    def red_copy(i, z2):
        c2, j, owner, block = half_tile(i)
        return remote(
            red_w.at[pl.ds(pl.multiple_of(block * HALF, HALF), HALF)],
            red_rows(j),
            red_s.at[i, z2],
            red_r.at[j],
            ident(r, 2 * z2 + c2),
        )

    def red_local(i):
        c2, j, owner, block = half_tile(i)
        return pltpu.make_async_copy(
            red_w.at[pl.ds(pl.multiple_of(block * HALF, HALF), HALF)], red_rows(j), red_l.at[j]
        )

    def red_goes(i, z2):
        c2, j, owner, block = half_tile(i)
        return (owner == f) & (2 * z2 + c2 != f) & (inner | (z2 + z != 3))

    def red_stops(i):
        c2, j, owner, block = half_tile(i)
        return (c2 == c) & (owner // 2 == across[2])

    def red_onward(i):
        c2, j, owner, block = half_tile(i)
        return remote(
            red_rows(j), red_rows(j), red_f.at[j], red_r.at[j], ident(r, 2 * across[1] + c)
        )

    def each_half(step):
        def body(i, carry):
            step(i)
            return carry

        lax.fori_loop(0, 2 * blocks, body, 0)

    def red_send():
        def step(i):
            c2, j, owner, block = half_tile(i)
            for z2 in range(4):
                pl.when(red_goes(i, z2))(red_copy(i, z2).start)
            pl.when((owner == f) & (c2 == c))(red_local(i).start)

        each_half(step)

    def red_pass():
        def step(i):
            @pl.when(red_stops(i))
            def _():
                red_copy(i, z).wait_recv()
                pl.when(inner)(red_onward(i).start)

        each_half(step)

    def red_wait():
        def step(i):
            c2, j, owner, block = half_tile(i)
            pl.when((c2 == c) & (owner != f) & (owner // 2 != across[2]))(red_copy(i, z).wait_recv)
            pl.when((owner == f) & (c2 == c))(red_local(i).wait)

        each_half(step)

    def red_drain():
        def step(i):
            for z2 in range(4):
                pl.when(red_goes(i, z2))(red_copy(i, z2).wait_send)
            pl.when(red_stops(i) & inner)(red_onward(i).wait_send)

        each_half(step)

    exp_main = (1, w_s, w_r, exp_src, exp_dst)
    proj_main = (0, w_s, w_r, proj_src, proj_dst)

    def first_src(f2, c2):
        return exp_pack.at[0, :, head]

    exp_lead = (2, w_s, w_r, first_src, exp_head)

    def lead_send(start):
        for k, (z2, c2) in enumerate(line):
            keep = c2 == 0
            if k in far:
                keep = keep & inner
            cp = line_copy(exp_lead[0], k, *exp_lead[1:])
            pl.when(keep)(cp.start if start else cp.wait_send)

    def exp_send():
        relay_send(*exp_main)
        lead_send(True)

    def exp_pass():
        relay_pass(*exp_main)

        @pl.when(c == 0)
        def _():
            relay_pass(*exp_lead)

    def exp_wait():
        relay_wait(*exp_main)

        @pl.when(c == 0)
        def _():
            relay_wait(*exp_lead)

    def exp_drain():
        relay_drain(*exp_main)
        lead_send(False)

        @pl.when((c == 0) & inner)
        def _():
            for k in via:
                relay_copy(k, *exp_lead).wait_send()

    sent = line_send(0, small_s, small_r, cond_src, cond_dst)
    packs = []
    for c2 in range(2):
        for i in range(slots_of):
            if c2 and not i:
                continue
            tile = r + 4 * (4 * c2 + i)
            cp = pltpu.make_async_copy(
                exp_w.at[:, pl.ds(pl.multiple_of(tile * LANES, LANES), LANES)],
                exp_pack.at[c2, :, pl.ds(i * LANES, LANES)],
                pe_s.at[c2, i],
            )
            cp.start()
            packs.append(cp)
    live_sent = []
    for k, (r2, c2) in enumerate(board):
        cp = remote(
            live_row,
            live_all.at[me],
            small_s.at[3, k],
            small_r.at[3, me],
            ident(r2, 2 * z + c2),
        )
        cp.start()
        live_sent.append(cp)
    local = [
        pltpu.make_async_copy(cond_pack.at[f], cond_all.at[f], local_sem.at[0]),
        pltpu.make_async_copy(extra.at[c], extra_all.at[f], local_sem.at[1]),
        pltpu.make_async_copy(live_row, live_all.at[me], local_sem.at[5]),
    ]
    for cp in local:
        cp.start()

    def one_hot():
        ids = lax.broadcasted_iota(jnp.int32, (latents.shape[0], rows), 0)
        return jnp.where(ids == slots[...], 1.0, 0.0)

    def dot(a, b):
        return jnp.dot(a, b, preferred_element_type=f32)

    def dot_t(a, b):
        return lax.dot_general(a, b, (((1,), (1,)), ((), ())), preferred_element_type=f32)

    def t_dot(a, b):
        return lax.dot_general(a, b, (((0,), (0,)), ((), ())), preferred_element_type=f32)

    wide_columns = proj_all.shape[1]
    for c2 in range(2):
        t = 2 * r + c2
        picked = jnp.zeros((part, wide_columns), f32)
        for q in range(3):
            window = proj_w[
                :, pl.ds(pl.multiple_of(q * width + t * LANES, LANES), LANES_Q)
            ]
            source = lax.broadcasted_iota(jnp.int32, (LANES_Q, wide_columns), 0)
            goal = lax.broadcasted_iota(jnp.int32, (LANES_Q, wide_columns), 1)
            picks = (source - t * (part - LANES) == goal - q * part) & (
                (goal >= q * part) & (goal < (q + 1) * part)
            )
            picked += dot(window, jnp.where(picks, 1.0, 0.0).astype(bf16))
        proj_pack[c2] = picked.astype(bf16)
    local[0].wait()
    line_wait(0, small_s, small_r, cond_src, cond_dst)
    cond_cols = jnp.sum(cond_all[...].astype(f32), axis=1).astype(bf16)
    mod_send[...] = jnp.zeros(mod_send.shape, f32)
    for p in range(6):
        piece = dot(cond_cols, mod_w[:, p * width : (p + 1) * width]) + mod_bias[p : p + 1, :]
        mod_send[:, p, :] = piece

    def mod_src(f2, c2):
        return mod_send.at[f2]

    def mod_dst(f2):
        return mod_all.at[f2]

    sent += line_send(2, small_s, small_r, mod_src, mod_dst)
    mod_all[f] = mod_send[f]

    relay_send(0, w_s, w_r, proj_src, proj_dst)
    sent += line_send(1, small_s, small_r, extra_src, extra_dst)
    own_proj = pltpu.make_async_copy(proj_pack.at[c], proj_dst(f), local_sem.at[2])
    own_proj.start()
    local.append(own_proj)

    kept[...] = t_dot(one_hot().astype(bf16), latents[...])
    g_rows[...] = t_dot((one_hot() * live_row[0:1, :]).astype(bf16), cotangent[...])

    def normalise(values, norm_ref, rstd_ref):
        centred = values - jnp.mean(values, axis=-1, keepdims=True)
        rstd = lax.rsqrt(jnp.mean(centred * centred, axis=-1, keepdims=True) + 1e-06)
        norm_ref[...] = centred * rstd
        rstd_ref[...] = rstd

    normalise(kept[...], norm_one, rstd_one)
    out_w[part:, :] = jnp.zeros((out_w.shape[0] - part, width), bf16)
    split = lax.broadcasted_iota(jnp.int32, spread.shape, 0)
    column = lax.broadcasted_iota(jnp.int32, spread.shape, 1)
    skip = jnp.where(split >= part, LANES_Q - part, 0) + jnp.where(
        split >= 2 * part, LANES_Q - part, 0
    )
    spread[...] = jnp.where(column == split + skip, 1.0, 0.0).astype(bf16)

    @pl.when(c == 1)
    def _():
        exp_all[:, :LANES] = jnp.zeros((width, LANES), bf16)
        red_all[:LANES, :] = jnp.zeros((LANES, width), bf16)

    for cp in local[1:]:
        cp.wait()

    line_wait(2, small_s, small_r, mod_src, mod_dst)
    modulation = jnp.sum(mod_all[...], axis=0)
    shift_attn, scale_attn, gate_attn, shift_mlp, scale_mlp, gate_mlp = [
        modulation[p : p + 1, :] for p in range(6)
    ]

    def own(ref):
        return ref.at[pl.ds(pl.multiple_of(me * rows, rows), rows)]

    def slot(ref, u):
        return ref.at[pl.ds(pl.multiple_of(u * rows, rows), rows)]

    def gather_start(kind, buf):
        copies = [
            remote(own(buf), own(buf), ag_s.at[kind, 0], ag_r.at[kind, me], sibling),
        ]
        for k, (dx, dy) in enumerate(SAME_CORE):
            copies.append(
                remote(
                    own(buf),
                    own(buf),
                    ag_s.at[kind, 1 + k],
                    ag_r.at[kind, me],
                    ident(plane(dx, dy), f),
                )
            )
        for cp in copies:
            cp.start()

    def gather_pass(kind, buf, k):
        u = 4 * c + plane(*SAME_CORE[k])
        cp = remote(slot(buf, u), slot(buf, u), ag_s.at[kind, 4 + k], ag_r.at[kind, u], sibling)
        cp.wait_recv()
        cp.start()

    def gather_take(kind, buf, r2):
        u = 4 * other + r2
        remote(slot(buf, u), slot(buf, u), ag_s.at[kind, 0], ag_r.at[kind, u], sibling).wait_recv()

    def gather_near(kind, buf):
        gather_pass(kind, buf, 0)
        gather_pass(kind, buf, 1)
        gather_take(kind, buf, r)
        gather_take(kind, buf, plane(1, 0))

    def gather_far(kind, buf):
        gather_pass(kind, buf, 2)
        gather_take(kind, buf, plane(0, 1))
        gather_take(kind, buf, plane(1, 1))

    def gather_drain(kind, buf):
        for k in range(7):
            remote(
                own(buf), own(buf), ag_s.at[kind, k], ag_r.at[kind, me], sibling
            ).wait_send()

    def reduce_send(kind, buf, landing, r2):
        remote(
            slot(buf, 4 * c + r2),
            landing.at[r],
            rs_s.at[kind, r2],
            rs_r.at[kind, r],
            ident(r2, f),
        ).start()

    def chunk_of(k):
        cc, pair = (c + 1 + k) % 2, (y + k // 2) % 2
        first = 4 * cc + 2 * pair
        return first, pair, pl.ds(pl.multiple_of(first * rows, 2 * rows), 2 * rows)

    def reduce_chunk(kind, k, values, buf, sib, landing, hold=False):
        first, pair, here = chunk_of(k)
        there = pl.ds(pl.multiple_of(pair * 2 * rows, 2 * rows), 2 * rows)
        hop = remote(
            buf.at[here], sib.at[there], sb_s.at[kind, pair], sb_r.at[kind, pair], sibling
        )

        @pl.when(k % 2 == 0)
        def _():
            buf[here, :] = values.astype(bf16)
            hop.start()

        @pl.when(k % 2 == 1)
        def _():
            hop.wait_recv()
            buf[here, :] = (values + sib[there, :].astype(f32)).astype(bf16)
            for x2 in range(0 if hold else 2):
                r2 = 2 * pair + x2

                @pl.when(r2 != r)
                def _():
                    reduce_send(kind, buf, landing, r2)

    def reduce_end(kind, buf, landing):
        total = own(buf)[...].astype(f32)
        for dx, dy in SAME_CORE:
            r2 = plane(dx, dy)
            remote(
                own(buf), landing.at[r2], rs_s.at[kind, r2], rs_r.at[kind, r2], ident(r2, f)
            ).wait_recv()
            total += landing[r2].astype(f32)
        return total

    def reduce_drain(kind, buf, sib, landing):
        for k in range(2):
            there = pl.ds(k * 2 * rows, 2 * rows)
            remote(
                sib.at[there], sib.at[there], sb_s.at[kind, k], sb_r.at[kind, k], sibling
            ).wait_send()
        for dx, dy in SAME_CORE:
            r2 = plane(dx, dy)
            remote(
                own(buf), landing.at[r2], rs_s.at[kind, r2], rs_r.at[kind, r2], ident(r2, f)
            ).wait_send()

    own(x_one)[...] = (norm_one[...] * (1.0 + scale_attn) + shift_attn).astype(bf16)
    gather_start(0, x_one)
    grad_mlp = (gate_mlp * g_rows[...]).astype(bf16)
    own(g_mlp)[...] = grad_mlp
    gather_start(1, g_mlp)
    slab[...] = jnp.zeros(slab.shape, f32)
    slab[6:7, :] = jnp.sum(grad_mlp.astype(f32), axis=0, keepdims=True)

    def out_copy(z2):
        return remote(
            out_shard,
            out_w.at[pl.ds(0, part)],
            ow_s.at[z2],
            ow_r.at[0],
            ident(r, 2 * z2 + c),
        )

    def out_onward():
        return remote(
            out_w.at[pl.ds(0, part)],
            out_w.at[pl.ds(0, part)],
            ow_s.at[7],
            ow_r.at[0],
            ident(r, 2 * across[1] + c),
        )

    def out_goes(z2):
        return (z == r) & (z2 != z) & (inner | (z2 + z != 3))


    @pl.when(z == r)
    def _():
        out_w[:part, :] = out_shard[...]

    relay_pass(*proj_main)
    for z2 in range(4):
        pl.when(out_goes(z2))(out_copy(z2).start)
    relay_wait(*proj_main)
    for cp in packs:
        cp.wait()
    own_exp = pltpu.make_async_copy(exp_pack.at[c, :, tail], exp_dst(f), local_sem.at[3])
    own_exp.start()

    @pl.when(c == 0)
    def _():
        cp = pltpu.make_async_copy(exp_pack.at[0, :, head], exp_head(f), local_sem.at[6])
        cp.start()
        cp.wait()

    exp_send()
    proj_wide[...] = dot(proj_all[...], spread[...]).astype(bf16)
    line_wait(1, small_s, small_r, extra_src, extra_dst)
    biases = jnp.sum(extra_all[...].astype(f32), axis=0)
    out_b, red_b, exp_b, qv_b = [
        jnp.concatenate([biases[3 * p + q : 3 * p + q + 1, :] for q in range(3)], axis=1)
        for p in range(4)
    ]
    for k, (r2, c2) in enumerate(board):
        remote(
            live_row,
            live_all.at[4 * c2 + r2],
            small_s.at[3, k],
            small_r.at[3, 4 * c2 + r2],
            ident(r2, 2 * z + c2),
        ).wait_recv()
    gather_near(0, x_one)
    cond_sent = []
    for k, (dx, dy) in enumerate(SAME_CORE):
        cp = remote(
            cond_all,
            o_cond.at[r],
            small_s.at[4, k],
            small_r.at[4, r],
            ident(plane(dx, dy), f),
        )
        cp.start()
        cond_sent.append(cp)
    own_cond = pltpu.make_async_copy(cond_all, o_cond.at[r], local_sem.at[0])
    own_cond.start()

    lane = lax.broadcasted_iota(jnp.int32, (1, LANES_Q), 1)
    heads = [
        jnp.where((lane >= h * HEAD_DIM) & (lane < (h + 1) * HEAD_DIM), 1.0, 0.0).astype(bf16)
        for h in range(2)
    ]
    scale = HEAD_DIM ** (-0.5)

    @pl.when(z != r)
    def _():
        out_copy(z).wait_recv()

    pl.when(inner & (across[2] == r))(out_onward().start)
    red_send()

    def attend(k, carry):
        first, pair, here = chunk_of(k)

        @pl.when(k == 2)
        def _():
            gather_far(0, x_one)

        wide = dot(x_one[here, :], proj_wide[...])
        qkv[here, :LANES_Q] = (wide[:, :LANES_Q] + qv_b[:, :LANES_Q]).astype(bf16)
        qkv[here, LANES_Q : 2 * LANES_Q] = wide[:, LANES_Q : 2 * LANES_Q].astype(bf16)
        qkv[here, 2 * LANES_Q :] = (
            wide[:, 2 * LANES_Q :] + qv_b[:, LANES_Q : 2 * LANES_Q]
        ).astype(bf16)
        for i in range(2):
            u = first + i
            at = pl.ds(pl.multiple_of(u * rows, rows), rows)
            q = qkv[at, :LANES_Q]
            key = qkv[at, LANES_Q : 2 * LANES_Q]
            val = qkv[at, 2 * LANES_Q :]
            alive = live_all[u][0:1, :] > 0.5
            total = jnp.zeros((rows, LANES_Q), f32)
            for h in range(2):
                s = dot_t(q * heads[h], key) * scale
                s = jnp.where(alive, s, -1e30)
                e = jnp.exp(s - jnp.max(s, axis=-1, keepdims=True))
                p = e / jnp.sum(e, axis=-1, keepdims=True)
                probs[2 * u + h] = p
                total += dot(p.astype(bf16), val) * heads[h].astype(f32)
            attended[at, :] = total.astype(bf16)
        values = dot(attended[here, :], out_w[...])
        reduce_chunk(0, k, values, part_a, sib_a, rows_a)
        return carry

    lax.fori_loop(0, 4, attend, 0)
    exp_pass()
    branch = reduce_end(0, part_a, rows_a) + out_b
    branch_a[...] = branch
    mixed[...] = kept[...] + gate_attn * branch
    normalise(mixed[...], norm_two, rstd_two)
    own(x_two)[...] = (norm_two[...] * (1.0 + scale_mlp) + shift_mlp).astype(bf16)
    gather_start(2, x_two)
    gather_near(1, g_mlp)
    gather_far(1, g_mlp)
    red_pass()
    exp_wait()
    own_exp.wait()
    red_wait()
    gather_near(2, x_two)
    reduce_drain(0, part_a, sib_a, rows_a)

    k_gelu = 0.7978845608028654
    hid_b = exp_b[:, : exp_all.shape[1]]

    def feed(k, carry):
        first, pair, here = chunk_of(k)

        @pl.when(k == 2)
        def _():
            gather_far(2, x_two)

        hid = dot(x_two[here, :], exp_all[...]) + hid_b
        square = hid * hid
        th = jnp.tanh(k_gelu * hid * (1.0 + 0.044715 * square))
        proj_wide[here, hid_lanes] = (0.5 * hid * (1.0 + th)).astype(bf16)
        slope = 0.5 * (1.0 + th) + 0.5 * hid * (1.0 - th * th) * k_gelu * (
            1.0 + 3.0 * 0.044715 * square
        )
        grad = (dot_t(g_mlp[here, :], red_all[...]) * slope).astype(bf16)
        g_hid[here, :] = grad
        values = dot_t(grad, exp_all[...])
        reduce_chunk(1, k, values, part_b, sib_b, rows_b)
        return carry

    lax.fori_loop(0, 4, feed, 0)

    hid_sum = jnp.sum(g_hid[...].astype(f32), axis=0, keepdims=True)
    slab[8:9, : exp_all.shape[1]] = hid_sum

    def line_rows(src, z2, lanes):
        return src.at[pl.ds(pl.multiple_of(z2 * 2 * part, 16), 2 * part), lanes]

    def line_term(kind, src, landing, lanes, q):
        stop = q == 0
        index = 3 if stop else q - 1
        return remote(
            line_rows(src, across[3] if stop else across[q], lanes),
            landing.at[index, :, lanes],
            dz_s.at[kind, index],
            dz_r.at[kind, index],
            ident(r, 2 * across[1 if stop else q] + c),
        )

    def line_out(*what):
        line_term(*what, 1).start()

        @pl.when(outer)
        def _():
            line_term(*what, 0).start()
            line_term(*what, 2).start()

        @pl.when(inner)
        def _():
            line_term(*what, 3).start()

    def line_join(kind, src, landing, lanes):
        @pl.when(inner)
        def _():
            line_term(kind, src, landing, lanes, 0).wait_recv()
            term = line_rows(src, across[2], lanes)
            term[...] = (term[...].astype(f32) + landing[3, :, lanes].astype(f32)).astype(bf16)
            line_term(kind, src, landing, lanes, 2).start()

    def line_sum(kind, src, landing, lanes):
        mine_now = line_rows(src, z, lanes)
        total = mine_now[...].astype(f32)
        for q in (1, 2):
            line_term(kind, src, landing, lanes, q).wait_recv()
            total += landing[q - 1, :, lanes].astype(f32)

        @pl.when(outer)
        def _():
            mine_now[...] = total.astype(bf16)

        @pl.when(inner)
        def _():
            line_term(kind, src, landing, lanes, 3).wait_recv()
            mine_now[...] = (total + landing[2, :, lanes].astype(f32)).astype(bf16)

    def line_drain(*what):
        line_term(*what, 1).wait_send()
        line_term(*what, 2).wait_send()

        @pl.when(outer)
        def _():
            line_term(*what, 0).wait_send()

        @pl.when(inner)
        def _():
            line_term(*what, 3).wait_send()

    every = slice(None)
    exp_tail = (0, d_exp, z_exp, tail)
    exp_front = (1, d_exp, z_exp, head)
    proj_sum = (2, d_proj, z_proj, every)

    def exp_sides(step):
        step(*exp_tail)

        @pl.when(c == 0)
        def _():
            step(*exp_front)

    def wide_grad(k, carry):
        at = pl.ds(pl.multiple_of(k * third, 128), third)
        d_exp[at, :] = t_dot(x_two[:, at], g_hid[...]).astype(bf16)
        return carry

    lax.fori_loop(0, 3, wide_grad, 0)
    exp_sides(line_out)

    def red_grad(k, carry):
        at = pl.ds(pl.multiple_of(k * third, 128), third)
        d_red[:, at] = t_dot(proj_wide[:total_rows, hid_lanes], g_mlp[:, at]).astype(bf16)
        return carry

    lax.fori_loop(0, 3, red_grad, 0)

    def red_tile(i):
        p = 4 * c + i
        at = r + 4 * p
        return (p >= 5 * c), at, (2 * at) // (2 * blocks)

    def apart(goal):
        return 2 * ((z // 2 + goal // 2) % 2) + (z + goal) % 2

    def red_up(i, index, z2):
        return remote(
            d_red.at[pl.ds(i * LANES, LANES)],
            z_red.at[index, i % 3],
            zr_s.at[i],
            zr_r.at[index, i % 3],
            ident(r, 2 * z2 + c),
        )

    for i in range(slots_of):
        real, at, goal = red_tile(i)
        q = apart(goal)
        stop = outer & (q == 3)
        pl.when(real & stop)(red_up(i, 3, across[1]).start)
        direct = (q != 0) & jnp.logical_not(stop) & jnp.logical_not(inner & (q == 2))
        pl.when(real & direct)(red_up(i, (q + 3) % 4, goal).start)

    grad_two = reduce_end(1, part_b, rows_b)

    def back_norm(grad, scale_part, norm, rstd):
        g_shift = jnp.sum(grad, axis=0, keepdims=True)
        g_scale = jnp.sum(grad * norm, axis=0, keepdims=True)
        e = grad * (1.0 + scale_part)
        inner = jnp.mean(e * norm, axis=-1, keepdims=True)
        return g_shift, g_scale, (e - jnp.mean(e, axis=-1, keepdims=True) - norm * inner) * rstd

    g_shift, g_scale, through = back_norm(grad_two, scale_mlp, norm_two[...], rstd_two[...])
    slab[3:4, :] = g_shift
    slab[4:5, :] = g_scale
    g_mixed[...] = g_rows[...] + through
    slab[2:3, :] = jnp.sum(g_mixed[...] * branch_a[...], axis=0, keepdims=True)
    grad_at = (gate_attn * g_mixed[...]).astype(bf16)
    own(g_attn)[...] = grad_at
    slab[7:8, :] = jnp.sum(grad_at.astype(f32), axis=0, keepdims=True)
    gather_start(3, g_attn)

    reduce_drain(1, part_b, sib_b, rows_b)
    def feed_out(k, carry):
        first, pair, here = chunk_of(k)
        values = dot(proj_wide[here, hid_lanes], red_all[...])
        reduce_chunk(3, k, values, part_b, sib_a, rows_b, hold=True)
        return carry

    lax.fori_loop(0, 4, feed_out, 0)

    gather_near(3, g_attn)
    exp_sides(line_join)
    for dx, dy in SAME_CORE[:2]:
        reduce_send(3, part_b, rows_b, plane(dx, dy))
    def attend_back(k, carry):
        first, pair, here = chunk_of(k)

        @pl.when(k == 2)
        def _():
            gather_far(3, g_attn)
            reduce_send(3, part_b, rows_b, plane(1, 1))

        g_att = dot_t(g_attn[here, :], out_w[...]).astype(bf16)
        for i in range(2):
            u = first + i
            at = pl.ds(pl.multiple_of(u * rows, rows), rows)
            q = qkv[at, :LANES_Q]
            key = qkv[at, LANES_Q : 2 * LANES_Q]
            val = qkv[at, 2 * LANES_Q :]
            up = g_att[i * rows : (i + 1) * rows, :]
            g_q = jnp.zeros((rows, LANES_Q), f32)
            g_k = jnp.zeros((rows, LANES_Q), f32)
            g_v = jnp.zeros((rows, LANES_Q), f32)
            for h in range(2):
                p = probs[2 * u + h]
                up_h = up * heads[h]
                g_v += t_dot(p.astype(bf16), up_h)
                g_p = dot_t(up_h, val)
                inner = jnp.sum(g_p * p, axis=-1, keepdims=True)
                g_s = (p * (g_p - inner)).astype(bf16)
                g_q += dot(g_s, key) * heads[h].astype(f32)
                g_k += t_dot(g_s, q * heads[h])
            wide = jnp.concatenate([g_q * scale, g_k * scale, g_v], axis=1).astype(bf16)
            d_qkv[at, :] = dot_t(wide, spread[...]).astype(bf16)
        values = dot_t(d_qkv[here, :], proj_all[...])
        reduce_chunk(2, k, values, part_a, sib_b, rows_a)
        return carry

    lax.fori_loop(0, 4, attend_back, 0)
    def proj_grad(k, carry):
        at = pl.ds(pl.multiple_of(k * third, 128), third)
        d_proj[at, :] = t_dot(x_one[:, at], d_qkv[...]).astype(bf16)
        return carry

    lax.fori_loop(0, 3, proj_grad, 0)
    line_out(*proj_sum)
    d_out[...] = t_dot(attended[...], g_attn[...]).astype(bf16)

    def out_up(index, z2):
        return remote(
            d_out.at[pl.ds(0, part)],
            z_out.at[index],
            ow_s.at[8],
            ow_r.at[1 + index],
            ident(r, 2 * z2 + c),
        )

    q_out = apart(r)
    pl.when(outer & (q_out == 3))(out_up(3, across[1]).start)
    pl.when((q_out == 1) | (outer & (q_out == 2)) | (inner & (q_out == 3)))(
        out_up((q_out + 3) % 4, r).start
    )

    def exp_up(k, i, r2, c2):
        at = red_tile(i)[1]
        return remote(
            d_exp.at[
                pl.ds(pl.multiple_of(z * 2 * part + c2 * part, 16), part), pl.ds(i * LANES, LANES)
            ],
            o_exp.at[:, pl.ds(pl.multiple_of(at * LANES, LANES), LANES)],
            et_s.at[k, i],
            et_r.at[at],
            ident(r2, 2 * z + c2),
        )

    def exp_here(i):
        at = red_tile(i)[1]
        return pltpu.make_async_copy(
            d_exp.at[
                pl.ds(pl.multiple_of(z * 2 * part + c * part, 16), part), pl.ds(i * LANES, LANES)
            ],
            o_exp.at[:, pl.ds(pl.multiple_of(at * LANES, LANES), LANES)],
            et_l.at[i],
        )

    exp_sides(line_sum)

    for i in range(slots_of):

        @pl.when(red_tile(i)[0])
        def _():
            for k, (r2, c2) in enumerate(board):
                exp_up(k, i, r2, c2).start()
            exp_here(i).start()

    def red_out(i, h, r2):
        half = 2 * red_tile(i)[1] + h
        return remote(
            d_red.at[pl.ds(i * LANES + h * HALF, HALF)],
            o_red.at[pl.ds(pl.multiple_of(half % blocks * HALF, HALF), HALF)],
            pr_s.at[2 * i + h, r2],
            pr_r.at[half % blocks],
            ident(r2, half // blocks),
        )

    def red_here(i, h):
        half = 2 * red_tile(i)[1] + h
        return pltpu.make_async_copy(
            d_red.at[pl.ds(i * LANES + h * HALF, HALF)],
            o_red.at[pl.ds(pl.multiple_of(half % blocks * HALF, HALF), HALF)],
            pr_l.at[2 * i + h],
        )

    def red_each(i, remote_part, local_part):
        for h in range(2):
            owner = (2 * red_tile(i)[1] + h) // blocks
            for r2 in range(4):

                @pl.when((owner != f) | (r2 != r))
                def _():
                    remote_part(red_out(i, h, r2))

            @pl.when(owner == f)
            def _():
                local_part(red_here(i, h))


    slab[9:10, : d_qkv.shape[1]] = jnp.sum(d_qkv[...].astype(f32), axis=0, keepdims=True)


    for i in range(slots_of):
        real, at, goal = red_tile(i)

        @pl.when(real & inner & (apart(goal) == 2))
        def _():
            red_up(i, 3, z).wait_recv()
            rows_i = slice(i * LANES, (i + 1) * LANES)
            d_red[rows_i, :] = (
                d_red[rows_i, :].astype(f32) + z_red[3, i % 3].astype(f32)
            ).astype(bf16)
            red_up(i, 1, goal).start()


    for i in range(slots_of):
        real, at, goal = red_tile(i)

        @pl.when(real & (goal == z))
        def _():
            rows_i = slice(i * LANES, (i + 1) * LANES)
            total = d_red[rows_i, :].astype(f32)
            for there in range(2):
                red_up(i, there, z).wait_recv()
                total += z_red[there, i % 3].astype(f32)

            @pl.when(outer)
            def _():
                d_red[rows_i, :] = total.astype(bf16)

            @pl.when(inner)
            def _():
                red_up(i, 2, z).wait_recv()
                d_red[rows_i, :] = (total + z_red[2, i % 3].astype(f32)).astype(bf16)

            red_each(i, lambda cp: cp.start(), lambda cp: cp.start())

    def place(values, base):
        live_hot = one_hot() * live_row[0:1, :]
        placed = dot(live_hot.astype(bf16), values.astype(bf16))
        hit = jnp.sum(live_hot, axis=1, keepdims=True)
        return jnp.where(hit > 0.5, placed.astype(bf16), base)

    branch = reduce_end(3, part_b, rows_b) + red_b
    @pl.when(inner & (q_out == 2))
    def _():
        out_up(3, z).wait_recv()
        d_out[:part, :] = (d_out[:part, :].astype(f32) + z_out[3].astype(f32)).astype(bf16)
        out_up(1, r).start()

    slab[5:6, :] = jnp.sum(g_rows[...] * branch, axis=0, keepdims=True)
    o_block[...] = place(mixed[...] + gate_mlp * branch, latents[...])

    def slab_at(f2):
        return 4 * (f2 % 2) + f2 // 2

    grad_one = reduce_end(2, part_a, rows_a)
    g_shift, g_scale, through = back_norm(grad_one, scale_attn, norm_one[...], rstd_one[...])
    slab[0:1, :] = g_shift
    slab[1:2, :] = g_scale
    o_latents[...] = place(g_mixed[...] + through, cotangent[...])
    slabs[slab_at(f)] = slab[...].astype(bf16)

    def slab_src(f2, c2):
        return slabs.at[slab_at(f)]

    def slab_dst(f2):
        return slabs.at[slab_at(f2)]

    sent += line_send(5, small_s, small_r, slab_src, slab_dst)

    line_join(*proj_sum)
    @pl.when(z == r)
    def _():
        total = d_out[:part, :].astype(f32)
        for k in range(2):
            out_up(k, z).wait_recv()
            total += z_out[k].astype(f32)

        @pl.when(outer)
        def _():
            d_out[:part, :] = total.astype(bf16)

        @pl.when(inner)
        def _():
            out_up(2, z).wait_recv()
            d_out[:part, :] = (total + z_out[2].astype(f32)).astype(bf16)

        for k, (dx, dy) in enumerate(SAME_CORE):
            remote(
                d_out.at[pl.ds(0, part)], o_out, ow_s.at[4 + k], ow_r.at[5], ident(plane(dx, dy), f)
            ).start()
        cp = pltpu.make_async_copy(d_out.at[pl.ds(0, part)], o_out, local_sem.at[5])
        cp.start()
        cp.wait()

    line_wait(5, small_s, small_r, slab_src, slab_dst)
    mine = pl.ds(pl.multiple_of(4 * c, 4), 4)
    for k, (dx, dy) in enumerate(SAME_CORE):
        cp = remote(
            slabs.at[mine],
            o_slabs.at[r, mine],
            small_s.at[6, k],
            small_r.at[6, r],
            ident(plane(dx, dy), f),
        )
        cp.start()
        sent.append(cp)
    own_slabs = pltpu.make_async_copy(slabs, o_slabs.at[r], local_sem.at[4])
    own_slabs.start()
    back_cond = jnp.zeros((8, part), f32)
    for p in range(6):
        back_cond += dot_t(slabs[:, p, :], mod_w[:, p * width : (p + 1) * width])
    for i in range(8):
        gcond[2 * (i % 4) + i // 4] = jnp.broadcast_to(back_cond[i : i + 1, :], (8, part))

    def gc_src(f2, c2):
        return gcond.at[f2]

    def gc_dst(f2):
        return o_gcond.at[f2]

    sent += line_send(7, small_s, small_r, gc_src, gc_dst)
    o_gcond[f] = gcond[f]

    line_sum(*proj_sum)

    def proj_up(k, r2, c2):
        return remote(
            d_proj.at[pl.ds(pl.multiple_of(z * 2 * part + c2 * part, 16), part)],
            proj_land.at[me],
            dp_s.at[k],
            dp_r.at[me],
            ident(r2, 2 * z + c2),
        )

    for k, (r2, c2) in enumerate(board):
        proj_up(k, r2, c2).start()
    proj_land[me] = d_proj[pl.ds(pl.multiple_of(z * 2 * part + c * part, 16), part), :]

    for k, (dx, dy) in enumerate(SAME_CORE):
        r2 = plane(dx, dy)
        remote(
            slabs.at[mine], o_slabs.at[r2, mine], small_s.at[6, 0], small_r.at[6, r2], sibling
        ).wait_recv()
        cp = remote(
            o_slabs.at[r2, mine],
            o_slabs.at[r2, mine],
            small_s.at[6, 3 + k],
            small_r.at[6, 4 + r2],
            sibling,
        )
        cp.start()
        sent.append(cp)
    line_wait(7, small_s, small_r, gc_src, gc_dst)
    for dx, dy in SAME_CORE:
        r2 = plane(dx, dy)
        remote(
            cond_all, o_cond.at[r2], small_s.at[4, 0], small_r.at[4, r2], ident(r2, f)
        ).wait_recv()
        theirs = pl.ds(pl.multiple_of(4 * other, 4), 4)
        remote(
            slabs.at[theirs], o_slabs.at[r2, theirs], small_s.at[6, 3], small_r.at[6, 4 + r2], sibling
        ).wait_recv()
    o_proj[...] = jnp.zeros(o_proj.shape, bf16)

    def unpack(r2, c2):
        t = 2 * r2 + c2
        wide = dot(proj_land[4 * c2 + r2], spread[...])
        for q in range(3):
            piece = pltpu.roll(wide[:, q * LANES_Q : (q + 1) * LANES_Q], t * (part - LANES), 1)
            here = pl.ds(pl.multiple_of(q * width + t * LANES, LANES), LANES_Q)
            o_proj[:, here] = (o_proj[:, here].astype(f32) + piece).astype(bf16)

    unpack(r, c)
    for r2, c2 in board:
        u = 4 * c2 + r2
        remote(
            proj_land.at[u], proj_land.at[u], dp_s.at[0], dp_r.at[u], ident(r2, 2 * z + c2)
        ).wait_recv()
        unpack(r2, c2)

    def tile_arrival(at, carry):
        p = at // 4

        @pl.when((at % 4 != r) | (p // slots_of != c))
        def _():
            remote(
                d_exp.at[pl.ds(0, part), pl.ds(0, LANES)],
                o_exp.at[:, pl.ds(pl.multiple_of(at * LANES, LANES), LANES)],
                et_s.at[0, 0],
                et_r.at[at],
                sibling,
            ).wait_recv()

        return carry

    lax.fori_loop(0, tiles, tile_arrival, 0)

    def block_arrival(block, carry):
        at = (blocks * f + block) // 2
        p = at // 4

        @pl.when((at % 4 != r) | (p // slots_of != c))
        def _():
            remote(
                d_red.at[pl.ds(0, HALF)],
                o_red.at[pl.ds(pl.multiple_of(block * HALF, HALF), HALF)],
                pr_s.at[0, 0],
                pr_r.at[block],
                sibling,
            ).wait_recv()

        return carry

    lax.fori_loop(0, blocks, block_arrival, 0)
    for i in range(slots_of):
        real, at, goal = red_tile(i)

        @pl.when(real)
        def _():
            for k, (r2, c2) in enumerate(board):
                exp_up(k, i, r2, c2).wait_send()
            exp_here(i).wait()

        @pl.when(real & (goal == z))
        def _():
            red_each(i, lambda cp: cp.wait_send(), lambda cp: cp.wait())

        @pl.when(real & (goal != z))
        def _():
            red_up(i, 0, z).wait_send()

    for k, (r2, c2) in enumerate(board):
        proj_up(k, r2, c2).wait_send()
    red_drain()
    exp_drain()

    exp_sides(line_drain)
    line_drain(*proj_sum)
    for z2 in range(4):
        pl.when(out_goes(z2))(out_copy(z2).wait_send)
    pl.when(inner & (across[2] == r))(out_onward().wait_send)

    @pl.when(z == r)
    def _():
        for k in range(3):
            remote(out_shard, o_out, ow_s.at[4 + k], ow_r.at[5], ident(r, f)).wait_send()

    @pl.when(z != r)
    def _():
        remote(out_shard, o_out, ow_s.at[3], ow_r.at[5], ident(r, f)).wait_recv()
        out_up(0, r).wait_send()

    relay_drain(*proj_main)
    reduce_drain(2, part_a, sib_b, rows_a)
    reduce_drain(3, part_b, sib_a, rows_b)
    for kind, buf in enumerate((x_one, g_mlp, x_two, g_attn)):
        gather_drain(kind, buf)
    drain(sent)
    drain(live_sent)
    drain(cond_sent)
    own_cond.wait()
    own_slabs.wait()


def fused_local(
    latents,
    condition,
    bucket,
    keep_slots,
    modulation_weight,
    modulation_bias,
    projection_weight,
    query_value_bias,
    output_weight,
    output_bias,
    expand_weight,
    expand_bias,
    reduce_weight,
    reduce_bias,
    cotangent,
):
    f32 = jnp.float32
    bf16 = jnp.bfloat16
    r = lax.axis_index("replica")
    f = lax.axis_index("fsdp")
    slot_count, width = latents.shape[1:]
    rows = keep_slots.shape[1]
    part = output_weight.shape[0]
    hid = expand_weight.shape[1]
    slots_of = (hid // LANES + 7) // 8
    wide = slots_of * LANES

    def placed(shard, count):
        return lax.dynamic_update_slice_in_dim(
            jnp.zeros((count,), f32), shard.astype(f32), f * shard.shape[0], 0
        )

    def mine(value, axis):
        return lax.dynamic_slice_in_dim(value, 2 * r, 2, axis)

    cond_float = condition.astype(f32)
    cond_act = jax.nn.silu(cond_float).astype(bf16)
    cond_pack = jnp.pad(cond_act.reshape(8, 1, part), ((0, 0), (0, 15), (0, 0)))
    mod_bias = jnp.pad(placed(modulation_bias, 6 * width).reshape(6, width), ((0, 2), (0, 0)))
    live_count = jnp.where(bucket[0] == 0, slot_count, slot_count - 16) // 2
    live = (jnp.arange(rows, dtype=jnp.int32) < live_count).astype(f32)
    qv = mine(placed(query_value_bias, 2 * width).reshape(2, 8, part), 1)
    qv = jnp.pad(qv.transpose(1, 0, 2), ((0, 0), (0, 0), (0, LANES_Q - part))).reshape(2, -1)
    tiled_b = placed(expand_bias, hid).reshape(hid // (4 * LANES), 4, LANES)
    tiled_b = lax.dynamic_index_in_dim(tiled_b, r, 1, keepdims=False)
    second_b = jnp.pad(tiled_b[slots_of:], ((1, 0), (0, 0)))
    expand_b = jnp.stack([tiled_b[:slots_of].reshape(-1), second_b.reshape(-1)])
    extra = jnp.stack(
        [
            jnp.broadcast_to(placed(output_bias, width), (2, width)),
            jnp.broadcast_to(placed(reduce_bias, width), (2, width)),
            jnp.pad(expand_b, ((0, 0), (0, width - wide))),
            jnp.pad(qv, ((0, 0), (0, width - 2 * LANES_Q))),
        ],
        axis=1,
    ).astype(bf16)
    extra = jnp.pad(extra.reshape(2, 12, width // 3), ((0, 0), (0, 4), (0, 0)))
    total = 8 * rows
    vmem = pltpu.VMEM
    dma = pltpu.SemaphoreType.DMA
    scratch = [
        vmem((8, 16, part), bf16),
        vmem((8, 16, width // 3), bf16),
        vmem((8, 8, rows), f32),
        vmem((8, 8, width), f32),
        vmem((8, 8, width), f32),
        vmem((width, 3 * part), bf16),
        vmem((width, wide), bf16),
        vmem((wide, width), bf16),
        vmem((LANES_Q, width), bf16),
        vmem((2, part, 3 * part), bf16),
        vmem((2, part, wide), bf16),
        vmem((width, 3 * LANES_Q), bf16),
        vmem((3 * part, 3 * LANES_Q), bf16),
        vmem((total, width), bf16),
        vmem((total, width), bf16),
        vmem((total, width), bf16),
        vmem((total, width), bf16),
        vmem((total, 3 * LANES_Q), bf16),
        vmem((16, rows, rows), f32),
        vmem((total, LANES_Q), bf16),
        vmem((total, wide), bf16),
        vmem((total, 3 * part), bf16),
        vmem((total, width), bf16),
        vmem((total, width), bf16),
    ]
    scratch += [vmem((4 * rows, width), bf16)] * 2
    scratch += [vmem((4, rows, width), bf16)] * 2
    scratch += [
        vmem((rows, width), f32),
        vmem((rows, 1), f32),
        vmem((rows, width), f32),
        vmem((rows, width), f32),
        vmem((rows, width), f32),
        vmem((rows, width), f32),
        vmem((rows, 1), f32),
        vmem((rows, width), f32),
        vmem((16, width), f32),
        vmem((8, 16, width), bf16),
        vmem((8, 8, part), f32),
        vmem((width, wide), bf16),
        vmem((wide, width), bf16),
        vmem((width, 3 * part), bf16),
        vmem((LANES_Q, width), bf16),
        vmem((4, 2 * part, wide), bf16),
        vmem((4, 3, LANES, width), bf16),
        vmem((4, 2 * part, 3 * part), bf16),
        vmem((4, part, width), bf16),
        vmem((8, part, 3 * part), bf16),
        dma((8,)),
        dma((8, 7)),
        dma((8, 8)),
        dma((3, 7)),
        dma((3, 8)),
        dma((4, 8)),
        dma((4, 9)),
        dma((4, 2)),
        dma((4, 2)),
        dma((4, 4)),
        dma((4, 4)),
        dma((3, 4)),
        dma((3, 4)),
        dma((7,)),
        dma((8,)),
        dma((9,)),
        dma((6,)),
        dma((hid // HALF // 4, 4)),
        dma((2 * slots_of,)),
        dma((2 * slots_of,)),
        dma((slots_of,)),
        dma((4, 3)),
        dma((2, slots_of)),
        dma((7, slots_of)),
        dma((hid // LANES,)),
        dma((slots_of,)),
        dma((2 * slots_of, 4)),
        dma((hid // HALF // 8,)),
        dma((2 * slots_of,)),
        dma((3, 2)),
        dma((2 * slots_of,)),
    ]
    in_vmem = pl.BlockSpec(memory_space=pltpu.VMEM)
    anywhere = pl.BlockSpec(memory_space=pl.ANY)
    outputs = pl.pallas_call(
        fused_kernel,
        out_shape=(
            jax.ShapeDtypeStruct((slot_count, width), bf16),
            jax.ShapeDtypeStruct((slot_count, width), bf16),
            jax.ShapeDtypeStruct((4, 8, 16, width), bf16),
            jax.ShapeDtypeStruct((4, 8, 16, part), bf16),
            jax.ShapeDtypeStruct((8, 8, part), f32),
            jax.ShapeDtypeStruct((part, hid), bf16),
            jax.ShapeDtypeStruct((hid // 8, width), bf16),
            jax.ShapeDtypeStruct((part, 3 * width), bf16),
            jax.ShapeDtypeStruct((part, width), bf16),
        ),
        in_specs=[in_vmem] * 9 + [anywhere] * 2 + [in_vmem],
        out_specs=(
            in_vmem,
            in_vmem,
            anywhere,
            anywhere,
            in_vmem,
            anywhere,
            anywhere,
            in_vmem,
            anywhere,
        ),
        scratch_shapes=scratch,
        compiler_params=pltpu.CompilerParams(
            collective_id=0, has_side_effects=True, vmem_limit_bytes=60 << 20
        ),
    )(
        latents[0],
        cotangent[0],
        keep_slots,
        jnp.broadcast_to(live[None], (8, rows)),
        cond_pack,
        mod_bias,
        extra,
        modulation_weight,
        projection_weight,
        expand_weight,
        reduce_weight,
        output_weight,
    )
    block, grad_latents, slabs, conds, g_cond, g_exp, g_red, g_proj, g_out = outputs

    def shard(value, axis, size):
        return lax.dynamic_slice_in_dim(value, f * size, size, axis)

    slabs = slabs.reshape(32, 16, width)
    grad_mod = slabs[:, :6].reshape(32, 6 * width)
    cond_cols = conds[:, :, 0].reshape(4, 4, 2, part).transpose(0, 2, 1, 3).reshape(32, part)
    sum_mod_w = jnp.einsum("bd,be->de", cond_cols, grad_mod, preferred_element_type=f32)
    tails = jnp.sum(slabs.reshape(4, 2, 4, 16, width)[:, :, :, :10].astype(f32), axis=2)
    sums = jnp.sum(tails[:, :, :8], axis=(0, 1))
    tails = tails[:, :, 8:]
    sum_mod_b = shard(sums[:6].reshape(-1), 0, modulation_bias.shape[0])
    sum_red_b = shard(sums[6], 0, part)
    sum_out_b = shard(sums[7], 0, part)
    exp_sums = tails[:, :, 0, :wide].reshape(4, 2, slots_of, LANES)
    exp_sums = jnp.concatenate([exp_sums[:, 0], exp_sums[:, 1, 1:]], axis=1)
    sum_exp_b = shard(exp_sums.transpose(1, 0, 2).reshape(-1), 0, expand_bias.shape[0])
    qv_sums = tails[:, :, 1, : 3 * part].reshape(8, 3, part)
    qv_sums = jnp.concatenate([qv_sums[:, 0].reshape(-1), qv_sums[:, 2].reshape(-1)])
    sum_qv_b = shard(qv_sums, 0, query_value_bias.shape[0])
    grad_condition = jax.vjp(jax.nn.silu, cond_float)[1](g_cond[:, 0].reshape(1, width))[0]
    return (
        block[None],
        grad_latents[None],
        grad_condition,
        sum_mod_w,
        sum_mod_b,
        g_proj.astype(f32),
        sum_qv_b,
        g_out.astype(f32),
        sum_out_b,
        g_exp.astype(f32),
        sum_exp_b,
        g_red.astype(f32),
        sum_red_b,
    )


def solution(mesh):
    placed = (
        P(("replica", "fsdp"), None, None),
        P(("replica", "fsdp"), None),
        P(("replica", "fsdp")),
        P(("replica", "fsdp"), None),
        P("fsdp", None),
        P("fsdp"),
        P("fsdp", None),
        P("fsdp"),
        P("fsdp", None),
        P("fsdp"),
        P("fsdp", None),
        P("fsdp"),
        P("fsdp", None),
        P("fsdp"),
        P(("replica", "fsdp"), None, None),
    )
    body = fused_local if tuple(mesh.shape.values()) == (4, 8) else local
    return jax.shard_map(
        body,
        mesh=mesh,
        in_specs=placed,
        out_specs=(
            P(("replica", "fsdp"), None, None),
            P(("replica", "fsdp"), None, None),
            P(("replica", "fsdp"), None),
            P("fsdp", None),
            P("fsdp"),
            P("fsdp", None),
            P("fsdp"),
            P("fsdp", None),
            P("fsdp"),
            P("fsdp", None),
            P("fsdp"),
            P("fsdp", None),
            P("fsdp"),
        ),
        check_vma=False,
    )
```

```python
import jax
import jax.numpy as jnp
from jax import lax
from jax.experimental import pallas as pl
from jax.experimental.pallas import tpu as pltpu
from jax.sharding import PartitionSpec as P

HEADS = 16
HEAD_DIM = 72


def layer_norm(rows_in):
    row_mean = jnp.mean(rows_in, axis=-1, keepdims=True)
    centred = rows_in - row_mean
    row_var = jnp.mean(centred * centred, axis=-1, keepdims=True)
    return centred * lax.rsqrt(row_var + 1e-06)


def modulate(rows_in, shift_part, scale_part):
    return layer_norm(rows_in) * (1.0 + scale_part) + shift_part


def gelu_tanh(values_in):
    return jax.nn.gelu(values_in, approximate=True)


def place_rows(target_rows, target_index, new_rows):
    return target_rows.at[target_index].set(new_rows, mode="drop")


def column_sums(rows_in):
    return jnp.sum(rows_in.astype(jnp.float32), axis=0)


def local(
    latents,
    condition,
    bucket,
    keep_slots,
    modulation_weight,
    modulation_bias,
    projection_weight,
    query_value_bias,
    output_weight,
    output_bias,
    expand_weight,
    expand_bias,
    reduce_weight,
    reduce_bias,
    cotangent,
):
    f32 = jnp.float32
    bf16 = jnp.bfloat16
    images, slot_count, model_width = latents.shape
    kept_rows = keep_slots.shape[1]
    row_count = images * kept_rows
    score_scale = HEAD_DIM ** (-0.5)
    shape_heads = (images, kept_rows, HEADS, HEAD_DIM)
    (
        full_mod_w,
        full_mod_b,
        full_proj_w,
        full_qv_b,
        full_out_w,
        full_out_b,
        full_exp_w,
        full_exp_b,
        full_red_w,
        full_red_b,
    ) = (
        lax.all_gather(modulation_weight, "fsdp", axis=0, tiled=True),
        lax.all_gather(modulation_bias, "fsdp", axis=0, tiled=True),
        lax.all_gather(projection_weight, "fsdp", axis=0, tiled=True),
        lax.all_gather(query_value_bias, "fsdp", axis=0, tiled=True),
        lax.all_gather(output_weight, "fsdp", axis=0, tiled=True),
        lax.all_gather(output_bias, "fsdp", axis=0, tiled=True),
        lax.all_gather(expand_weight, "fsdp", axis=0, tiled=True),
        lax.all_gather(expand_bias, "fsdp", axis=0, tiled=True),
        lax.all_gather(reduce_weight, "fsdp", axis=0, tiled=True),
        lax.all_gather(reduce_bias, "fsdp", axis=0, tiled=True),
    )
    live_count = jnp.where(bucket == 0, slot_count, slot_count - 16) // 2
    live_rows = jnp.arange(kept_rows, dtype=jnp.int32)[None, :] < live_count[:, None]
    live_float = live_rows.astype(f32)[:, :, None]
    gather_index = keep_slots[:, :, None]
    kept = jnp.take_along_axis(latents, gather_index, axis=1).astype(f32)
    cond_float = condition.astype(f32)
    cond_act = jax.nn.silu(cond_float).astype(bf16)
    modulation = jnp.dot(cond_act, full_mod_w, preferred_element_type=f32) + full_mod_b.astype(f32)
    pieces = [modulation[:, None, i * model_width : (i + 1) * model_width] for i in range(6)]
    shift_attn, scale_attn, gate_attn, shift_mlp, scale_mlp, gate_mlp = pieces
    normed_one = modulate(kept, shift_attn, scale_attn).astype(bf16).reshape(row_count, model_width)
    projected = jnp.dot(normed_one, full_proj_w, preferred_element_type=f32)
    bias_qv = full_qv_b.astype(f32)
    query_rows = (
        (projected[:, :model_width] + bias_qv[:model_width]).astype(bf16).reshape(shape_heads)
    )
    key_rows = projected[:, model_width : 2 * model_width].astype(bf16).reshape(shape_heads)
    value_rows = (
        (projected[:, 2 * model_width :] + bias_qv[model_width:]).astype(bf16).reshape(shape_heads)
    )

    def masked_scores(queries, keys_in):
        raw = (
            jnp.einsum("bqhd,bkhd->bhqk", queries, keys_in, preferred_element_type=f32)
            * score_scale
        )
        return jnp.where(live_rows[:, None, None, :], raw, -1e30)

    scores = masked_scores(query_rows, key_rows)
    row_max = jnp.max(scores, axis=-1, keepdims=True)
    row_total = jnp.sum(jnp.exp(scores - row_max), axis=-1, keepdims=True)
    log_total = row_max + jnp.log(row_total)
    probs = jnp.exp(scores - log_total)
    attended = (
        jnp.einsum("bhqk,bkhd->bqhd", probs.astype(bf16), value_rows, preferred_element_type=f32)
        .astype(bf16)
        .reshape(row_count, model_width)
    )
    branch_attn = (
        jnp.dot(attended, full_out_w, preferred_element_type=f32) + full_out_b.astype(f32)
    ).reshape(images, kept_rows, model_width)
    mixed = kept + gate_attn * branch_attn
    normed_two = modulate(mixed, shift_mlp, scale_mlp).astype(bf16).reshape(row_count, model_width)
    hidden = jnp.dot(normed_two, full_exp_w, preferred_element_type=f32) + full_exp_b.astype(f32)
    activation = gelu_tanh(hidden).astype(bf16)
    branch_mlp = (
        jnp.dot(activation, full_red_w, preferred_element_type=f32) + full_red_b.astype(f32)
    ).reshape(images, kept_rows, model_width)
    result = mixed + gate_mlp * branch_mlp
    target = jnp.where(live_rows, keep_slots, slot_count)
    block_out = jax.vmap(place_rows)(latents, target, result.astype(bf16))
    back_mod_w, back_proj_w, back_out_w, back_exp_w, back_red_w = (
        lax.all_gather(modulation_weight, "fsdp", axis=0, tiled=True),
        lax.all_gather(projection_weight, "fsdp", axis=0, tiled=True),
        lax.all_gather(output_weight, "fsdp", axis=0, tiled=True),
        lax.all_gather(expand_weight, "fsdp", axis=0, tiled=True),
        lax.all_gather(reduce_weight, "fsdp", axis=0, tiled=True),
    )
    grad_rows = jnp.take_along_axis(cotangent, gather_index, axis=1).astype(f32) * live_float
    grad_gate_mlp = jnp.sum(grad_rows * branch_mlp, axis=1)
    grad_mlp = (gate_mlp * grad_rows).astype(bf16).reshape(row_count, model_width)
    local_red_w = jnp.einsum("rm,rd->md", activation, grad_mlp, preferred_element_type=f32)
    local_red_b = column_sums(grad_mlp)
    grad_act = jnp.einsum("rd,md->rm", grad_mlp, back_red_w, preferred_element_type=f32)
    gelu_pull = jax.vjp(gelu_tanh, hidden)[1]
    grad_hidden = gelu_pull(grad_act)[0].astype(bf16)
    local_exp_w = jnp.einsum("rd,rm->dm", normed_two, grad_hidden, preferred_element_type=f32)
    local_exp_b = column_sums(grad_hidden)
    mlp_red_w, mlp_red_b, mlp_exp_w, mlp_exp_b = (
        lax.psum_scatter(
            local_red_w.astype(jnp.bfloat16), "fsdp", scatter_dimension=0, tiled=True
        ).astype(jnp.float32),
        lax.psum_scatter(
            local_red_b.astype(jnp.bfloat16), "fsdp", scatter_dimension=0, tiled=True
        ).astype(jnp.float32),
        lax.psum_scatter(
            local_exp_w.astype(jnp.bfloat16), "fsdp", scatter_dimension=0, tiled=True
        ).astype(jnp.float32),
        lax.psum_scatter(
            local_exp_b.astype(jnp.bfloat16), "fsdp", scatter_dimension=0, tiled=True
        ).astype(jnp.float32),
    )
    grad_normed_two = jnp.einsum(
        "rm,dm->rd", grad_hidden, back_exp_w, preferred_element_type=f32
    ).reshape(images, kept_rows, model_width)
    pull_two = jax.vjp(modulate, mixed, shift_mlp, scale_mlp)[1]
    grad_mixed_ln, grad_shift_mlp, grad_scale_mlp = pull_two(grad_normed_two)
    grad_mixed = grad_rows + grad_mixed_ln
    grad_gate_attn = jnp.sum(grad_mixed * branch_attn, axis=1)
    grad_attn = (gate_attn * grad_mixed).astype(bf16).reshape(row_count, model_width)
    local_out_w = jnp.einsum("rd,re->de", attended, grad_attn, preferred_element_type=f32)
    local_out_b = column_sums(grad_attn)
    grad_attended = (
        jnp.einsum("re,de->rd", grad_attn, back_out_w, preferred_element_type=f32)
        .astype(bf16)
        .reshape(shape_heads)
    )
    scores_again = masked_scores(query_rows, key_rows)
    probs_again = jnp.exp(scores_again - log_total)
    grad_values = jnp.einsum(
        "bhqk,bqhd->bkhd", probs_again.astype(bf16), grad_attended, preferred_element_type=f32
    ).astype(bf16)
    grad_probs = jnp.einsum(
        "bqhd,bkhd->bhqk", grad_attended, value_rows, preferred_element_type=f32
    )
    row_inner = jnp.sum(grad_probs * probs_again, axis=-1, keepdims=True)
    grad_scores = (probs_again * (grad_probs - row_inner)).astype(bf16)
    grad_query = (
        jnp.einsum("bhqk,bkhd->bqhd", grad_scores, key_rows, preferred_element_type=f32)
        * score_scale
    ).astype(bf16)
    grad_keys = (
        jnp.einsum("bhqk,bqhd->bkhd", grad_scores, query_rows, preferred_element_type=f32)
        * score_scale
    ).astype(bf16)
    grad_projected = jnp.concatenate(
        [
            grad_query.reshape(row_count, model_width),
            grad_keys.reshape(row_count, model_width),
            grad_values.reshape(row_count, model_width),
        ],
        axis=1,
    )
    local_proj_w = jnp.einsum("rd,re->de", normed_one, grad_projected, preferred_element_type=f32)
    local_qv_b = jnp.concatenate(
        [
            column_sums(grad_projected[:, :model_width]),
            column_sums(grad_projected[:, 2 * model_width :]),
        ]
    )
    grad_normed_one = jnp.einsum(
        "re,de->rd", grad_projected, back_proj_w, preferred_element_type=f32
    ).reshape(images, kept_rows, model_width)
    pull_one = jax.vjp(modulate, kept, shift_attn, scale_attn)[1]
    grad_kept_ln, grad_shift_attn, grad_scale_attn = pull_one(grad_normed_one)
    grad_kept = grad_mixed + grad_kept_ln
    grad_latents = jax.vmap(place_rows)(cotangent, target, grad_kept.astype(bf16))
    grad_modulation = jnp.concatenate(
        [
            grad_shift_attn[:, 0],
            grad_scale_attn[:, 0],
            grad_gate_attn,
            grad_shift_mlp[:, 0],
            grad_scale_mlp[:, 0],
            grad_gate_mlp,
        ],
        axis=1,
    ).astype(bf16)
    grad_cond_act = jnp.einsum("be,de->bd", grad_modulation, back_mod_w, preferred_element_type=f32)
    silu_pull = jax.vjp(jax.nn.silu, cond_float)[1]
    grad_condition = silu_pull(grad_cond_act)[0]
    local_mod_w = jnp.einsum("bd,be->de", cond_act, grad_modulation, preferred_element_type=f32)
    local_mod_b = column_sums(grad_modulation)
    rest_mod_w, rest_mod_b, rest_proj_w, rest_qv_b, rest_out_w, rest_out_b = (
        lax.psum_scatter(
            local_mod_w.astype(jnp.bfloat16), "fsdp", scatter_dimension=0, tiled=True
        ).astype(jnp.float32),
        lax.psum_scatter(
            local_mod_b.astype(jnp.bfloat16), "fsdp", scatter_dimension=0, tiled=True
        ).astype(jnp.float32),
        lax.psum_scatter(
            local_proj_w.astype(jnp.bfloat16), "fsdp", scatter_dimension=0, tiled=True
        ).astype(jnp.float32),
        lax.psum_scatter(
            local_qv_b.astype(jnp.bfloat16), "fsdp", scatter_dimension=0, tiled=True
        ).astype(jnp.float32),
        lax.psum_scatter(
            local_out_w.astype(jnp.bfloat16), "fsdp", scatter_dimension=0, tiled=True
        ).astype(jnp.float32),
        lax.psum_scatter(
            local_out_b.astype(jnp.bfloat16), "fsdp", scatter_dimension=0, tiled=True
        ).astype(jnp.float32),
    )
    shares = (
        lax.psum_scatter(
            rest_mod_w.astype(jnp.bfloat16), "replica", scatter_dimension=1, tiled=True
        ).astype(jnp.float32),
        lax.psum_scatter(
            rest_proj_w.astype(jnp.bfloat16), "replica", scatter_dimension=1, tiled=True
        ).astype(jnp.float32),
        lax.psum_scatter(
            rest_out_w.astype(jnp.bfloat16), "replica", scatter_dimension=1, tiled=True
        ).astype(jnp.float32),
        lax.psum_scatter(
            mlp_exp_w.astype(jnp.bfloat16), "replica", scatter_dimension=1, tiled=True
        ).astype(jnp.float32),
        lax.psum_scatter(
            mlp_red_w.astype(jnp.bfloat16), "replica", scatter_dimension=1, tiled=True
        ).astype(jnp.float32),
    )
    sum_mod_w, sum_proj_w, sum_out_w, sum_exp_w, sum_red_w = (
        lax.all_gather(shares[0].astype(jnp.bfloat16), "replica", axis=1, tiled=True).astype(
            jnp.float32
        ),
        lax.all_gather(shares[1].astype(jnp.bfloat16), "replica", axis=1, tiled=True).astype(
            jnp.float32
        ),
        lax.all_gather(shares[2].astype(jnp.bfloat16), "replica", axis=1, tiled=True).astype(
            jnp.float32
        ),
        lax.all_gather(shares[3].astype(jnp.bfloat16), "replica", axis=1, tiled=True).astype(
            jnp.float32
        ),
        lax.all_gather(shares[4].astype(jnp.bfloat16), "replica", axis=1, tiled=True).astype(
            jnp.float32
        ),
    )
    sum_mod_b, sum_qv_b, sum_out_b, sum_exp_b, sum_red_b = lax.psum(
        (rest_mod_b, rest_qv_b, rest_out_b, mlp_exp_b, mlp_red_b), "replica"
    )
    return (
        block_out,
        grad_latents,
        grad_condition,
        sum_mod_w,
        sum_mod_b,
        sum_proj_w,
        sum_qv_b,
        sum_out_w,
        sum_out_b,
        sum_exp_w,
        sum_exp_b,
        sum_red_w,
        sum_red_b,
    )


MESH = pl.DeviceIdType.MESH
SAME_CORE = ((1, 0), (0, 1), (1, 1))
LANES = 128
HALF = 64
LANES_Q = 256


def fused_kernel(
    latents,
    cotangent,
    slots,
    live_row,
    cond_pack,
    mod_bias,
    extra,
    mod_w,
    proj_w,
    exp_w,
    red_w,
    out_shard,
    o_block,
    o_latents,
    o_slabs,
    o_cond,
    o_gcond,
    o_exp,
    o_red,
    o_proj,
    o_out,
    cond_all,
    extra_all,
    live_all,
    mod_send,
    mod_all,
    proj_all,
    exp_all,
    red_all,
    out_w,
    proj_pack,
    exp_pack,
    proj_wide,
    spread,
    x_one,
    x_two,
    g_mlp,
    g_attn,
    qkv,
    probs,
    attended,
    g_hid,
    d_qkv,
    part_a,
    part_b,
    sib_a,
    sib_b,
    rows_a,
    rows_b,
    norm_one,
    rstd_one,
    g_rows,
    branch_a,
    mixed,
    norm_two,
    rstd_two,
    g_mixed,
    slab,
    slabs,
    gcond,
    d_exp,
    d_red,
    d_proj,
    d_out,
    z_exp,
    z_red,
    z_proj,
    z_out,
    proj_land,
    local_sem,
    small_s,
    small_r,
    w_s,
    w_r,
    ag_s,
    ag_r,
    sb_s,
    sb_r,
    rs_s,
    rs_r,
    dz_s,
    dz_r,
    dp_s,
    dp_r,
    ow_s,
    ow_r,
    red_s,
    red_r,
    red_l,
    zr_s,
    zr_r,
    pe_s,
    et_s,
    et_r,
    et_l,
    pr_s,
    pr_r,
    pr_l,
    relay_s,
    red_f,
):
    f32 = jnp.float32
    bf16 = jnp.bfloat16
    r = lax.axis_index("replica")
    f = lax.axis_index("fsdp")
    x, y, c, z = r % 2, r // 2, f % 2, f // 2
    width = latents.shape[1]
    rows = slots.shape[1]
    part = out_shard.shape[0]
    third = width // 3
    kept = g_mixed
    total_rows = x_one.shape[0]
    hid_lanes = pl.ds(0, red_all.shape[0])
    blocks = red_w.shape[0] // HALF
    slots_of = red_all.shape[0] // LANES
    tiles = exp_w.shape[1] // LANES
    me = 4 * c + r
    other = (c + 1) % 2

    def ident(r2, f2):
        return {"replica": r2, "fsdp": f2}

    def remote(src, dst, s_sem, r_sem, dev):
        return pltpu.make_async_remote_copy(
            src_ref=src,
            dst_ref=dst,
            send_sem=s_sem,
            recv_sem=r_sem,
            device_id=dev,
            device_id_type=MESH,
        )

    def plane(dx, dy):
        return ((y + dy) % 2) * 2 + (x + dx) % 2

    sibling = ident(r, 2 * z + other)
    line = []
    across = (z, z + 1 - 2 * (z % 2), (z + 2) % 4, 3 - z)
    for dz in (2, 1, 3, 0):
        for dc in range(2):
            if dz or dc:
                line.append((across[dz], (c + dc) % 2))
    far = (4, 5)
    via = (0, 1)
    outer = (z == 0) | (z == 3)
    inner = (z == 1) | (z == 2)
    board = []
    for dx in range(2):
        for dy in range(2):
            for dc in range(2):
                if dx or dy or dc:
                    board.append((plane(dx, dy), (c + dc) % 2))

    barrier = pltpu.get_barrier_semaphore()
    for z2, c2 in line:
        pl.semaphore_signal(barrier, inc=1, device_id=ident(r, 2 * z2 + c2), device_id_type=MESH)
    for r2, c2 in board:
        pl.semaphore_signal(barrier, inc=1, device_id=ident(r2, 2 * z + c2), device_id_type=MESH)
    pl.semaphore_wait(barrier, len(line) + len(board))

    def line_copy(kind, k, sems_s, sems_r, src_of, dst_of):
        z2, c2 = line[k]
        f2 = 2 * z2 + c2
        return remote(
            src_of(f2, c2), dst_of(f), sems_s.at[kind, k], sems_r.at[kind, f], ident(r, f2)
        )

    def line_from(kind, k, sems_s, sems_r, src_of, dst_of):
        z2, c2 = line[k]
        f2 = 2 * z2 + c2
        return remote(
            src_of(f, c), dst_of(f2), sems_s.at[kind, k], sems_r.at[kind, f2], ident(r, f2)
        )

    def line_send(*what):
        copies = [line_copy(what[0], k, *what[1:]) for k in range(len(line))]
        for cp in copies:
            cp.start()
        return copies

    def line_wait(*what):
        for k in range(len(line)):
            line_from(what[0], k, *what[1:]).wait_recv()

    def relay_send(*what):
        for k in range(len(line)):
            cp = line_copy(what[0], k, *what[1:])
            if k in far:
                pl.when(inner)(cp.start)
            else:
                cp.start()

    def relay_copy(k, kind, sems_s, sems_r, src_of, dst_of):
        z2, c2 = line[k]
        f2 = 2 * z2 + c2
        return remote(
            dst_of(f2),
            dst_of(f2),
            relay_s.at[kind, k],
            sems_r.at[kind, f2],
            ident(r, 2 * across[1] + c),
        )

    def relay_pass(*what):
        @pl.when(outer)
        def _():
            for k in via:
                line_from(what[0], k, *what[1:]).wait_recv()

        @pl.when(inner)
        def _():
            for k in via:
                line_from(what[0], k, *what[1:]).wait_recv()
                relay_copy(k, *what).start()

    def relay_wait(*what):
        for k in range(len(line)):
            if k not in via:
                line_from(what[0], k, *what[1:]).wait_recv()

    def relay_drain(*what):
        for k in range(len(line)):
            cp = line_copy(what[0], k, *what[1:])
            if k in far:
                pl.when(inner)(cp.wait_send)
            else:
                cp.wait_send()

        @pl.when(inner)
        def _():
            for k in via:
                relay_copy(k, *what).wait_send()

    def drain(copies):
        for cp in copies:
            cp.wait_send()

    def cond_src(f2, c2):
        return cond_pack.at[f2]

    def cond_dst(f2):
        return cond_all.at[f2]

    def extra_src(f2, c2):
        return extra.at[c2]

    def extra_dst(f2):
        return extra_all.at[f2]

    def proj_src(f2, c2):
        return proj_pack.at[c2]

    def proj_dst(f2):
        return proj_all.at[pl.ds(pl.multiple_of(f2 * part, 16), part)]

    tail = pl.ds(LANES, exp_all.shape[1] - LANES)
    head = pl.ds(0, LANES)

    def exp_src(f2, c2):
        return exp_pack.at[c2, :, tail]

    def exp_dst(f2):
        return exp_all.at[pl.ds(pl.multiple_of(f2 * part, 16), part), tail]

    def exp_head(f2):
        return exp_all.at[pl.ds(pl.multiple_of(f2 * part, 16), part), head]

    def half_tile(i):
        p = i // 2
        c2 = p // slots_of
        at = 2 * (r + 4 * p) + i % 2
        return c2, 2 * (p - 4 * c2) + i % 2, at // blocks, at % blocks

    def red_rows(j):
        return red_all.at[pl.ds(pl.multiple_of(j * HALF, HALF), HALF)]

    def red_copy(i, z2):
        c2, j, owner, block = half_tile(i)
        return remote(
            red_w.at[pl.ds(pl.multiple_of(block * HALF, HALF), HALF)],
            red_rows(j),
            red_s.at[i, z2],
            red_r.at[j],
            ident(r, 2 * z2 + c2),
        )

    def red_local(i):
        c2, j, owner, block = half_tile(i)
        return pltpu.make_async_copy(
            red_w.at[pl.ds(pl.multiple_of(block * HALF, HALF), HALF)], red_rows(j), red_l.at[j]
        )

    def red_goes(i, z2):
        c2, j, owner, block = half_tile(i)
        return (owner == f) & (2 * z2 + c2 != f) & (inner | (z2 + z != 3))

    def red_stops(i):
        c2, j, owner, block = half_tile(i)
        return (c2 == c) & (owner // 2 == across[2])

    def red_onward(i):
        c2, j, owner, block = half_tile(i)
        return remote(
            red_rows(j), red_rows(j), red_f.at[j], red_r.at[j], ident(r, 2 * across[1] + c)
        )

    def each_half(step):
        def body(i, carry):
            step(i)
            return carry

        lax.fori_loop(0, 2 * blocks, body, 0)

    def red_send():
        def step(i):
            c2, j, owner, block = half_tile(i)
            for z2 in range(4):
                pl.when(red_goes(i, z2))(red_copy(i, z2).start)
            pl.when((owner == f) & (c2 == c))(red_local(i).start)

        each_half(step)

    def red_pass():
        def step(i):
            @pl.when(red_stops(i))
            def _():
                red_copy(i, z).wait_recv()
                pl.when(inner)(red_onward(i).start)

        each_half(step)

    def red_wait():
        def step(i):
            c2, j, owner, block = half_tile(i)
            pl.when((c2 == c) & (owner != f) & (owner // 2 != across[2]))(red_copy(i, z).wait_recv)
            pl.when((owner == f) & (c2 == c))(red_local(i).wait)

        each_half(step)

    def red_drain():
        def step(i):
            for z2 in range(4):
                pl.when(red_goes(i, z2))(red_copy(i, z2).wait_send)
            pl.when(red_stops(i) & inner)(red_onward(i).wait_send)

        each_half(step)

    exp_main = (1, w_s, w_r, exp_src, exp_dst)
    proj_main = (0, w_s, w_r, proj_src, proj_dst)

    def first_src(f2, c2):
        return exp_pack.at[0, :, head]

    exp_lead = (2, w_s, w_r, first_src, exp_head)

    def lead_send(start):
        for k, (z2, c2) in enumerate(line):
            keep = c2 == 0
            if k in far:
                keep = keep & inner
            cp = line_copy(exp_lead[0], k, *exp_lead[1:])
            pl.when(keep)(cp.start if start else cp.wait_send)

    def exp_send():
        relay_send(*exp_main)
        lead_send(True)

    def exp_pass():
        relay_pass(*exp_main)

        @pl.when(c == 0)
        def _():
            relay_pass(*exp_lead)

    def exp_wait():
        relay_wait(*exp_main)

        @pl.when(c == 0)
        def _():
            relay_wait(*exp_lead)

    def exp_drain():
        relay_drain(*exp_main)
        lead_send(False)

        @pl.when((c == 0) & inner)
        def _():
            for k in via:
                relay_copy(k, *exp_lead).wait_send()

    sent = line_send(0, small_s, small_r, cond_src, cond_dst)
    packs = []
    for c2 in range(2):
        for i in range(slots_of):
            if c2 and not i:
                continue
            tile = r + 4 * (4 * c2 + i)
            cp = pltpu.make_async_copy(
                exp_w.at[:, pl.ds(pl.multiple_of(tile * LANES, LANES), LANES)],
                exp_pack.at[c2, :, pl.ds(i * LANES, LANES)],
                pe_s.at[c2, i],
            )
            cp.start()
            packs.append(cp)
    live_sent = []
    for k, (r2, c2) in enumerate(board):
        cp = remote(
            live_row,
            live_all.at[me],
            small_s.at[3, k],
            small_r.at[3, me],
            ident(r2, 2 * z + c2),
        )
        cp.start()
        live_sent.append(cp)
    local = [
        pltpu.make_async_copy(cond_pack.at[f], cond_all.at[f], local_sem.at[0]),
        pltpu.make_async_copy(extra.at[c], extra_all.at[f], local_sem.at[1]),
        pltpu.make_async_copy(live_row, live_all.at[me], local_sem.at[5]),
    ]
    for cp in local:
        cp.start()

    def one_hot():
        ids = lax.broadcasted_iota(jnp.int32, (latents.shape[0], rows), 0)
        return jnp.where(ids == slots[...], 1.0, 0.0)

    def dot(a, b):
        return jnp.dot(a, b, preferred_element_type=f32)

    def dot_t(a, b):
        return lax.dot_general(a, b, (((1,), (1,)), ((), ())), preferred_element_type=f32)

    def t_dot(a, b):
        return lax.dot_general(a, b, (((0,), (0,)), ((), ())), preferred_element_type=f32)

    wide_columns = proj_all.shape[1]
    for c2 in range(2):
        t = 2 * r + c2
        picked = jnp.zeros((part, wide_columns), f32)
        for q in range(3):
            window = proj_w[
                :, pl.ds(pl.multiple_of(q * width + t * LANES, LANES), LANES_Q)
            ]
            source = lax.broadcasted_iota(jnp.int32, (LANES_Q, wide_columns), 0)
            goal = lax.broadcasted_iota(jnp.int32, (LANES_Q, wide_columns), 1)
            picks = (source - t * (part - LANES) == goal - q * part) & (
                (goal >= q * part) & (goal < (q + 1) * part)
            )
            picked += dot(window, jnp.where(picks, 1.0, 0.0).astype(bf16))
        proj_pack[c2] = picked.astype(bf16)
    local[0].wait()
    line_wait(0, small_s, small_r, cond_src, cond_dst)
    cond_cols = jnp.sum(cond_all[...].astype(f32), axis=1).astype(bf16)
    mod_send[...] = jnp.zeros(mod_send.shape, f32)
    for p in range(6):
        piece = dot(cond_cols, mod_w[:, p * width : (p + 1) * width]) + mod_bias[p : p + 1, :]
        mod_send[:, p, :] = piece

    def mod_src(f2, c2):
        return mod_send.at[f2]

    def mod_dst(f2):
        return mod_all.at[f2]

    sent += line_send(2, small_s, small_r, mod_src, mod_dst)
    mod_all[f] = mod_send[f]

    relay_send(0, w_s, w_r, proj_src, proj_dst)
    sent += line_send(1, small_s, small_r, extra_src, extra_dst)
    own_proj = pltpu.make_async_copy(proj_pack.at[c], proj_dst(f), local_sem.at[2])
    own_proj.start()
    local.append(own_proj)

    kept[...] = t_dot(one_hot().astype(bf16), latents[...])
    g_rows[...] = t_dot((one_hot() * live_row[0:1, :]).astype(bf16), cotangent[...])

    def normalise(values, norm_ref, rstd_ref):
        centred = values - jnp.mean(values, axis=-1, keepdims=True)
        rstd = lax.rsqrt(jnp.mean(centred * centred, axis=-1, keepdims=True) + 1e-06)
        norm_ref[...] = centred * rstd
        rstd_ref[...] = rstd

    normalise(kept[...], norm_one, rstd_one)
    out_w[part:, :] = jnp.zeros((out_w.shape[0] - part, width), bf16)
    split = lax.broadcasted_iota(jnp.int32, spread.shape, 0)
    column = lax.broadcasted_iota(jnp.int32, spread.shape, 1)
    skip = jnp.where(split >= part, LANES_Q - part, 0) + jnp.where(
        split >= 2 * part, LANES_Q - part, 0
    )
    spread[...] = jnp.where(column == split + skip, 1.0, 0.0).astype(bf16)

    @pl.when(c == 1)
    def _():
        exp_all[:, :LANES] = jnp.zeros((width, LANES), bf16)
        red_all[:LANES, :] = jnp.zeros((LANES, width), bf16)

    for cp in local[1:]:
        cp.wait()

    line_wait(2, small_s, small_r, mod_src, mod_dst)
    modulation = jnp.sum(mod_all[...], axis=0)
    shift_attn, scale_attn, gate_attn, shift_mlp, scale_mlp, gate_mlp = [
        modulation[p : p + 1, :] for p in range(6)
    ]

    def own(ref):
        return ref.at[pl.ds(pl.multiple_of(me * rows, rows), rows)]

    def slot(ref, u):
        return ref.at[pl.ds(pl.multiple_of(u * rows, rows), rows)]

    def gather_start(kind, buf):
        copies = [
            remote(own(buf), own(buf), ag_s.at[kind, 0], ag_r.at[kind, me], sibling),
        ]
        for k, (dx, dy) in enumerate(SAME_CORE):
            copies.append(
                remote(
                    own(buf),
                    own(buf),
                    ag_s.at[kind, 1 + k],
                    ag_r.at[kind, me],
                    ident(plane(dx, dy), f),
                )
            )
        for cp in copies:
            cp.start()

    def gather_pass(kind, buf, k):
        u = 4 * c + plane(*SAME_CORE[k])
        cp = remote(slot(buf, u), slot(buf, u), ag_s.at[kind, 4 + k], ag_r.at[kind, u], sibling)
        cp.wait_recv()
        cp.start()

    def gather_take(kind, buf, r2):
        u = 4 * other + r2
        remote(slot(buf, u), slot(buf, u), ag_s.at[kind, 0], ag_r.at[kind, u], sibling).wait_recv()

    def gather_near(kind, buf):
        gather_pass(kind, buf, 0)
        gather_pass(kind, buf, 1)
        gather_take(kind, buf, r)
        gather_take(kind, buf, plane(1, 0))

    def gather_far(kind, buf):
        gather_pass(kind, buf, 2)
        gather_take(kind, buf, plane(0, 1))
        gather_take(kind, buf, plane(1, 1))

    def gather_drain(kind, buf):
        for k in range(7):
            remote(
                own(buf), own(buf), ag_s.at[kind, k], ag_r.at[kind, me], sibling
            ).wait_send()

    def reduce_send(kind, buf, landing, r2):
        remote(
            slot(buf, 4 * c + r2),
            landing.at[r],
            rs_s.at[kind, r2],
            rs_r.at[kind, r],
            ident(r2, f),
        ).start()

    def chunk_of(k):
        cc, pair = (c + 1 + k) % 2, (y + k // 2) % 2
        first = 4 * cc + 2 * pair
        return first, pair, pl.ds(pl.multiple_of(first * rows, 2 * rows), 2 * rows)

    def reduce_chunk(kind, k, values, buf, sib, landing, hold=False):
        first, pair, here = chunk_of(k)
        there = pl.ds(pl.multiple_of(pair * 2 * rows, 2 * rows), 2 * rows)
        hop = remote(
            buf.at[here], sib.at[there], sb_s.at[kind, pair], sb_r.at[kind, pair], sibling
        )

        @pl.when(k % 2 == 0)
        def _():
            buf[here, :] = values.astype(bf16)
            hop.start()

        @pl.when(k % 2 == 1)
        def _():
            hop.wait_recv()
            buf[here, :] = (values + sib[there, :].astype(f32)).astype(bf16)
            for x2 in range(0 if hold else 2):
                r2 = 2 * pair + x2

                @pl.when(r2 != r)
                def _():
                    reduce_send(kind, buf, landing, r2)

    def reduce_end(kind, buf, landing):
        total = own(buf)[...].astype(f32)
        for dx, dy in SAME_CORE:
            r2 = plane(dx, dy)
            remote(
                own(buf), landing.at[r2], rs_s.at[kind, r2], rs_r.at[kind, r2], ident(r2, f)
            ).wait_recv()
            total += landing[r2].astype(f32)
        return total

    def reduce_drain(kind, buf, sib, landing):
        for k in range(2):
            there = pl.ds(k * 2 * rows, 2 * rows)
            remote(
                sib.at[there], sib.at[there], sb_s.at[kind, k], sb_r.at[kind, k], sibling
            ).wait_send()
        for dx, dy in SAME_CORE:
            r2 = plane(dx, dy)
            remote(
                own(buf), landing.at[r2], rs_s.at[kind, r2], rs_r.at[kind, r2], ident(r2, f)
            ).wait_send()

    own(x_one)[...] = (norm_one[...] * (1.0 + scale_attn) + shift_attn).astype(bf16)
    gather_start(0, x_one)
    grad_mlp = (gate_mlp * g_rows[...]).astype(bf16)
    own(g_mlp)[...] = grad_mlp
    gather_start(1, g_mlp)
    slab[...] = jnp.zeros(slab.shape, f32)
    slab[6:7, :] = jnp.sum(grad_mlp.astype(f32), axis=0, keepdims=True)

    def out_copy(z2):
        return remote(
            out_shard,
            out_w.at[pl.ds(0, part)],
            ow_s.at[z2],
            ow_r.at[0],
            ident(r, 2 * z2 + c),
        )

    def out_onward():
        return remote(
            out_w.at[pl.ds(0, part)],
            out_w.at[pl.ds(0, part)],
            ow_s.at[7],
            ow_r.at[0],
            ident(r, 2 * across[1] + c),
        )

    def out_goes(z2):
        return (z == r) & (z2 != z) & (inner | (z2 + z != 3))


    @pl.when(z == r)
    def _():
        out_w[:part, :] = out_shard[...]

    for z2 in range(4):
        pl.when(out_goes(z2))(out_copy(z2).start)
    relay_pass(*proj_main)
    relay_wait(*proj_main)
    @pl.when(z != r)
    def _():
        out_copy(z).wait_recv()

    pl.when(inner & (across[2] == r))(out_onward().start)
    for cp in packs:
        cp.wait()
    own_exp = pltpu.make_async_copy(exp_pack.at[c, :, tail], exp_dst(f), local_sem.at[3])
    own_exp.start()

    @pl.when(c == 0)
    def _():
        cp = pltpu.make_async_copy(exp_pack.at[0, :, head], exp_head(f), local_sem.at[6])
        cp.start()
        cp.wait()

    exp_send()
    proj_wide[...] = dot(proj_all[...], spread[...]).astype(bf16)
    line_wait(1, small_s, small_r, extra_src, extra_dst)
    biases = jnp.sum(extra_all[...].astype(f32), axis=0)
    out_b, red_b, exp_b, qv_b = [
        jnp.concatenate([biases[3 * p + q : 3 * p + q + 1, :] for q in range(3)], axis=1)
        for p in range(4)
    ]
    for k, (r2, c2) in enumerate(board):
        remote(
            live_row,
            live_all.at[4 * c2 + r2],
            small_s.at[3, k],
            small_r.at[3, 4 * c2 + r2],
            ident(r2, 2 * z + c2),
        ).wait_recv()
    gather_near(0, x_one)
    cond_sent = []
    for k, (dx, dy) in enumerate(SAME_CORE):
        cp = remote(
            cond_all,
            o_cond.at[r],
            small_s.at[4, k],
            small_r.at[4, r],
            ident(plane(dx, dy), f),
        )
        cp.start()
        cond_sent.append(cp)
    own_cond = pltpu.make_async_copy(cond_all, o_cond.at[r], local_sem.at[0])
    own_cond.start()

    lane = lax.broadcasted_iota(jnp.int32, (1, LANES_Q), 1)
    heads = [
        jnp.where((lane >= h * HEAD_DIM) & (lane < (h + 1) * HEAD_DIM), 1.0, 0.0).astype(bf16)
        for h in range(2)
    ]
    scale = HEAD_DIM ** (-0.5)

    red_send()

    def attend(k, carry):
        first, pair, here = chunk_of(k)

        @pl.when(k == 2)
        def _():
            gather_far(0, x_one)

        wide = dot(x_one[here, :], proj_wide[...])
        qkv[here, :LANES_Q] = (wide[:, :LANES_Q] + qv_b[:, :LANES_Q]).astype(bf16)
        qkv[here, LANES_Q : 2 * LANES_Q] = wide[:, LANES_Q : 2 * LANES_Q].astype(bf16)
        qkv[here, 2 * LANES_Q :] = (
            wide[:, 2 * LANES_Q :] + qv_b[:, LANES_Q : 2 * LANES_Q]
        ).astype(bf16)
        for i in range(2):
            u = first + i
            at = pl.ds(pl.multiple_of(u * rows, rows), rows)
            q = qkv[at, :LANES_Q]
            key = qkv[at, LANES_Q : 2 * LANES_Q]
            val = qkv[at, 2 * LANES_Q :]
            alive = live_all[u][0:1, :] > 0.5
            total = jnp.zeros((rows, LANES_Q), f32)
            for h in range(2):
                s = dot_t(q * heads[h], key) * scale
                s = jnp.where(alive, s, -1e30)
                e = jnp.exp(s - jnp.max(s, axis=-1, keepdims=True))
                p = e / jnp.sum(e, axis=-1, keepdims=True)
                probs[2 * u + h] = p
                total += dot(p.astype(bf16), val) * heads[h].astype(f32)
            attended[at, :] = total.astype(bf16)
        values = dot(attended[here, :], out_w[...])
        reduce_chunk(0, k, values, part_a, sib_a, rows_a)
        return carry

    lax.fori_loop(0, 4, attend, 0)
    exp_pass()
    branch = reduce_end(0, part_a, rows_a) + out_b
    branch_a[...] = branch
    mixed[...] = kept[...] + gate_attn * branch
    normalise(mixed[...], norm_two, rstd_two)
    own(x_two)[...] = (norm_two[...] * (1.0 + scale_mlp) + shift_mlp).astype(bf16)
    gather_start(2, x_two)
    gather_near(1, g_mlp)
    gather_far(1, g_mlp)
    red_pass()
    exp_wait()
    own_exp.wait()
    red_wait()
    gather_near(2, x_two)
    reduce_drain(0, part_a, sib_a, rows_a)

    k_gelu = 0.7978845608028654
    hid_b = exp_b[:, : exp_all.shape[1]]

    def feed(k, carry):
        first, pair, here = chunk_of(k)

        @pl.when(k == 2)
        def _():
            gather_far(2, x_two)

        hid = dot(x_two[here, :], exp_all[...]) + hid_b
        square = hid * hid
        th = jnp.tanh(k_gelu * hid * (1.0 + 0.044715 * square))
        proj_wide[here, hid_lanes] = (0.5 * hid * (1.0 + th)).astype(bf16)
        slope = 0.5 * (1.0 + th) + 0.5 * hid * (1.0 - th * th) * k_gelu * (
            1.0 + 3.0 * 0.044715 * square
        )
        grad = (dot_t(g_mlp[here, :], red_all[...]) * slope).astype(bf16)
        g_hid[here, :] = grad
        values = dot_t(grad, exp_all[...])
        reduce_chunk(1, k, values, part_b, sib_b, rows_b)
        return carry

    lax.fori_loop(0, 4, feed, 0)

    hid_sum = jnp.sum(g_hid[...].astype(f32), axis=0, keepdims=True)
    slab[8:9, : exp_all.shape[1]] = hid_sum

    def line_rows(src, z2, lanes):
        return src.at[pl.ds(pl.multiple_of(z2 * 2 * part, 16), 2 * part), lanes]

    def line_term(kind, src, landing, lanes, q):
        stop = q == 0
        index = 3 if stop else q - 1
        return remote(
            line_rows(src, across[3] if stop else across[q], lanes),
            landing.at[index, :, lanes],
            dz_s.at[kind, index],
            dz_r.at[kind, index],
            ident(r, 2 * across[1 if stop else q] + c),
        )

    def line_out(*what):
        line_term(*what, 1).start()

        @pl.when(outer)
        def _():
            line_term(*what, 0).start()
            line_term(*what, 2).start()

        @pl.when(inner)
        def _():
            line_term(*what, 3).start()

    def line_join(kind, src, landing, lanes):
        @pl.when(inner)
        def _():
            line_term(kind, src, landing, lanes, 0).wait_recv()
            term = line_rows(src, across[2], lanes)
            term[...] = (term[...].astype(f32) + landing[3, :, lanes].astype(f32)).astype(bf16)
            line_term(kind, src, landing, lanes, 2).start()

    def line_sum(kind, src, landing, lanes):
        mine_now = line_rows(src, z, lanes)
        total = mine_now[...].astype(f32)
        for q in (1, 2):
            line_term(kind, src, landing, lanes, q).wait_recv()
            total += landing[q - 1, :, lanes].astype(f32)

        @pl.when(outer)
        def _():
            mine_now[...] = total.astype(bf16)

        @pl.when(inner)
        def _():
            line_term(kind, src, landing, lanes, 3).wait_recv()
            mine_now[...] = (total + landing[2, :, lanes].astype(f32)).astype(bf16)

    def line_drain(*what):
        line_term(*what, 1).wait_send()
        line_term(*what, 2).wait_send()

        @pl.when(outer)
        def _():
            line_term(*what, 0).wait_send()

        @pl.when(inner)
        def _():
            line_term(*what, 3).wait_send()

    every = slice(None)
    exp_tail = (0, d_exp, z_exp, tail)
    exp_front = (1, d_exp, z_exp, head)
    proj_sum = (2, d_proj, z_proj, every)

    def exp_sides(step):
        step(*exp_tail)

        @pl.when(c == 0)
        def _():
            step(*exp_front)

    def wide_grad(k, carry):
        at = pl.ds(pl.multiple_of(k * third, 128), third)
        d_exp[at, :] = t_dot(x_two[:, at], g_hid[...]).astype(bf16)
        return carry

    lax.fori_loop(0, 3, wide_grad, 0)
    exp_sides(line_out)

    def red_grad(k, carry):
        at = pl.ds(pl.multiple_of(k * third, 128), third)
        d_red[:, at] = t_dot(proj_wide[:total_rows, hid_lanes], g_mlp[:, at]).astype(bf16)
        return carry

    lax.fori_loop(0, 3, red_grad, 0)

    def red_tile(i):
        p = 4 * c + i
        at = r + 4 * p
        return (p >= 5 * c), at, (2 * at) // (2 * blocks)

    def apart(goal):
        return 2 * ((z // 2 + goal // 2) % 2) + (z + goal) % 2

    def red_up(i, index, z2):
        return remote(
            d_red.at[pl.ds(i * LANES, LANES)],
            z_red.at[index, i % 3],
            zr_s.at[i],
            zr_r.at[index, i % 3],
            ident(r, 2 * z2 + c),
        )

    for i in range(slots_of):
        real, at, goal = red_tile(i)
        q = apart(goal)
        stop = outer & (q == 3)
        pl.when(real & stop)(red_up(i, 3, across[1]).start)
        direct = (q != 0) & jnp.logical_not(stop) & jnp.logical_not(inner & (q == 2))
        pl.when(real & direct)(red_up(i, (q + 3) % 4, goal).start)

    grad_two = reduce_end(1, part_b, rows_b)

    def back_norm(grad, scale_part, norm, rstd):
        g_shift = jnp.sum(grad, axis=0, keepdims=True)
        g_scale = jnp.sum(grad * norm, axis=0, keepdims=True)
        e = grad * (1.0 + scale_part)
        inner = jnp.mean(e * norm, axis=-1, keepdims=True)
        return g_shift, g_scale, (e - jnp.mean(e, axis=-1, keepdims=True) - norm * inner) * rstd

    g_shift, g_scale, through = back_norm(grad_two, scale_mlp, norm_two[...], rstd_two[...])
    slab[3:4, :] = g_shift
    slab[4:5, :] = g_scale
    g_mixed[...] = g_rows[...] + through
    slab[2:3, :] = jnp.sum(g_mixed[...] * branch_a[...], axis=0, keepdims=True)
    grad_at = (gate_attn * g_mixed[...]).astype(bf16)
    own(g_attn)[...] = grad_at
    slab[7:8, :] = jnp.sum(grad_at.astype(f32), axis=0, keepdims=True)
    gather_start(3, g_attn)

    reduce_drain(1, part_b, sib_b, rows_b)
    def feed_out(k, carry):
        first, pair, here = chunk_of(k)
        values = dot(proj_wide[here, hid_lanes], red_all[...])
        reduce_chunk(3, k, values, part_b, sib_a, rows_b, hold=True)
        return carry

    lax.fori_loop(0, 4, feed_out, 0)

    gather_near(3, g_attn)
    exp_sides(line_join)
    for dx, dy in SAME_CORE[:2]:
        reduce_send(3, part_b, rows_b, plane(dx, dy))
    def attend_back(k, carry):
        first, pair, here = chunk_of(k)

        @pl.when(k == 2)
        def _():
            gather_far(3, g_attn)
            reduce_send(3, part_b, rows_b, plane(1, 1))

        g_att = dot_t(g_attn[here, :], out_w[...]).astype(bf16)
        for i in range(2):
            u = first + i
            at = pl.ds(pl.multiple_of(u * rows, rows), rows)
            q = qkv[at, :LANES_Q]
            key = qkv[at, LANES_Q : 2 * LANES_Q]
            val = qkv[at, 2 * LANES_Q :]
            up = g_att[i * rows : (i + 1) * rows, :]
            g_q = jnp.zeros((rows, LANES_Q), f32)
            g_k = jnp.zeros((rows, LANES_Q), f32)
            g_v = jnp.zeros((rows, LANES_Q), f32)
            for h in range(2):
                p = probs[2 * u + h]
                up_h = up * heads[h]
                g_v += t_dot(p.astype(bf16), up_h)
                g_p = dot_t(up_h, val)
                inner = jnp.sum(g_p * p, axis=-1, keepdims=True)
                g_s = (p * (g_p - inner)).astype(bf16)
                g_q += dot(g_s, key) * heads[h].astype(f32)
                g_k += t_dot(g_s, q * heads[h])
            wide = jnp.concatenate([g_q * scale, g_k * scale, g_v], axis=1).astype(bf16)
            d_qkv[at, :] = dot_t(wide, spread[...]).astype(bf16)
        values = dot_t(d_qkv[here, :], proj_all[...])
        reduce_chunk(2, k, values, part_a, sib_b, rows_a)
        return carry

    lax.fori_loop(0, 4, attend_back, 0)
    def proj_grad(k, carry):
        at = pl.ds(pl.multiple_of(k * third, 128), third)
        d_proj[at, :] = t_dot(x_one[:, at], d_qkv[...]).astype(bf16)
        return carry

    lax.fori_loop(0, 3, proj_grad, 0)
    line_out(*proj_sum)
    d_out[...] = t_dot(attended[...], g_attn[...]).astype(bf16)

    def out_up(index, z2):
        return remote(
            d_out.at[pl.ds(0, part)],
            z_out.at[index],
            ow_s.at[8],
            ow_r.at[1 + index],
            ident(r, 2 * z2 + c),
        )

    q_out = apart(r)
    pl.when(outer & (q_out == 3))(out_up(3, across[1]).start)
    pl.when((q_out == 1) | (outer & (q_out == 2)) | (inner & (q_out == 3)))(
        out_up((q_out + 3) % 4, r).start
    )

    def exp_up(k, i, r2, c2):
        at = red_tile(i)[1]
        return remote(
            d_exp.at[
                pl.ds(pl.multiple_of(z * 2 * part + c2 * part, 16), part), pl.ds(i * LANES, LANES)
            ],
            o_exp.at[:, pl.ds(pl.multiple_of(at * LANES, LANES), LANES)],
            et_s.at[k, i],
            et_r.at[at],
            ident(r2, 2 * z + c2),
        )

    def exp_here(i):
        at = red_tile(i)[1]
        return pltpu.make_async_copy(
            d_exp.at[
                pl.ds(pl.multiple_of(z * 2 * part + c * part, 16), part), pl.ds(i * LANES, LANES)
            ],
            o_exp.at[:, pl.ds(pl.multiple_of(at * LANES, LANES), LANES)],
            et_l.at[i],
        )

    exp_sides(line_sum)

    for i in range(slots_of):

        @pl.when(red_tile(i)[0])
        def _():
            for k, (r2, c2) in enumerate(board):
                exp_up(k, i, r2, c2).start()
            exp_here(i).start()

    def red_out(i, h, r2):
        half = 2 * red_tile(i)[1] + h
        return remote(
            d_red.at[pl.ds(i * LANES + h * HALF, HALF)],
            o_red.at[pl.ds(pl.multiple_of(half % blocks * HALF, HALF), HALF)],
            pr_s.at[2 * i + h, r2],
            pr_r.at[half % blocks],
            ident(r2, half // blocks),
        )

    def red_here(i, h):
        half = 2 * red_tile(i)[1] + h
        return pltpu.make_async_copy(
            d_red.at[pl.ds(i * LANES + h * HALF, HALF)],
            o_red.at[pl.ds(pl.multiple_of(half % blocks * HALF, HALF), HALF)],
            pr_l.at[2 * i + h],
        )

    def red_each(i, remote_part, local_part):
        for h in range(2):
            owner = (2 * red_tile(i)[1] + h) // blocks
            for r2 in range(4):

                @pl.when((owner != f) | (r2 != r))
                def _():
                    remote_part(red_out(i, h, r2))

            @pl.when(owner == f)
            def _():
                local_part(red_here(i, h))


    slab[9:10, : d_qkv.shape[1]] = jnp.sum(d_qkv[...].astype(f32), axis=0, keepdims=True)


    for i in range(slots_of):
        real, at, goal = red_tile(i)

        @pl.when(real & inner & (apart(goal) == 2))
        def _():
            red_up(i, 3, z).wait_recv()
            rows_i = slice(i * LANES, (i + 1) * LANES)
            d_red[rows_i, :] = (
                d_red[rows_i, :].astype(f32) + z_red[3, i % 3].astype(f32)
            ).astype(bf16)
            red_up(i, 1, goal).start()


    for i in range(slots_of):
        real, at, goal = red_tile(i)

        @pl.when(real & (goal == z))
        def _():
            rows_i = slice(i * LANES, (i + 1) * LANES)
            total = d_red[rows_i, :].astype(f32)
            for there in range(2):
                red_up(i, there, z).wait_recv()
                total += z_red[there, i % 3].astype(f32)

            @pl.when(outer)
            def _():
                d_red[rows_i, :] = total.astype(bf16)

            @pl.when(inner)
            def _():
                red_up(i, 2, z).wait_recv()
                d_red[rows_i, :] = (total + z_red[2, i % 3].astype(f32)).astype(bf16)

            red_each(i, lambda cp: cp.start(), lambda cp: cp.start())

    def place(values, base):
        live_hot = one_hot() * live_row[0:1, :]
        placed = dot(live_hot.astype(bf16), values.astype(bf16))
        hit = jnp.sum(live_hot, axis=1, keepdims=True)
        return jnp.where(hit > 0.5, placed.astype(bf16), base)

    branch = reduce_end(3, part_b, rows_b) + red_b
    @pl.when(inner & (q_out == 2))
    def _():
        out_up(3, z).wait_recv()
        d_out[:part, :] = (d_out[:part, :].astype(f32) + z_out[3].astype(f32)).astype(bf16)
        out_up(1, r).start()

    slab[5:6, :] = jnp.sum(g_rows[...] * branch, axis=0, keepdims=True)

    def slab_at(f2):
        return 4 * (f2 % 2) + f2 // 2

    grad_one = reduce_end(2, part_a, rows_a)
    g_shift, g_scale, through = back_norm(grad_one, scale_attn, norm_one[...], rstd_one[...])
    slab[0:1, :] = g_shift
    slab[1:2, :] = g_scale
    slabs[slab_at(f)] = slab[...].astype(bf16)

    def slab_src(f2, c2):
        return slabs.at[slab_at(f)]

    def slab_dst(f2):
        return slabs.at[slab_at(f2)]

    sent += line_send(5, small_s, small_r, slab_src, slab_dst)
    o_latents[...] = place(g_mixed[...] + through, cotangent[...])
    o_block[...] = place(mixed[...] + gate_mlp * branch, latents[...])

    line_join(*proj_sum)
    @pl.when(z == r)
    def _():
        total = d_out[:part, :].astype(f32)
        for k in range(2):
            out_up(k, z).wait_recv()
            total += z_out[k].astype(f32)

        @pl.when(outer)
        def _():
            d_out[:part, :] = total.astype(bf16)

        @pl.when(inner)
        def _():
            out_up(2, z).wait_recv()
            d_out[:part, :] = (total + z_out[2].astype(f32)).astype(bf16)

        for k, (dx, dy) in enumerate(SAME_CORE):
            remote(
                d_out.at[pl.ds(0, part)], o_out, ow_s.at[4 + k], ow_r.at[5], ident(plane(dx, dy), f)
            ).start()
        cp = pltpu.make_async_copy(d_out.at[pl.ds(0, part)], o_out, local_sem.at[5])
        cp.start()
        cp.wait()

    line_wait(5, small_s, small_r, slab_src, slab_dst)
    mine = pl.ds(pl.multiple_of(4 * c, 4), 4)
    for k, (dx, dy) in enumerate(SAME_CORE):
        cp = remote(
            slabs.at[mine],
            o_slabs.at[r, mine],
            small_s.at[6, k],
            small_r.at[6, r],
            ident(plane(dx, dy), f),
        )
        cp.start()
        sent.append(cp)
    own_slabs = pltpu.make_async_copy(slabs, o_slabs.at[r], local_sem.at[4])
    own_slabs.start()
    back_cond = jnp.zeros((8, part), f32)
    for p in range(6):
        back_cond += dot_t(slabs[:, p, :], mod_w[:, p * width : (p + 1) * width])
    for i in range(8):
        gcond[2 * (i % 4) + i // 4] = jnp.broadcast_to(back_cond[i : i + 1, :], (8, part))

    def gc_src(f2, c2):
        return gcond.at[f2]

    def gc_dst(f2):
        return o_gcond.at[f2]

    sent += line_send(7, small_s, small_r, gc_src, gc_dst)
    o_gcond[f] = gcond[f]

    line_sum(*proj_sum)

    def proj_up(k, r2, c2):
        return remote(
            d_proj.at[pl.ds(pl.multiple_of(z * 2 * part + c2 * part, 16), part)],
            proj_land.at[me],
            dp_s.at[k],
            dp_r.at[me],
            ident(r2, 2 * z + c2),
        )

    for k, (r2, c2) in enumerate(board):
        proj_up(k, r2, c2).start()
    proj_land[me] = d_proj[pl.ds(pl.multiple_of(z * 2 * part + c * part, 16), part), :]

    for k, (dx, dy) in enumerate(SAME_CORE):
        r2 = plane(dx, dy)
        remote(
            slabs.at[mine], o_slabs.at[r2, mine], small_s.at[6, 0], small_r.at[6, r2], sibling
        ).wait_recv()
        cp = remote(
            o_slabs.at[r2, mine],
            o_slabs.at[r2, mine],
            small_s.at[6, 3 + k],
            small_r.at[6, 4 + r2],
            sibling,
        )
        cp.start()
        sent.append(cp)
    line_wait(7, small_s, small_r, gc_src, gc_dst)
    for dx, dy in SAME_CORE:
        r2 = plane(dx, dy)
        remote(
            cond_all, o_cond.at[r2], small_s.at[4, 0], small_r.at[4, r2], ident(r2, f)
        ).wait_recv()
        theirs = pl.ds(pl.multiple_of(4 * other, 4), 4)
        remote(
            slabs.at[theirs], o_slabs.at[r2, theirs], small_s.at[6, 3], small_r.at[6, 4 + r2], sibling
        ).wait_recv()
    o_proj[...] = jnp.zeros(o_proj.shape, bf16)

    def unpack(r2, c2):
        t = 2 * r2 + c2
        wide = dot(proj_land[4 * c2 + r2], spread[...])
        for q in range(3):
            piece = pltpu.roll(wide[:, q * LANES_Q : (q + 1) * LANES_Q], t * (part - LANES), 1)
            here = pl.ds(pl.multiple_of(q * width + t * LANES, LANES), LANES_Q)
            o_proj[:, here] = (o_proj[:, here].astype(f32) + piece).astype(bf16)

    unpack(r, c)
    for r2, c2 in board:
        u = 4 * c2 + r2
        remote(
            proj_land.at[u], proj_land.at[u], dp_s.at[0], dp_r.at[u], ident(r2, 2 * z + c2)
        ).wait_recv()
        unpack(r2, c2)

    def tile_arrival(at, carry):
        p = at // 4

        @pl.when((at % 4 != r) | (p // slots_of != c))
        def _():
            remote(
                d_exp.at[pl.ds(0, part), pl.ds(0, LANES)],
                o_exp.at[:, pl.ds(pl.multiple_of(at * LANES, LANES), LANES)],
                et_s.at[0, 0],
                et_r.at[at],
                sibling,
            ).wait_recv()

        return carry

    lax.fori_loop(0, tiles, tile_arrival, 0)

    def block_arrival(block, carry):
        at = (blocks * f + block) // 2
        p = at // 4

        @pl.when((at % 4 != r) | (p // slots_of != c))
        def _():
            remote(
                d_red.at[pl.ds(0, HALF)],
                o_red.at[pl.ds(pl.multiple_of(block * HALF, HALF), HALF)],
                pr_s.at[0, 0],
                pr_r.at[block],
                sibling,
            ).wait_recv()

        return carry

    lax.fori_loop(0, blocks, block_arrival, 0)
    for i in range(slots_of):
        real, at, goal = red_tile(i)

        @pl.when(real)
        def _():
            for k, (r2, c2) in enumerate(board):
                exp_up(k, i, r2, c2).wait_send()
            exp_here(i).wait()

        @pl.when(real & (goal == z))
        def _():
            red_each(i, lambda cp: cp.wait_send(), lambda cp: cp.wait())

        @pl.when(real & (goal != z))
        def _():
            red_up(i, 0, z).wait_send()

    for k, (r2, c2) in enumerate(board):
        proj_up(k, r2, c2).wait_send()
    red_drain()
    exp_drain()

    exp_sides(line_drain)
    line_drain(*proj_sum)
    for z2 in range(4):
        pl.when(out_goes(z2))(out_copy(z2).wait_send)
    pl.when(inner & (across[2] == r))(out_onward().wait_send)

    @pl.when(z == r)
    def _():
        for k in range(3):
            remote(out_shard, o_out, ow_s.at[4 + k], ow_r.at[5], ident(r, f)).wait_send()

    @pl.when(z != r)
    def _():
        remote(out_shard, o_out, ow_s.at[3], ow_r.at[5], ident(r, f)).wait_recv()
        out_up(0, r).wait_send()

    relay_drain(*proj_main)
    reduce_drain(2, part_a, sib_b, rows_a)
    reduce_drain(3, part_b, sib_a, rows_b)
    for kind, buf in enumerate((x_one, g_mlp, x_two, g_attn)):
        gather_drain(kind, buf)
    drain(sent)
    drain(live_sent)
    drain(cond_sent)
    own_cond.wait()
    own_slabs.wait()


def fused_local(
    latents,
    condition,
    bucket,
    keep_slots,
    modulation_weight,
    modulation_bias,
    projection_weight,
    query_value_bias,
    output_weight,
    output_bias,
    expand_weight,
    expand_bias,
    reduce_weight,
    reduce_bias,
    cotangent,
):
    f32 = jnp.float32
    bf16 = jnp.bfloat16
    r = lax.axis_index("replica")
    f = lax.axis_index("fsdp")
    slot_count, width = latents.shape[1:]
    rows = keep_slots.shape[1]
    part = output_weight.shape[0]
    hid = expand_weight.shape[1]
    slots_of = (hid // LANES + 7) // 8
    wide = slots_of * LANES

    def placed(shard, count):
        return lax.dynamic_update_slice_in_dim(
            jnp.zeros((count,), f32), shard.astype(f32), f * shard.shape[0], 0
        )

    def mine(value, axis):
        return lax.dynamic_slice_in_dim(value, 2 * r, 2, axis)

    cond_float = condition.astype(f32)
    cond_act = jax.nn.silu(cond_float).astype(bf16)
    cond_pack = jnp.pad(cond_act.reshape(8, 1, part), ((0, 0), (0, 15), (0, 0)))
    mod_bias = jnp.pad(placed(modulation_bias, 6 * width).reshape(6, width), ((0, 2), (0, 0)))
    live_count = jnp.where(bucket[0] == 0, slot_count, slot_count - 16) // 2
    live = (jnp.arange(rows, dtype=jnp.int32) < live_count).astype(f32)
    qv = mine(placed(query_value_bias, 2 * width).reshape(2, 8, part), 1)
    qv = jnp.pad(qv.transpose(1, 0, 2), ((0, 0), (0, 0), (0, LANES_Q - part))).reshape(2, -1)
    tiled_b = placed(expand_bias, hid).reshape(hid // (4 * LANES), 4, LANES)
    tiled_b = lax.dynamic_index_in_dim(tiled_b, r, 1, keepdims=False)
    second_b = jnp.pad(tiled_b[slots_of:], ((1, 0), (0, 0)))
    expand_b = jnp.stack([tiled_b[:slots_of].reshape(-1), second_b.reshape(-1)])
    extra = jnp.stack(
        [
            jnp.broadcast_to(placed(output_bias, width), (2, width)),
            jnp.broadcast_to(placed(reduce_bias, width), (2, width)),
            jnp.pad(expand_b, ((0, 0), (0, width - wide))),
            jnp.pad(qv, ((0, 0), (0, width - 2 * LANES_Q))),
        ],
        axis=1,
    ).astype(bf16)
    extra = jnp.pad(extra.reshape(2, 12, width // 3), ((0, 0), (0, 4), (0, 0)))
    total = 8 * rows
    vmem = pltpu.VMEM
    dma = pltpu.SemaphoreType.DMA
    scratch = [
        vmem((8, 16, part), bf16),
        vmem((8, 16, width // 3), bf16),
        vmem((8, 8, rows), f32),
        vmem((8, 8, width), f32),
        vmem((8, 8, width), f32),
        vmem((width, 3 * part), bf16),
        vmem((width, wide), bf16),
        vmem((wide, width), bf16),
        vmem((LANES_Q, width), bf16),
        vmem((2, part, 3 * part), bf16),
        vmem((2, part, wide), bf16),
        vmem((width, 3 * LANES_Q), bf16),
        vmem((3 * part, 3 * LANES_Q), bf16),
        vmem((total, width), bf16),
        vmem((total, width), bf16),
        vmem((total, width), bf16),
        vmem((total, width), bf16),
        vmem((total, 3 * LANES_Q), bf16),
        vmem((16, rows, rows), f32),
        vmem((total, LANES_Q), bf16),
        vmem((total, wide), bf16),
        vmem((total, 3 * part), bf16),
        vmem((total, width), bf16),
        vmem((total, width), bf16),
    ]
    scratch += [vmem((4 * rows, width), bf16)] * 2
    scratch += [vmem((4, rows, width), bf16)] * 2
    scratch += [
        vmem((rows, width), f32),
        vmem((rows, 1), f32),
        vmem((rows, width), f32),
        vmem((rows, width), f32),
        vmem((rows, width), f32),
        vmem((rows, width), f32),
        vmem((rows, 1), f32),
        vmem((rows, width), f32),
        vmem((16, width), f32),
        vmem((8, 16, width), bf16),
        vmem((8, 8, part), f32),
        vmem((width, wide), bf16),
        vmem((wide, width), bf16),
        vmem((width, 3 * part), bf16),
        vmem((LANES_Q, width), bf16),
        vmem((4, 2 * part, wide), bf16),
        vmem((4, 3, LANES, width), bf16),
        vmem((4, 2 * part, 3 * part), bf16),
        vmem((4, part, width), bf16),
        vmem((8, part, 3 * part), bf16),
        dma((8,)),
        dma((8, 7)),
        dma((8, 8)),
        dma((3, 7)),
        dma((3, 8)),
        dma((4, 8)),
        dma((4, 9)),
        dma((4, 2)),
        dma((4, 2)),
        dma((4, 4)),
        dma((4, 4)),
        dma((3, 4)),
        dma((3, 4)),
        dma((7,)),
        dma((8,)),
        dma((9,)),
        dma((6,)),
        dma((hid // HALF // 4, 4)),
        dma((2 * slots_of,)),
        dma((2 * slots_of,)),
        dma((slots_of,)),
        dma((4, 3)),
        dma((2, slots_of)),
        dma((7, slots_of)),
        dma((hid // LANES,)),
        dma((slots_of,)),
        dma((2 * slots_of, 4)),
        dma((hid // HALF // 8,)),
        dma((2 * slots_of,)),
        dma((3, 2)),
        dma((2 * slots_of,)),
    ]
    in_vmem = pl.BlockSpec(memory_space=pltpu.VMEM)
    anywhere = pl.BlockSpec(memory_space=pl.ANY)
    outputs = pl.pallas_call(
        fused_kernel,
        out_shape=(
            jax.ShapeDtypeStruct((slot_count, width), bf16),
            jax.ShapeDtypeStruct((slot_count, width), bf16),
            jax.ShapeDtypeStruct((4, 8, 16, width), bf16),
            jax.ShapeDtypeStruct((4, 8, 16, part), bf16),
            jax.ShapeDtypeStruct((8, 8, part), f32),
            jax.ShapeDtypeStruct((part, hid), bf16),
            jax.ShapeDtypeStruct((hid // 8, width), bf16),
            jax.ShapeDtypeStruct((part, 3 * width), bf16),
            jax.ShapeDtypeStruct((part, width), bf16),
        ),
        in_specs=[in_vmem] * 9 + [anywhere] * 2 + [in_vmem],
        out_specs=(
            in_vmem,
            in_vmem,
            anywhere,
            anywhere,
            in_vmem,
            anywhere,
            anywhere,
            in_vmem,
            anywhere,
        ),
        scratch_shapes=scratch,
        compiler_params=pltpu.CompilerParams(
            collective_id=0, has_side_effects=True, vmem_limit_bytes=60 << 20
        ),
    )(
        latents[0],
        cotangent[0],
        keep_slots,
        jnp.broadcast_to(live[None], (8, rows)),
        cond_pack,
        mod_bias,
        extra,
        modulation_weight,
        projection_weight,
        expand_weight,
        reduce_weight,
        output_weight,
    )
    block, grad_latents, slabs, conds, g_cond, g_exp, g_red, g_proj, g_out = outputs

    def shard(value, axis, size):
        return lax.dynamic_slice_in_dim(value, f * size, size, axis)

    slabs = slabs.reshape(32, 16, width)
    grad_mod = slabs[:, :6].reshape(32, 6 * width)
    cond_cols = conds[:, :, 0].reshape(4, 4, 2, part).transpose(0, 2, 1, 3).reshape(32, part)
    sum_mod_w = jnp.einsum("bd,be->de", cond_cols, grad_mod, preferred_element_type=f32)
    tails = jnp.sum(slabs.reshape(4, 2, 4, 16, width)[:, :, :, :10].astype(f32), axis=2)
    sums = jnp.sum(tails[:, :, :8], axis=(0, 1))
    tails = tails[:, :, 8:]
    sum_mod_b = shard(sums[:6].reshape(-1), 0, modulation_bias.shape[0])
    sum_red_b = shard(sums[6], 0, part)
    sum_out_b = shard(sums[7], 0, part)
    exp_sums = tails[:, :, 0, :wide].reshape(4, 2, slots_of, LANES)
    exp_sums = jnp.concatenate([exp_sums[:, 0], exp_sums[:, 1, 1:]], axis=1)
    sum_exp_b = shard(exp_sums.transpose(1, 0, 2).reshape(-1), 0, expand_bias.shape[0])
    qv_sums = tails[:, :, 1, : 3 * part].reshape(8, 3, part)
    qv_sums = jnp.concatenate([qv_sums[:, 0].reshape(-1), qv_sums[:, 2].reshape(-1)])
    sum_qv_b = shard(qv_sums, 0, query_value_bias.shape[0])
    grad_condition = jax.vjp(jax.nn.silu, cond_float)[1](g_cond[:, 0].reshape(1, width))[0]
    return (
        block[None],
        grad_latents[None],
        grad_condition,
        sum_mod_w,
        sum_mod_b,
        g_proj.astype(f32),
        sum_qv_b,
        g_out.astype(f32),
        sum_out_b,
        g_exp.astype(f32),
        sum_exp_b,
        g_red.astype(f32),
        sum_red_b,
    )


def solution(mesh):
    placed = (
        P(("replica", "fsdp"), None, None),
        P(("replica", "fsdp"), None),
        P(("replica", "fsdp")),
        P(("replica", "fsdp"), None),
        P("fsdp", None),
        P("fsdp"),
        P("fsdp", None),
        P("fsdp"),
        P("fsdp", None),
        P("fsdp"),
        P("fsdp", None),
        P("fsdp"),
        P("fsdp", None),
        P("fsdp"),
        P(("replica", "fsdp"), None, None),
    )
    body = fused_local if tuple(mesh.shape.values()) == (4, 8) else local
    return jax.shard_map(
        body,
        mesh=mesh,
        in_specs=placed,
        out_specs=(
            P(("replica", "fsdp"), None, None),
            P(("replica", "fsdp"), None, None),
            P(("replica", "fsdp"), None),
            P("fsdp", None),
            P("fsdp"),
            P("fsdp", None),
            P("fsdp"),
            P("fsdp", None),
            P("fsdp"),
            P("fsdp", None),
            P("fsdp"),
            P("fsdp", None),
            P("fsdp"),
        ),
        check_vma=False,
    )
```
